32 devices in a mesh: ctx: 8 (over y, x, core), ch: 4 (over z).
Axes of the slice: x: 2, y: 2, z: 4, core: 2. Of those that a mesh axis runs over, the one named last changes fastest.
Arguments:
- query: bfloat16 [8192, 4096], P(('ctx', 'ch')), may hold values from -6 to 6
- key_in: bfloat16 [8192, 4096], P(('ctx', 'ch')), may hold values from -6 to 6
- value: bfloat16 [8192, 4096], P(('ctx', 'ch')), may hold values from -6 to 6
- residues: float32 [4096, 16], P('ch'), may hold values from -0.05 to 0.05
- decay_rates: float32 [4096, 16], P('ch'), may hold values from 2e-05 to 0.03
- skip_gain: float32 [4096], P('ch'), may hold values from 0.5 to 1.5
Outputs:
- output: bfloat16 [8192, 4096], P(('ctx', 'ch'))
The draws below stay inside these ranges and needn't reach their ends.
All inputs are finite; a program needn't handle non-finite values.
Results may differ from the reference program's by a relative error of at most 0.0056.
Values may be sent and summed in bfloat16 or wider, within the bound.
No kernel may reach another device: no remote copies, remote signals or barrier semaphores. Data moves between devices by JAX's collectives and lax.ppermute only.
A program may use at most 192 MiB of HBM per device.

```python
import math
import jax
import jax.numpy as jnp
from jax import lax

CH = 4096
MODES = 16
PART = 1024
FILTER_PARTS = 4
TOKENS = 8192
N_CH = 4


def level_of(key, dims, split, smallest, high):
    loudness = 1.0
    for dim, blocks in split:
        heights = jax.random.uniform(jax.random.fold_in(jax.random.fold_in(key, 6), dim), (blocks,), jnp.float32, smallest / len(split), high / len(split))
        loudness = loudness * jnp.repeat(jnp.exp(heights), dims[dim] // blocks).reshape((-1,) + (1,) * (len(dims) - 1 - dim))
    return loudness


def gaussian(stream_key, dims, spread, reach, cuts=(), kind=jnp.bfloat16):
    gain = level_of(stream_key, dims, cuts, -0.22, 0.18) if cuts else 1.0
    values = jax.random.normal(stream_key, dims, jnp.float32) * spread * gain
    return jnp.minimum(jnp.maximum(values, -reach), reach).astype(kind)


def setup_inputs(seed: int = 0) -> dict:
    arg_keys = jax.random.split(jax.random.key(seed), 7)
    query = gaussian(arg_keys[0], (TOKENS, CH), 1.0, 6.0, ((0, 32),))
    key_in = gaussian(arg_keys[1], (TOKENS, CH), 1.0, 6.0, ((0, 32),))
    value = gaussian(arg_keys[2], (TOKENS, CH), 1.0, 6.0, ((0, 32),))
    residues = gaussian(arg_keys[3], (CH, MODES), 0.008, 0.05, ((0, 4),), jnp.float32)
    decay_rates = jnp.clip(jnp.exp(math.log(0.03) - 7.3132204 * jax.random.uniform(arg_keys[4], (CH, MODES), jnp.float32) ** level_of(arg_keys[4], (CH, MODES), ((0, 4),), -0.2, 0.2)), 1.9999999494757503e-05, 0.03)
    skip_gain = jnp.clip(0.5 + 1.0 * jax.random.uniform(arg_keys[5], (CH,), jnp.float32) ** level_of(arg_keys[5], (CH,), ((0, 4),), -0.2, 0.2), 0.5, 1.5)
    return {"query": query, "key_in": key_in, "value": value, "residues": residues, "decay_rates": decay_rates, "skip_gain": skip_gain}


def modal_filter(res_group, rate_group, count):
    positions = jnp.arange(count).astype(jnp.float32)
    decays = jnp.exp(-positions[:, None, None] * rate_group[None, :, :])
    return jnp.sum(decays * res_group[None, :, :], axis=2)


def reference(query, key_in, value, residues, decay_rates, skip_gain):
    product = (query.astype(jnp.float32) * key_in.astype(jnp.float32)).astype(jnp.bfloat16)
    product = lax.optimization_barrier(product).astype(jnp.float32)
    length = product.shape[0]
    n_fft = 2 * length
    span = FILTER_PARTS * PART
    group = CH // N_CH
    count = CH // group

    def one_group(start):
        inputs = lax.dynamic_slice_in_dim(product, start, group, 1)
        res_group = lax.dynamic_slice_in_dim(residues, start, group, 0)
        rate_group = lax.dynamic_slice_in_dim(decay_rates, start, group, 0)
        gains = lax.dynamic_slice_in_dim(skip_gain, start, group, 0)
        filter_taps = modal_filter(res_group, rate_group, span)
        spectrum = jnp.fft.rfft(inputs, n=n_fft, axis=0) * jnp.fft.rfft(filter_taps, n=n_fft, axis=0)
        convolved = jnp.fft.irfft(spectrum, n=n_fft, axis=0)[:length]
        return (convolved + gains[None, :] * inputs).astype(jnp.bfloat16)

    starts = jnp.arange(count).astype(jnp.int32) * group
    pieces = lax.map(one_group, starts)
    mixed = jnp.transpose(pieces, (1, 0, 2)).reshape(length, CH)
    mixed = lax.optimization_barrier(mixed)
    return (value.astype(jnp.float32) * mixed.astype(jnp.float32)).astype(jnp.bfloat16)
```

```python
import functools

import jax
import jax.numpy as jnp
from jax import lax
from jax.experimental import pallas as pl
from jax.experimental.pallas import tpu as pltpu
from jax.sharding import PartitionSpec as P

FILTER_PARTS = 4
LANES = 128
SEGMENTS = 8
WIDE = 4
SHARES = (8, 8, 8, 4, 4)


def from_behind(value, axis, steps):
    count = lax.axis_size(axis)
    return lax.ppermute(value, axis, [(source, source + steps) for source in range(count - steps)])


def rows_of(table, modes):
    return [jnp.broadcast_to(table[m : m + 1, :], (SEGMENTS, table.shape[1])) for m in range(modes)]


def shifted(value, steps, row):
    return jnp.where(row >= steps, pltpu.roll(value, steps, 0), 0.0)


def scan_segments(rate, scr, length):
    modes = rate.shape[0]
    steps = length // SEGMENTS
    decay = rows_of(jnp.exp(-rate), modes)
    state = None
    for i in range(steps):
        tokens = scr[pl.ds(i, SEGMENTS, stride=steps), :]
        if state is None:
            state = [tokens] * modes
        else:
            state = [d * s + tokens for d, s in zip(decay, state)]
    return state


def chain_segments(rate, state, length):
    modes = rate.shape[0]
    steps = length // SEGMENTS
    row = lax.broadcasted_iota(jnp.int32, (SEGMENTS, rate.shape[1]), 0)
    reach = 1
    while reach < SEGMENTS:
        jump = rows_of(jnp.exp(-rate * float(steps * reach)), modes)
        state = [s + j * shifted(s, reach, row) for j, s in zip(jump, state)]
        reach *= 2
    return state


def emit(rate, weight, state, scr, out_scr, length):
    modes = rate.shape[0]
    steps = length // SEGMENTS
    decay = rows_of(jnp.exp(-rate), modes)
    weight = rows_of(weight, modes)
    for i in range(steps):
        tokens = scr[pl.ds(i, SEGMENTS, stride=steps), :]
        state = [d * s + tokens for d, s in zip(decay, state)]
        terms = [w * s for w, s in zip(weight, state)]
        while len(terms) > 1:
            terms = [a + b for a, b in zip(terms[::2], terms[1::2])]
        out_scr[pl.ds(i, SEGMENTS, stride=steps), :] = terms[0]


def product_of(query, key_in):
    return (query.astype(jnp.float32) * key_in.astype(jnp.float32)).astype(jnp.bfloat16)


def over_tiles(ref, body):
    def step(t, carry):
        body(pl.ds(pl.multiple_of(t * LANES, LANES), LANES))
        return carry

    lax.fori_loop(0, ref.shape[1] // LANES, step, 0)


def states_kernel(query, key_in, rate_ref, carry_out, state_out, scr):
    length = query.shape[0]
    modes = rate_ref.shape[1]

    def body(cols):
        scr[...] = product_of(query[:, cols], key_in[:, cols]).astype(jnp.float32)
        rate = rate_ref[0, :, cols]
        state = chain_segments(rate, scan_segments(rate, scr, length), length)
        row = lax.broadcasted_iota(jnp.int32, (SEGMENTS, LANES), 0)
        for m in range(modes):
            carry_out[pl.ds(m * SEGMENTS, SEGMENTS), cols] = shifted(state[m], 1, row)
            state_out[0, pl.ds(m, 1), cols] = state[m][SEGMENTS - 1 :, :]

    over_tiles(query, body)


def own_terms(query, key_in, rate_ref, weight_ref, gain_ref, carry_ref, before_ref, scr, out_scr, cols):
    length = query.shape[0]
    modes = rate_ref.shape[1]
    steps = length // SEGMENTS
    scr[...] = product_of(query[:, cols], key_in[:, cols]).astype(jnp.float32)
    rate = rate_ref[0, :, cols]
    first = (lax.broadcasted_iota(jnp.int32, (SEGMENTS, LANES), 0) * steps).astype(jnp.float32)
    rates = rows_of(rate, modes)
    before = rows_of(before_ref[0, :, cols], modes)
    state = [
        carry_ref[pl.ds(m * SEGMENTS, SEGMENTS), cols] + jnp.exp(-rates[m] * first) * before[m]
        for m in range(modes)
    ]
    emit(rate, weight_ref[0, :, cols], state, scr, out_scr, length)
    return out_scr[...] + gain_ref[0, :, cols] * scr[...]


def gate(value, mixed):
    mixed = mixed.astype(jnp.bfloat16)
    return (value.astype(jnp.float32) * mixed.astype(jnp.float32)).astype(jnp.bfloat16)


def finish_kernel(
    query, key_in, rate_ref, weight_ref, gain_ref, carry_ref, before_ref, value, over_ref, out, scr, out_scr
):
    def body(cols):
        terms = own_terms(
            query, key_in, rate_ref, weight_ref, gain_ref, carry_ref, before_ref, scr, out_scr, cols
        )
        out[:, cols] = gate(value[:, cols], terms - over_ref[:, cols])

    over_tiles(query, body)


def own_kernel(
    query, key_in, rate_ref, weight_ref, gain_ref, carry_ref, before_ref, out, scr, out_scr
):
    def body(cols):
        out[:, cols] = own_terms(
            query, key_in, rate_ref, weight_ref, gain_ref, carry_ref, before_ref, scr, out_scr, cols
        )

    over_tiles(query, body)


def over_terms(past, rate_ref, weight_ref, span, scr, out_scr, cols):
    length = past.shape[0]
    scr[...] = past[:, cols].astype(jnp.float32)
    rate = rate_ref[0, :, cols]
    state = chain_segments(rate, scan_segments(rate, scr, length), length)
    row = lax.broadcasted_iota(jnp.int32, (SEGMENTS, LANES), 0)
    state = [shifted(s, 1, row) for s in state]
    weight = weight_ref[0, :, cols] * jnp.exp(-rate * float(span))
    emit(rate, weight, state, scr, out_scr, length)
    return out_scr[...]


def over_kernel(past, rate_ref, weight_ref, out, scr, out_scr, *, span):
    def body(cols):
        out[:, cols] = over_terms(past, rate_ref, weight_ref, span, scr, out_scr, cols)

    over_tiles(past, body)


def last_kernel(past, rate_ref, weight_ref, terms, value, partial, out, scr, out_scr, *, span):
    del partial

    def body(cols):
        over = over_terms(past, rate_ref, weight_ref, span, scr, out_scr, cols)
        out[:, cols] = gate(value[:, cols], terms[:, cols] - over)

    over_tiles(past, body)


def local(query, key_in, value, residues, decay_rates, skip_gain):
    length, channels = query.shape
    group, modes = residues.shape
    n_ch = channels // group
    wide = min(WIDE * LANES, group)
    part = length * n_ch
    span = FILTER_PARTS * part
    f32 = jnp.float32

    unit = channels // sum(SHARES)
    starts = [unit * sum(SHARES[:k]) for k in range(len(SHARES) + 1)]
    chunks = list(zip(starts[:-1], starts[1:]))
    pasts = [
        from_behind(product_of(query[:, a:b], key_in[:, a:b]), "ctx", FILTER_PARTS) for a, b in chunks
    ]

    def to_all(value):
        spread = jnp.broadcast_to(value[None], (n_ch,) + value.shape)
        return lax.all_to_all(spread, "ch", split_axis=0, concat_axis=0, tiled=True)

    own_rate = decay_rates.T
    rates = to_all(own_rate)
    weights = to_all(residues.T)
    gains = to_all(skip_gain[None])

    def tokens_spec(first, width=wide):
        return pl.BlockSpec((length, width), lambda t: (0, first // width + t))

    def table_spec(first, rows, width=wide):
        per = group // width
        return pl.BlockSpec(
            (1, rows, width), lambda t: ((first // width + t) // per, 0, (first // width + t) % per)
        )

    def carry_spec(first, width=wide):
        return pl.BlockSpec((modes * SEGMENTS, width), lambda t: (0, first // width + t))

    scratch = pltpu.VMEM((length, LANES), f32)

    carries, totals = pl.pallas_call(
        states_kernel,
        grid=(channels // wide,),
        in_specs=[tokens_spec(0), tokens_spec(0), table_spec(0, modes)],
        out_specs=[carry_spec(0), table_spec(0, modes)],
        out_shape=[
            jax.ShapeDtypeStruct((modes * SEGMENTS, channels), f32),
            jax.ShapeDtypeStruct((n_ch, modes, group), f32),
        ],
        scratch_shapes=[scratch],
        name="states",
    )(query, key_in, rates)

    blocks = lax.all_to_all(totals, "ch", split_axis=0, concat_axis=0, tiled=True)
    jump = jnp.exp(-own_rate * float(length))
    tails = [None] * n_ch
    weight_to_end = jnp.ones_like(own_rate)
    running = jnp.zeros_like(own_rate)
    for q in reversed(range(n_ch)):
        running = running + jnp.exp(-own_rate * float(length * (n_ch - 1 - q))) * blocks[q]
        tails[q] = running
    whole = tails[0]
    older = sum(
        jnp.exp(-own_rate * float(part * (j - 1))) * from_behind(whole, "ctx", j)
        for j in range(1, FILTER_PARTS)
    )
    oldest = from_behind(jnp.stack(tails), "ctx", FILTER_PARTS)
    heads = []
    running = jnp.zeros_like(own_rate)
    for q in range(n_ch):
        earlier = older + jnp.exp(-own_rate * float(part * (FILTER_PARTS - 1))) * oldest[q]
        heads.append(running + jnp.exp(-own_rate * float(length * q)) * earlier)
        running = jump * running + blocks[q]
    before = lax.all_to_all(jnp.stack(heads), "ch", split_axis=0, concat_axis=0, tiled=True)

    overs = []
    for (a, b), past in zip(chunks[:-1], pasts[:-1]):
        width = min(wide, b - a)
        overs.append(
            pl.pallas_call(
                functools.partial(over_kernel, span=span),
                grid=((b - a) // width,),
                in_specs=[tokens_spec(0, width), table_spec(a, modes, width), table_spec(a, modes, width)],
                out_specs=tokens_spec(0, width),
                out_shape=jax.ShapeDtypeStruct((length, b - a), f32),
                scratch_shapes=[scratch, scratch],
                name="over",
            )(past, rates, weights)
        )

    def own_specs(first, width):
        return [
            tokens_spec(first, width),
            tokens_spec(first, width),
            table_spec(first, modes, width),
            table_spec(first, modes, width),
            table_spec(first, 1, width),
            carry_spec(first, width),
            table_spec(first, modes, width),
        ]

    own_args = (query, key_in, rates, weights, gains, carries, before)
    result = None
    for (a, b), over in zip(chunks[:-1], overs):
        width = min(wide, b - a)
        extra = [] if result is None else [result]
        kernel = finish_kernel
        if extra:
            def kernel(*refs):
                finish_kernel(*refs[:9], *refs[10:])
        result = pl.pallas_call(
            kernel,
            grid=((b - a) // width,),
            in_specs=own_specs(a, width)
            + [tokens_spec(a, width), tokens_spec(0, width)]
            + [pl.BlockSpec(memory_space=pl.ANY)] * len(extra),
            out_specs=tokens_spec(a, width),
            out_shape=jax.ShapeDtypeStruct((length, channels), jnp.bfloat16),
            scratch_shapes=[scratch, scratch],
            input_output_aliases={9: 0} if extra else {},
            name="finish",
        )(*own_args, value, over, *extra)

    a, b = chunks[-1]
    width = min(wide, b - a)
    terms = pl.pallas_call(
        own_kernel,
        grid=((b - a) // width,),
        in_specs=own_specs(a, width),
        out_specs=tokens_spec(0, width),
        out_shape=jax.ShapeDtypeStruct((length, b - a), f32),
        scratch_shapes=[scratch, scratch],
        name="own",
    )(*own_args)
    return pl.pallas_call(
        functools.partial(last_kernel, span=span),
        grid=((b - a) // width,),
        in_specs=[
            tokens_spec(0, width),
            table_spec(a, modes, width),
            table_spec(a, modes, width),
            tokens_spec(0, width),
            tokens_spec(a, width),
            pl.BlockSpec(memory_space=pl.ANY),
        ],
        out_specs=tokens_spec(a, width),
        out_shape=jax.ShapeDtypeStruct((length, channels), jnp.bfloat16),
        scratch_shapes=[scratch, scratch],
        input_output_aliases={5: 0},
        name="last",
    )(pasts[-1], rates, weights, terms, value, result)


def solution(mesh):
    return jax.shard_map(
        local,
        mesh=mesh,
        in_specs=(
            P(("ctx", "ch"), None),
            P(("ctx", "ch"), None),
            P(("ctx", "ch"), None),
            P("ch", None),
            P("ch", None),
            P("ch"),
        ),
        out_specs=P(("ctx", "ch"), None),
        check_vma=False,
    )
```

```python
import functools

import jax
import jax.numpy as jnp
from jax import lax
from jax.experimental import pallas as pl
from jax.experimental.pallas import tpu as pltpu
from jax.sharding import PartitionSpec as P


FILTER_PARTS = 4
LANES = 128
SEGMENTS = 8
WIDE = 4
RAW_SHARES = (2, 1)
DONE_SHARES = (2, 2, 1)
F32 = jnp.float32


def from_behind(value, axis, steps):
    count = lax.axis_size(axis)
    return lax.ppermute(value, axis, [(source, source + steps) for source in range(count - steps)])


def row_of(table, m):
    return jnp.broadcast_to(table[pl.ds(m, 1), :], (SEGMENTS, LANES))


def shifted(value, steps):
    row = lax.broadcasted_iota(jnp.int32, value.shape, 0)
    return jnp.where(row >= steps, pltpu.roll(value, steps, 0), 0.0)


def step_rows(i):
    return pl.ds(i * SEGMENTS, SEGMENTS)


def over_tiles(width, body):
    def step(t, carry):
        body(t, pl.ds(pl.multiple_of(t * LANES, LANES), LANES))
        return carry

    lax.fori_loop(0, width // LANES, step, 0)


def scan_segments(table, tokens):
    modes = table.shape[1]
    steps = tokens.shape[0] // SEGMENTS
    decay = [row_of(table.at[0], m) for m in range(modes)]
    state = [tokens[step_rows(0), :]] * modes
    for i in range(1, steps):
        now = tokens[step_rows(i), :]
        state = [d * s + now for d, s in zip(decay, state)]
    chained = []
    for m in range(modes):
        value = state[m]
        for level in range(3):
            value = value + row_of(table.at[1 + level], m) * shifted(value, 1 << level)
        chained.append(value)
    return chained


def fill_jumps(table, rate, steps):
    table[0] = jnp.exp(-rate)
    for level in range(3):
        table[1 + level] = jnp.exp(-rate * float(steps << level))


def emit(table, weights, state, tokens, write):
    modes = table.shape[1]
    steps = tokens.shape[0] // SEGMENTS
    decay = [row_of(table.at[0], m) for m in range(modes)]
    weight = [row_of(weights, m) for m in range(modes)]
    for i in range(steps):
        now = tokens[step_rows(i), :]
        state = [d * s + now for d, s in zip(decay, state)]
        terms = [w * s for w, s in zip(weight, state)]
        while len(terms) > 1:
            terms = [a + b for a, b in zip(terms[::2], terms[1::2])]
        write(i, terms[0], now)


def product_kernel(query, key_in, order, *outs):
    product = (query[...].astype(F32) * key_in[...].astype(F32)).astype(jnp.bfloat16)
    product = jnp.dot(order[...], product, preferred_element_type=F32).astype(jnp.bfloat16)
    for out in outs:
        out[...] = product


def states_kernel(product, params, carry_out, state_out, tokens, table, *, modes):
    steps = product.shape[0] // SEGMENTS

    def body(t, cols):
        tokens[...] = product[:, cols].astype(F32)
        fill_jumps(table, params[0, pl.ds(0, modes), cols], steps)
        state = scan_segments(table, tokens)
        for m in range(modes):
            carry_out[pl.ds(m * SEGMENTS, SEGMENTS), cols] = shifted(state[m], 1)
            state_out[t, pl.ds(m, 1), :] = state[m][SEGMENTS - 1 :, :]

    over_tiles(product.shape[1], body)


def combine_kernel(blocks, rate, out, scr, *, window, length):
    count = blocks.shape[0]
    zero = jnp.zeros(blocks.shape[1:], F32)
    rates = rate[...]

    def at(level, b):
        return scr[level, b] if b >= 0 else zero

    for b in range(count):
        scr[0, b] = blocks[b]
    level, reach, covered = 0, 1, None
    total = None
    while True:
        if window & reach:
            if total is None:
                total, covered = [at(level, b) for b in range(count)], reach
            else:
                jump = jnp.exp(-rates * float(length * reach))
                old = total
                total = [
                    at(level, b) + (jump * old[b - reach] if b >= reach else zero) for b in range(count)
                ]
                covered += reach
        if covered == window:
            break
        jump = jnp.exp(-rates * float(length * reach))
        for b in range(count):
            scr[1 - level, b] = at(level, b) + jump * at(level, b - reach)
        level, reach = 1 - level, reach * 2
    out[0] = zero
    for b in range(1, count):
        out[b] = total[b - 1]


def over_kernel(flag, past, params, *rest, span, modes):
    out, tokens, table, weights = rest[-4:]
    steps = past.shape[0] // SEGMENTS

    @pl.when(flag[0] > 0)
    def _():
        def body(t, cols):
            tokens[...] = past[:, cols].astype(F32)
            rate = params[0, pl.ds(0, modes), cols]
            fill_jumps(table, rate, steps)
            weights[...] = params[0, pl.ds(modes, modes), cols] * jnp.exp(-rate * float(span))
            state = [shifted(s, 1) for s in scan_segments(table, tokens)]

            def write(i, value, now):
                out[step_rows(i), cols] = value

            emit(table, weights, state, tokens, write)

        over_tiles(past.shape[1], body)

    @pl.when(flag[0] == 0)
    def _():
        out[...] = jnp.zeros_like(out)


def ahead_kernel(flag, product, params, carry, out, tokens, table, weights, scr, *, span, modes):
    @pl.when(flag[1] > 0)
    def _():
        def body(t, cols):
            tokens[...] = product[:, cols].astype(F32)
            rate = params[0, pl.ds(0, modes), cols]
            table[0] = jnp.exp(-rate)
            weights[...] = params[0, pl.ds(modes, modes), cols] * jnp.exp(-rate * float(span))
            state = [carry[pl.ds(m * SEGMENTS, SEGMENTS), cols] for m in range(modes)]

            def write(i, value, now):
                scr[step_rows(i), :] = value

            emit(table, weights, state, tokens, write)
            out[:, cols] = scr[...].astype(jnp.bfloat16)

        over_tiles(product.shape[1], body)


def finish_kernel(product, params, carry, before, over, value, order, *rest, modes):
    out, tokens, table, weights, scr, mixed = rest[-6:]
    length, width = product.shape
    steps = length // SEGMENTS

    def place(t):
        cols = pl.ds(pl.multiple_of(t * LANES, LANES), LANES)
        plain = lax.dot_general(
            order[...], mixed[:, cols], (((0,), (0,)), ((), ())), preferred_element_type=F32
        )
        out[:, cols] = (value[:, cols].astype(F32) * plain).astype(jnp.bfloat16)

    def body(t, cols):
        place(jnp.maximum(t - 1, 0))
        tokens[...] = product[:, cols].astype(F32)
        rate = params[0, pl.ds(0, modes), cols]
        table[0] = jnp.exp(-rate)
        weights[...] = params[0, pl.ds(modes, modes), cols]
        gain = jnp.broadcast_to(params[0, pl.ds(2 * modes, 1), cols], (SEGMENTS, LANES))
        first = (lax.broadcasted_iota(jnp.int32, (SEGMENTS, LANES), 0) * steps).astype(F32)
        state = []
        for m in range(modes):
            own_rate = jnp.broadcast_to(params[0, pl.ds(m, 1), cols], (SEGMENTS, LANES))
            ahead = jnp.broadcast_to(before[t, pl.ds(m, 1), :], (SEGMENTS, LANES))
            state.append(carry[pl.ds(m * SEGMENTS, SEGMENTS), cols] + jnp.exp(-own_rate * first) * ahead)

        def write(i, value, now):
            scr[step_rows(i), :] = value + gain * now

        emit(table, weights, state, tokens, write)
        mixed[:, cols] = (scr[...] - over[:, cols].astype(F32)).astype(jnp.bfloat16)

    mixed[:, pl.ds(0, LANES)] = jnp.zeros((length, LANES), jnp.bfloat16)
    over_tiles(width, body)
    place(width // LANES - 1)


def shard_program(query, key_in, value, residues, decay_rates, skip_gain):
    length, channels = query.shape
    group, modes = residues.shape
    n_ch, n_ctx = lax.axis_size("ch"), lax.axis_size("ctx")
    devices = n_ctx * n_ch
    per = channels // devices
    wide = min(WIDE * LANES, group)
    part = length * n_ch
    span = FILTER_PARTS * part
    steps = length // SEGMENTS
    tiles = channels // LANES
    bf16 = jnp.bfloat16

    unit = channels // sum(RAW_SHARES + DONE_SHARES)
    shares = (RAW_SHARES + DONE_SHARES)
    unit = channels // 8
    edges = [unit * sum(shares[:k]) for k in range(len(shares) + 1)]
    chunks = list(zip(edges[:-1], edges[1:]))
    raw, done = chunks[: len(RAW_SHARES)], chunks[len(RAW_SHARES) :]

    ctx = lax.axis_index("ctx")
    flags = jnp.stack([ctx >= FILTER_PARTS, ctx + FILTER_PARTS < n_ctx]).astype(jnp.int32)
    smem = pl.BlockSpec(memory_space=pltpu.SMEM)
    hbm = pl.BlockSpec(memory_space=pl.ANY)

    row = jnp.arange(length, dtype=jnp.int32)[:, None]
    col = jnp.arange(length, dtype=jnp.int32)[None, :]
    order = (row % SEGMENTS * steps + row // SEGMENTS == col).astype(bf16)
    order_spec = pl.BlockSpec((length, length), lambda t: (0, 0))

    def tokens_spec(first, width=wide):
        return pl.BlockSpec((length, width), lambda t: (0, first // width + t))

    rows = -(-(2 * modes + 1) // SEGMENTS) * SEGMENTS
    per_group = group // wide

    def params_spec(first):
        return pl.BlockSpec(
            (1, rows, wide), lambda t: ((first // wide + t) // per_group, 0, (first // wide + t) % per_group)
        )

    def carry_spec(first):
        return pl.BlockSpec((modes * SEGMENTS, wide), lambda t: (0, first // wide + t))

    def states_spec(first):
        return pl.BlockSpec((wide // LANES, modes, LANES), lambda t: (first // wide + t, 0, 0))

    tokens_scr = pltpu.VMEM((length, LANES), F32)
    table_scr = pltpu.VMEM((4, modes, LANES), F32)
    weights_scr = pltpu.VMEM((modes, LANES), F32)

    def call(kernel, cols, in_specs, out_specs, out_shape, scratch, args, aliases=None):
        return pl.pallas_call(
            kernel,
            grid=((cols[1] - cols[0]) // wide,),
            in_specs=in_specs,
            out_specs=out_specs,
            out_shape=out_shape,
            scratch_shapes=scratch,
            input_output_aliases=aliases or {},
        )(*args)

    def shape(columns, dtype):
        return jax.ShapeDtypeStruct((length, columns), dtype)

    packed = jnp.concatenate(
        [decay_rates.T, residues.T, skip_gain[None], jnp.zeros((rows - 2 * modes - 1, group), F32)]
    )
    packed = jnp.broadcast_to(packed[None], (n_ch,) + packed.shape)
    params = lax.all_to_all(packed, "ch", split_axis=0, concat_axis=0, tiled=True)

    product, pasts = None, []
    ends = raw + [(raw[-1][1], channels)]
    for k, (a, b) in enumerate(ends):
        extra = [] if product is None else [product]
        sent = k < len(raw)

        def kernel(q, k_in, o, *refs, skip=len(extra)):
            product_kernel(q, k_in, o, *refs[skip:])

        outs = call(
            kernel,
            (a, b),
            [tokens_spec(a), tokens_spec(a), order_spec] + [hbm] * len(extra),
            [tokens_spec(a)] + [tokens_spec(0)] * sent,
            [shape(channels, bf16)] + [shape(b - a, bf16)] * sent,
            [],
            (query, key_in, order, *extra),
            {3: 0} if extra else None,
        )
        product = outs[0]
        if sent:
            pasts.append(from_behind(outs[1], "ctx", FILTER_PARTS))

    carries, totals = call(
        functools.partial(states_kernel, modes=modes),
        (0, channels),
        [tokens_spec(0), params_spec(0)],
        [carry_spec(0), states_spec(0)],
        [
            jax.ShapeDtypeStruct((modes * SEGMENTS, channels), F32),
            jax.ShapeDtypeStruct((tiles, modes, LANES), F32),
        ],
        [tokens_scr, table_scr],
        (product, params),
    )

    def swap(blocks):
        return lax.all_to_all(blocks, ("ctx", "ch"), split_axis=0, concat_axis=0, tiled=True)

    if per >= LANES:
        chips = (per // LANES, modes, LANES)
        totals = totals.reshape((devices,) + chips)
    else:
        chips = (modes, per)
        totals = totals.reshape(tiles, modes, LANES // per, per).transpose(0, 2, 1, 3).reshape((devices,) + chips)
    blocks = swap(totals)
    mine = (ctx * n_ch + lax.axis_index("ch")) * per
    rate_mine = lax.dynamic_slice(
        params, (mine // group, 0, mine % group), (1, modes, per)
    ).reshape(modes, per)
    if per >= LANES:
        rate_mine = rate_mine.reshape(modes, per // LANES, LANES).transpose(1, 0, 2)
    heads = pl.pallas_call(
        functools.partial(combine_kernel, window=FILTER_PARTS * n_ch, length=length),
        out_shape=jax.ShapeDtypeStruct(blocks.shape, F32),
        scratch_shapes=[pltpu.VMEM((2,) + blocks.shape, F32)],
        name="combine",
    )(blocks, rate_mine)
    before = swap(heads)
    if per >= LANES:
        before = before.reshape(tiles, modes, LANES)
    else:
        before = before.reshape(tiles, LANES // per, modes, per).transpose(0, 2, 1, 3).reshape(tiles, modes, LANES)

    aheads = []
    for a, b in done:
        ahead = call(
            functools.partial(ahead_kernel, span=span, modes=modes),
            (a, b),
            [smem, tokens_spec(a), params_spec(a), carry_spec(a)],
            tokens_spec(0),
            shape(b - a, bf16),
            [tokens_scr, table_scr, weights_scr, tokens_scr],
            (flags, product, params, carries),
        )
        aheads.append(from_behind(ahead, "ctx", FILTER_PARTS))

    over = None
    for (a, b), past in zip(raw, pasts):
        extra = [] if over is None else [over]
        over = call(
            functools.partial(over_kernel, span=span, modes=modes),
            (a, b),
            [smem, tokens_spec(0), params_spec(a)] + [hbm] * len(extra),
            tokens_spec(a),
            shape(raw[-1][1], F32),
            [tokens_scr, table_scr, weights_scr],
            (flags, past, params, *extra),
            {3: 0} if extra else None,
        )

    result = None
    last = [((0, raw[-1][1]), over)] + list(zip(done, aheads))
    for (a, b), past in last:
        extra = [] if result is None else [result]
        result = call(
            functools.partial(finish_kernel, modes=modes),
            (a, b),
            [
                tokens_spec(a),
                params_spec(a),
                carry_spec(a),
                states_spec(a),
                tokens_spec(0),
                tokens_spec(a),
                order_spec,
            ]
            + [hbm] * len(extra),
            tokens_spec(a),
            shape(channels, bf16),
            [tokens_scr, table_scr, weights_scr, tokens_scr, pltpu.VMEM((length, wide), bf16)],
            (product, params, carries, before, past, value, order, *extra),
            {7: 0} if extra else None,
        )
    return result


def solution(mesh):
    return jax.shard_map(
        shard_program,
        mesh=mesh,
        in_specs=(
            P(("ctx", "ch"), None),
            P(("ctx", "ch"), None),
            P(("ctx", "ch"), None),
            P("ch", None),
            P("ch", None),
            P("ch"),
        ),
        out_specs=P(("ctx", "ch"), None),
        check_vma=False,
    )
```

```python
import functools
import math

import jax
import jax.numpy as jnp
from jax import lax
from jax.experimental import pallas as pl
from jax.experimental.pallas import tpu as pltpu
from jax.sharding import PartitionSpec as P


FILTER_PARTS = 4
LANES = 128
SEGMENTS = 8
RAW_SHARES = (2, 2)
DONE_SHARES = (2, 2)
VMEM_BYTES = 16 << 20
F32 = jnp.float32


def from_behind(value, axis, steps):
    count = lax.axis_size(axis)
    return lax.ppermute(value, axis, [(source, source + steps) for source in range(count - steps)])


def row_of(table, m):
    return jnp.broadcast_to(table[pl.ds(m, 1), :], (SEGMENTS, LANES))


def shifted(value, steps):
    row = lax.broadcasted_iota(jnp.int32, value.shape, 0)
    return jnp.where(row >= steps, pltpu.roll(value, steps, 0), 0.0)


def step_rows(i):
    return pl.ds(i * SEGMENTS, SEGMENTS)


def lanes(start):
    return pl.ds(pl.multiple_of(start, LANES), LANES)


def over_tiles(width, body):
    def step(t, carry):
        body(t)
        return carry

    lax.fori_loop(0, width // LANES, step, 0)


def params_at(params, tile, first, count):
    per = params.shape[2] // LANES
    return params.at[tile // per, pl.ds(first, count), lanes(tile % per * LANES)]


def scan_segments(table, tokens):
    modes = table.shape[1]
    steps = tokens.shape[0] // SEGMENTS
    decay = [row_of(table.at[0], m) for m in range(modes)]
    state = [tokens[step_rows(0), :]] * modes
    for i in range(1, steps):
        now = tokens[step_rows(i), :]
        state = [d * s + now for d, s in zip(decay, state)]
    chained = []
    for m in range(modes):
        value = state[m]
        for level in range(3):
            value = value + row_of(table.at[1 + level], m) * shifted(value, 1 << level)
        chained.append(value)
    return chained


def fill_jumps(table, rate, steps):
    table[0] = jnp.exp(-rate)
    for level in range(3):
        table[1 + level] = jnp.exp(-rate * float(steps << level))


def emit(table, weights, state, tokens, write):
    modes = table.shape[1]
    steps = tokens.shape[0] // SEGMENTS
    decay = [row_of(table.at[0], m) for m in range(modes)]
    weight = [row_of(weights, m) for m in range(modes)]
    for i in range(steps):
        now = tokens[step_rows(i), :]
        state = [d * s + now for d, s in zip(decay, state)]
        terms = [w * s for w, s in zip(weight, state)]
        while len(terms) > 1:
            terms = [a + b for a, b in zip(terms[::2], terms[1::2])]
        write(i, terms[0], now)


def fill_order(order):
    length = order.shape[0]
    row = lax.broadcasted_iota(jnp.int32, order.shape, 0)
    col = lax.broadcasted_iota(jnp.int32, order.shape, 1)
    order[...] = jnp.where(row % SEGMENTS * (length // SEGMENTS) + row // SEGMENTS == col, 1.0, 0.0).astype(
        order.dtype
    )


def product_kernel(query, key_in, *refs, first):
    outs, order = refs[:-1], refs[-1]
    fill_order(order)
    start = first
    for out in outs:
        width = out.shape[1]
        wide = math.gcd(width, 4 * LANES)
        for at in range(0, width, wide):
            cols = pl.ds(start + at, wide)
            product = (query[:, cols].astype(F32) * key_in[:, cols].astype(F32)).astype(jnp.bfloat16)
            out[:, pl.ds(at, wide)] = jnp.dot(
                order[...], product, preferred_element_type=F32
            ).astype(jnp.bfloat16)
        start += width


def states_kernel(*refs, modes, count):
    products, params = refs[:count], refs[count]
    carries, state_out = refs[count + 1 : 2 * count + 1], refs[2 * count + 1]
    tokens, table = refs[2 * count + 2 :]
    first = 0
    for product, carry_out in zip(products, carries):
        steps = product.shape[0] // SEGMENTS

        def body(t, first=first, product=product, carry_out=carry_out):
            cols = lanes(t * LANES)
            tokens[...] = product[:, cols].astype(F32)
            fill_jumps(table, params_at(params, first + t, 0, modes)[...], steps)
            state = scan_segments(table, tokens)
            for m in range(modes):
                carry_out[pl.ds(m * SEGMENTS, SEGMENTS), cols] = shifted(state[m], 1)
                state_out[first + t, pl.ds(m, 1), :] = state[m][SEGMENTS - 1 :, :]

        over_tiles(product.shape[1], body)
        first += product.shape[1] // LANES


def combine_kernel(blocks, rate, out, scr, *, window, length):
    count = blocks.shape[0]
    zero = jnp.zeros(blocks.shape[1:], F32)
    rates = rate[...]

    def at(level, b):
        return scr[level, b] if b >= 0 else zero

    for b in range(count):
        scr[0, b] = blocks[b]
    level, reach, covered = 0, 1, None
    total = None
    while True:
        if window & reach:
            if total is None:
                total, covered = [at(level, b) for b in range(count)], reach
            else:
                jump = jnp.exp(-rates * float(length * reach))
                old = total
                total = [
                    at(level, b) + (jump * old[b - reach] if b >= reach else zero) for b in range(count)
                ]
                covered += reach
        if covered == window:
            break
        jump = jnp.exp(-rates * float(length * reach))
        for b in range(count):
            scr[1 - level, b] = at(level, b) + jump * at(level, b - reach)
        level, reach = 1 - level, reach * 2
    out[0] = zero
    for b in range(1, count):
        out[b] = total[b - 1]


def over_kernel(past, params, out, tokens, table, weights, *, span, modes, first):
    steps = past.shape[0] // SEGMENTS
    needed = lax.axis_index("ctx") >= FILTER_PARTS

    @pl.when(needed)
    def _():
        def body(t):
            cols = lanes(t * LANES)
            tokens[...] = past[:, cols].astype(F32)
            rate = params_at(params, first + t, 0, modes)[...]
            fill_jumps(table, rate, steps)
            weights[...] = params_at(params, first + t, modes, modes)[...] * jnp.exp(-rate * float(span))
            state = [shifted(s, 1) for s in scan_segments(table, tokens)]

            def write(i, value, now):
                out[step_rows(i), cols] = value

            emit(table, weights, state, tokens, write)

        over_tiles(past.shape[1], body)

    @pl.when(jnp.logical_not(needed))
    def _():
        out[...] = jnp.zeros_like(out)


def ahead_kernel(product, params, carry, out, tokens, table, weights, scr, *, span, modes, first, n_ctx):
    @pl.when(lax.axis_index("ctx") + FILTER_PARTS < n_ctx)
    def _():
        def body(t):
            cols = lanes(t * LANES)
            tokens[...] = product[:, cols].astype(F32)
            rate = params_at(params, first + t, 0, modes)[...]
            table[0] = jnp.exp(-rate)
            weights[...] = params_at(params, first + t, modes, modes)[...] * jnp.exp(-rate * float(span))
            state = [carry[pl.ds(m * SEGMENTS, SEGMENTS), cols] for m in range(modes)]

            def write(i, value, now):
                scr[step_rows(i), :] = value

            emit(table, weights, state, tokens, write)
            out[:, cols] = scr[...].astype(jnp.bfloat16)

        over_tiles(product.shape[1], body)


def gated(order, mixed, value):
    plain = lax.dot_general(order[...], mixed, (((0,), (0,)), ((), ())), preferred_element_type=F32)
    return (value.astype(F32) * plain).astype(jnp.bfloat16)


def finish_kernel(*refs, modes, count):
    products, params = refs[:count], refs[count]
    carries, before, value = refs[count + 1 : 2 * count + 1], refs[2 * count + 1], refs[2 * count + 2]
    overs = refs[2 * count + 3 : 3 * count + 2]
    out, rest, tokens, table, weights, scr, order, mixed, done, sems = refs[3 * count + 2 :]
    length = value.shape[0]
    steps = length // SEGMENTS
    fill_order(order)
    copies = [None, None]
    first = 0
    for k in range(count):
        product, carry = products[k], carries[k]
        width = product.shape[1]
        slot = k % 2
        last = k == count - 1
        if copies[slot] is not None and not last:
            copies[slot].wait()
            copies[slot] = None

        def place(t, first=first, slot=slot):
            cols = lanes(t * LANES)
            done[slot, :, cols] = gated(order, mixed[:, cols], value[:, lanes((first + t) * LANES)])

        def body(t, first=first, product=product, carry=carry, last=last, place=place, k=k):
            cols = lanes(t * LANES)
            if not last:
                place(jnp.maximum(t - 1, 0))
            tokens[...] = product[:, cols].astype(F32)
            rates = params_at(params, first + t, 0, modes)
            table[0] = jnp.exp(-rates[...])
            weights[...] = params_at(params, first + t, modes, modes)[...]
            gain = row_of(params_at(params, first + t, 2 * modes, 1), 0)
            begin = (lax.broadcasted_iota(jnp.int32, (SEGMENTS, LANES), 0) * steps).astype(F32)
            state = []
            for m in range(modes):
                ahead = row_of(before.at[first + t], m)
                state.append(
                    carry[pl.ds(m * SEGMENTS, SEGMENTS), cols] + jnp.exp(-row_of(rates, m) * begin) * ahead
                )
            if last:

                def write(i, value, now):
                    rest[step_rows(i), cols] = value + gain * now

                emit(table, weights, state, tokens, write)
            else:

                def write(i, value, now):
                    scr[step_rows(i), :] = value + gain * now

                emit(table, weights, state, tokens, write)
                mixed[:, cols] = (scr[...] - overs[k][:, cols].astype(F32)).astype(jnp.bfloat16)

        if k == 0:
            mixed[:, pl.ds(0, LANES)] = jnp.zeros((length, LANES), jnp.bfloat16)
        over_tiles(width, body)
        if not last:
            place(width // LANES - 1)
            copies[slot] = pltpu.make_async_copy(
                done.at[slot, :, pl.ds(0, width)], out.at[:, pl.ds(first * LANES, width)], sems.at[slot]
            )
            copies[slot].start()
        first += width // LANES
    for copy in copies:
        if copy is not None:
            copy.wait()


def last_kernel(rest, over, value, partial, out, order, done, sem):
    del partial
    _, width = rest.shape
    first = value.shape[1] - width
    fill_order(order)
    wide = math.gcd(width, 4 * LANES)
    copies = []
    for k, at in enumerate(range(0, width, wide)):
        cols = pl.ds(at, wide)
        mixed = (rest[:, cols] - over[:, cols].astype(F32)).astype(jnp.bfloat16)
        done[:, cols] = gated(order, mixed, value[:, pl.ds(first + at, wide)])
        copies.append(
            pltpu.make_async_copy(done.at[:, cols], out.at[:, pl.ds(first + at, wide)], sem.at[k])
        )
        copies[-1].start()
    for copy in copies:
        copy.wait()


def shard_program(query, key_in, value, residues, decay_rates, skip_gain):
    length, channels = query.shape
    group, modes = residues.shape
    n_ch, n_ctx = lax.axis_size("ch"), lax.axis_size("ctx")
    devices = n_ctx * n_ch
    per = channels // devices
    span = FILTER_PARTS * length * n_ch
    tiles = channels // LANES
    bf16 = jnp.bfloat16

    shares = RAW_SHARES + DONE_SHARES
    unit = channels // sum(shares)
    widths = [unit * share for share in shares]
    firsts = [sum(widths[:k]) for k in range(len(widths))]
    count, n_raw = len(widths), len(RAW_SHARES)

    vmem = pl.BlockSpec(memory_space=pltpu.VMEM)
    anywhere = pl.BlockSpec(memory_space=pl.ANY)

    def shape(rows, columns, dtype=F32):
        return jax.ShapeDtypeStruct((rows, columns), dtype)

    tokens_scr = pltpu.VMEM((length, LANES), F32)
    table_scr = pltpu.VMEM((4, modes, LANES), F32)
    weights_scr = pltpu.VMEM((modes, LANES), F32)
    order_scr = pltpu.VMEM((length, length), bf16)

    def call(kernel, out_shape, scratch, args, **options):
        specs = dict(in_specs=[vmem] * len(args), out_specs=jax.tree.map(lambda _: vmem, out_shape))
        specs.update(options)
        return pl.pallas_call(
            kernel,
            out_shape=out_shape,
            scratch_shapes=scratch,
            compiler_params=pltpu.CompilerParams(vmem_limit_bytes=VMEM_BYTES),
            **specs,
        )(*args)

    rows = -(-(2 * modes + 1) // SEGMENTS) * SEGMENTS
    packed = jnp.concatenate(
        [decay_rates.T, residues.T, skip_gain[None], jnp.zeros((rows - 2 * modes - 1, group), F32)]
    )
    packed = jnp.broadcast_to(packed[None], (n_ch,) + packed.shape)
    params = lax.all_to_all(packed, "ch", split_axis=0, concat_axis=0, tiled=True)

    products, pasts = [], []
    batches = [[k] for k in range(n_raw)] + [list(range(n_raw, count))]
    for k, batch in enumerate(batches):
        products += call(
            functools.partial(product_kernel, first=firsts[batch[0]]),
            [shape(length, widths[j], bf16) for j in batch],
            [order_scr],
            (query, key_in),
        )
        if k < n_raw:
            pasts.append(from_behind(products[k], "ctx", FILTER_PARTS))

    *carries, totals = call(
        functools.partial(states_kernel, modes=modes, count=count),
        [shape(modes * SEGMENTS, width) for width in widths]
        + [jax.ShapeDtypeStruct((tiles, modes, LANES), F32)],
        [tokens_scr, table_scr],
        (*products, params),
    )

    def swap(blocks):
        return lax.all_to_all(blocks, ("ctx", "ch"), split_axis=0, concat_axis=0, tiled=True)

    mine = (lax.axis_index("ctx") * n_ch + lax.axis_index("ch")) * per
    rate_mine = lax.dynamic_slice(params, (mine // group, 0, mine % group), (1, modes, per))
    rate_mine = rate_mine.reshape(modes, per)
    split = max(per // LANES, 1)
    per_block = (split, modes, per // split)
    rate_mine = rate_mine.reshape(modes, split, per // split).transpose(1, 0, 2)
    if per >= LANES:
        totals = totals.reshape((devices,) + per_block)
    else:
        totals = totals.reshape(tiles, modes, LANES // per, per).transpose(0, 2, 1, 3)
        totals = totals.reshape((devices,) + per_block)
    blocks = swap(totals)
    heads = call(
        functools.partial(combine_kernel, window=FILTER_PARTS * n_ch, length=length),
        jax.ShapeDtypeStruct(blocks.shape, F32),
        [pltpu.VMEM((2,) + blocks.shape, F32)],
        (blocks, rate_mine),
    )
    before = swap(heads)
    if per < LANES:
        before = before.reshape(tiles, LANES // per, modes, per).transpose(0, 2, 1, 3)
    before = before.reshape(tiles, modes, LANES)

    overs = []
    for k in range(n_raw):
        overs.append(
            call(
                functools.partial(over_kernel, span=span, modes=modes, first=firsts[k] // LANES),
                shape(length, widths[k]),
                [tokens_scr, table_scr, weights_scr],
                (pasts[k], params),
            )
        )
    for k in range(n_raw, count):
        ahead = call(
            functools.partial(
                ahead_kernel, span=span, modes=modes, first=firsts[k] // LANES, n_ctx=n_ctx
            ),
            shape(length, widths[k], bf16),
            [tokens_scr, table_scr, weights_scr, tokens_scr],
            (products[k], params, carries[k]),
        )
        overs.append(from_behind(ahead, "ctx", FILTER_PARTS))

    widest = max(widths)
    partial, rest = call(
        functools.partial(finish_kernel, modes=modes, count=count),
        [shape(length, channels, bf16), shape(length, widths[-1])],
        [
            tokens_scr,
            table_scr,
            weights_scr,
            tokens_scr,
            order_scr,
            pltpu.VMEM((length, widest), bf16),
            pltpu.VMEM((2, length, widest), bf16),
            pltpu.SemaphoreType.DMA((2,)),
        ],
        (*products, params, *carries, before, value, *overs[:-1]),
        out_specs=[anywhere, vmem],
    )
    return call(
        last_kernel,
        shape(length, channels, bf16),
        [order_scr, pltpu.VMEM((length, widths[-1]), bf16), pltpu.SemaphoreType.DMA((8,))],
        (rest, overs[-1], value, partial),
        in_specs=[vmem, vmem, vmem, anywhere],
        out_specs=anywhere,
        input_output_aliases={3: 0},
    )


def solution(mesh):
    return jax.shard_map(
        shard_program,
        mesh=mesh,
        in_specs=(
            P(("ctx", "ch"), None),
            P(("ctx", "ch"), None),
            P(("ctx", "ch"), None),
            P("ch", None),
            P("ch", None),
            P("ch"),
        ),
        out_specs=P(("ctx", "ch"), None),
        check_vma=False,
    )
```

```python
import functools
import math

import jax
import jax.numpy as jnp
from jax import lax
from jax.experimental import pallas as pl
from jax.experimental.pallas import tpu as pltpu
from jax.sharding import PartitionSpec as P


FILTER_PARTS = 4
LANES = 128
SEGMENTS = 8
RAW_SHARES = (2, 2)
DONE_SHARES = (2, 2)
VMEM_BYTES = 16 << 20
F32 = jnp.float32


def from_behind(value, axis, steps):
    count = lax.axis_size(axis)
    return lax.ppermute(value, axis, [(source, source + steps) for source in range(count - steps)])


def ring(parts, axis):
    count = lax.axis_size(axis)
    moved = []
    for k, part in enumerate(parts):
        pairs = [(source, (source + k) % count) for source in range(count)]
        moved.append(lax.ppermute(part, axis, pairs) if k else part)
    return moved


def from_ring(refs, out):
    count = len(refs)
    mine = lax.axis_index("ch")
    for k, ref in enumerate(refs):
        out[(mine - k + count) % count] = ref[...]


def to_ring(whole, refs):
    count = len(refs)
    mine = lax.axis_index("ch")
    for k, ref in enumerate(refs):
        ref[...] = whole[(mine + k) % count]


def row_of(table, m):
    return jnp.broadcast_to(table[pl.ds(m, 1), :], (SEGMENTS, LANES))


def shifted(value, steps):
    row = lax.broadcasted_iota(jnp.int32, value.shape, 0)
    return jnp.where(row >= steps, pltpu.roll(value, steps, 0), 0.0)


def step_rows(i):
    return pl.ds(i * SEGMENTS, SEGMENTS)


def lanes(start):
    return pl.ds(pl.multiple_of(start, LANES), LANES)


def over_tiles(width, body):
    def step(t, carry):
        body(t)
        return carry

    lax.fori_loop(0, width // LANES, step, 0)


def at_tile(table, tile, first=0, count=None):
    per = table.shape[2] // LANES
    count = table.shape[1] if count is None else count
    return table.at[tile // per, pl.ds(first, count), lanes(tile % per * LANES)]


def scan_segments(table, tokens):
    modes = table.shape[1]
    steps = tokens.shape[0] // SEGMENTS
    decay = [row_of(table.at[0], m) for m in range(modes)]
    state = [tokens[step_rows(0), :]] * modes
    for i in range(1, steps):
        now = tokens[step_rows(i), :]
        state = [d * s + now for d, s in zip(decay, state)]
    chained = []
    for m in range(modes):
        value = state[m]
        for level in range(3):
            value = value + row_of(table.at[1 + level], m) * shifted(value, 1 << level)
        chained.append(value)
    return chained


def fill_jumps(table, rate, steps):
    table[0] = jnp.exp(-rate)
    for level in range(3):
        table[1 + level] = jnp.exp(-rate * float(steps << level))


def emit(table, weights, state, tokens, write):
    modes = table.shape[1]
    steps = tokens.shape[0] // SEGMENTS
    decay = [row_of(table.at[0], m) for m in range(modes)]
    weight = [row_of(weights, m) for m in range(modes)]
    for i in range(steps):
        now = tokens[step_rows(i), :]
        state = [d * s + now for d, s in zip(decay, state)]
        terms = [w * s for w, s in zip(weight, state)]
        while len(terms) > 1:
            terms = [a + b for a, b in zip(terms[::2], terms[1::2])]
        write(i, terms[0], now)


def fill_order(order, back=False):
    length = order.shape[0]
    row = lax.broadcasted_iota(jnp.int32, order.shape, 0)
    col = lax.broadcasted_iota(jnp.int32, order.shape, 1)
    inner = length // SEGMENTS if back else SEGMENTS
    order[...] = jnp.where(row % inner * (length // inner) + row // inner == col, 1.0, 0.0).astype(order.dtype)


def product_kernel(query, key_in, *refs, first):
    outs, order = refs[:-1], refs[-1]
    fill_order(order)
    start = first
    for out in outs:
        width = out.shape[1]
        wide = math.gcd(width, 4 * LANES)
        for at in range(0, width, wide):
            cols = pl.ds(start + at, wide)
            product = (query[:, cols].astype(F32) * key_in[:, cols].astype(F32)).astype(jnp.bfloat16)
            out[:, pl.ds(at, wide)] = jnp.dot(
                order[...], product, preferred_element_type=F32
            ).astype(jnp.bfloat16)
        start += width


def states_kernel(*refs, count, n_ch):
    products, parts = refs[:count], refs[count : count + n_ch]
    carries, sums = refs[count + n_ch : 2 * count + n_ch], refs[2 * count + n_ch : 2 * count + 2 * n_ch]
    rates, tokens, table, totals = refs[2 * count + 2 * n_ch :]
    from_ring(parts, rates)
    modes = rates.shape[1]
    first = 0
    for product, carry_out in zip(products, carries):
        steps = product.shape[0] // SEGMENTS

        def body(t, first=first, product=product, carry_out=carry_out):
            cols = lanes(t * LANES)
            tokens[...] = product[:, cols].astype(F32)
            fill_jumps(table, at_tile(rates, first + t)[...], steps)
            state = scan_segments(table, tokens)
            into = at_tile(totals, first + t)
            for m in range(modes):
                carry_out[pl.ds(m * SEGMENTS, SEGMENTS), cols] = shifted(state[m], 1)
                into[pl.ds(m, 1), :] = state[m][SEGMENTS - 1 :, :]

        over_tiles(product.shape[1], body)
        first += product.shape[1] // LANES
    to_ring(totals, sums)


def assemble_kernel(*refs):
    from_ring(refs[:-1], refs[-1])


def tails_kernel(*refs, length):
    *parts, rate, blocks, tails, whole = refs
    from_ring(parts, blocks)
    count = len(parts)
    running = None
    for q in reversed(range(count)):
        now = blocks[q]
        if running is not None:
            now = running + jnp.exp(-rate[...] * float(length * (count - 1 - q))) * now
        running = now
        tails[q] = running
    whole[...] = running


def heads_kernel(*refs, length, parts):
    blocks, rate, oldest, *rest = refs
    wholes, outs, heads = rest[: parts - 1], rest[parts - 1 : -1], rest[-1]
    count = blocks.shape[0]
    rates = rate[...]
    older = wholes[0][...]
    for j in range(1, parts - 1):
        older = older + jnp.exp(-rates * float(length * count * j)) * wholes[j][...]
    last = jnp.exp(-rates * float(length * count * (parts - 1)))
    jump = jnp.exp(-rates * float(length))
    running = None
    for q in range(count):
        earlier = older + last * oldest[q]
        if running is None:
            heads[q] = earlier
            running = blocks[q]
        else:
            heads[q] = running + jnp.exp(-rates * float(length * q)) * earlier
            running = jump * running + blocks[q]
    to_ring(heads, outs)


def over_kernel(past, rates, weighing, out, tokens, table, weights, *, span, first):
    steps = past.shape[0] // SEGMENTS
    modes = rates.shape[1]
    needed = lax.axis_index("ctx") >= FILTER_PARTS

    @pl.when(needed)
    def _():
        def body(t):
            cols = lanes(t * LANES)
            tokens[...] = past[:, cols].astype(F32)
            rate = at_tile(rates, first + t)[...]
            fill_jumps(table, rate, steps)
            weights[...] = at_tile(weighing, first + t, 0, modes)[...] * jnp.exp(-rate * float(span))
            state = [shifted(s, 1) for s in scan_segments(table, tokens)]

            def write(i, value, now):
                out[step_rows(i), cols] = value

            emit(table, weights, state, tokens, write)

        over_tiles(past.shape[1], body)

    @pl.when(jnp.logical_not(needed))
    def _():
        out[...] = jnp.zeros_like(out)


def ahead_kernel(product, rates, weighing, carry, out, tokens, table, weights, scr, *, span, first, n_ctx):
    modes = rates.shape[1]

    @pl.when(lax.axis_index("ctx") + FILTER_PARTS < n_ctx)
    def _():
        def body(t):
            cols = lanes(t * LANES)
            tokens[...] = product[:, cols].astype(F32)
            rate = at_tile(rates, first + t)[...]
            table[0] = jnp.exp(-rate)
            weights[...] = at_tile(weighing, first + t, 0, modes)[...] * jnp.exp(-rate * float(span))
            state = [carry[pl.ds(m * SEGMENTS, SEGMENTS), cols] for m in range(modes)]

            def write(i, value, now):
                scr[step_rows(i), :] = value

            emit(table, weights, state, tokens, write)
            out[:, cols] = scr[...].astype(jnp.bfloat16)

        over_tiles(product.shape[1], body)


def gated(back, mixed, value):
    plain = jnp.dot(back[...], mixed, preferred_element_type=F32)
    return (value.astype(F32) * plain).astype(jnp.bfloat16)


def finish_kernel(*refs, count, n_ch):
    products, carries, overs = refs[:count], refs[count : 2 * count], refs[2 * count : 3 * count - 1]
    refs = refs[3 * count - 1 :]
    befores, (rates, weighing, value, out, rest) = refs[:n_ch], refs[n_ch : n_ch + 5]
    tokens, table, weights, scr, back, before, mixed, done, sems = refs[n_ch + 5 :]
    modes = rates.shape[1]
    length = value.shape[0]
    steps = length // SEGMENTS
    from_ring(befores, before)
    fill_order(back, True)
    copies = [None, None]
    first = 0
    for k in range(count):
        product, carry = products[k], carries[k]
        width = product.shape[1]
        slot = k % 2
        last = k == count - 1

        def body(t, first=first, product=product, carry=carry, last=last, k=k):
            cols = lanes(t * LANES)
            tokens[...] = product[:, cols].astype(F32)
            own = at_tile(rates, first + t)
            table[0] = jnp.exp(-own[...])
            weights[...] = at_tile(weighing, first + t, 0, modes)[...]
            gain = row_of(at_tile(weighing, first + t, modes, 1), 0)
            begin = (lax.broadcasted_iota(jnp.int32, (SEGMENTS, LANES), 0) * steps).astype(F32)
            ahead = at_tile(before, first + t)
            state = []
            for m in range(modes):
                state.append(
                    carry[pl.ds(m * SEGMENTS, SEGMENTS), cols]
                    + jnp.exp(-row_of(own, m) * begin) * row_of(ahead, m)
                )
            if last:

                def write(i, value, now):
                    rest[step_rows(i), cols] = value + gain * now

                emit(table, weights, state, tokens, write)
            else:

                def write(i, value, now):
                    scr[step_rows(i), :] = value + gain * now

                emit(table, weights, state, tokens, write)
                mixed[:, cols] = (scr[...] - overs[k][:, cols].astype(F32)).astype(jnp.bfloat16)

        over_tiles(width, body)
        if not last:
            if copies[slot] is not None:
                copies[slot].wait()
            wide = math.gcd(width, 4 * LANES)
            for at in range(0, width, wide):
                cols = pl.ds(at, wide)
                done[slot, :, cols] = gated(back, mixed[:, cols], value[:, pl.ds(first * LANES + at, wide)])
            copies[slot] = pltpu.make_async_copy(
                done.at[slot, :, pl.ds(0, width)], out.at[:, pl.ds(first * LANES, width)], sems.at[slot]
            )
            copies[slot].start()
        first += width // LANES
    for copy in copies:
        if copy is not None:
            copy.wait()


def last_kernel(rest, over, value, partial, out, back, done, sem):
    del partial
    _, width = rest.shape
    first = value.shape[1] - width
    fill_order(back, True)
    wide = math.gcd(width, 4 * LANES)
    copies = []
    for k, at in enumerate(range(0, width, wide)):
        cols = pl.ds(at, wide)
        mixed = (rest[:, cols] - over[:, cols].astype(F32)).astype(jnp.bfloat16)
        done[:, cols] = gated(back, mixed, value[:, pl.ds(first + at, wide)])
        copies.append(
            pltpu.make_async_copy(done.at[:, cols], out.at[:, pl.ds(first + at, wide)], sem.at[k])
        )
        copies[-1].start()
    for copy in copies:
        copy.wait()


def shard_program(query, key_in, value, residues, decay_rates, skip_gain):
    length, channels = query.shape
    group, modes = residues.shape
    n_ch, n_ctx = lax.axis_size("ch"), lax.axis_size("ctx")
    span = FILTER_PARTS * length * n_ch
    bf16 = jnp.bfloat16

    shares = RAW_SHARES + DONE_SHARES
    unit = channels // sum(shares)
    widths = [unit * share for share in shares]
    firsts = [sum(widths[:k]) for k in range(len(widths))]
    count, n_raw = len(widths), len(RAW_SHARES)

    vmem = pl.BlockSpec(memory_space=pltpu.VMEM)
    anywhere = pl.BlockSpec(memory_space=pl.ANY)

    def shape(rows, columns, dtype=F32):
        return jax.ShapeDtypeStruct((rows, columns), dtype)

    def stack(rows):
        return jax.ShapeDtypeStruct((n_ch, rows, group), F32)

    tokens_scr = pltpu.VMEM((length, LANES), F32)
    table_scr = pltpu.VMEM((4, modes, LANES), F32)
    weights_scr = pltpu.VMEM((modes, LANES), F32)
    order_scr = pltpu.VMEM((length, length), bf16)

    def call(kernel, out_shape, scratch, args, **options):
        specs = dict(in_specs=[vmem] * len(args), out_specs=jax.tree.map(lambda _: vmem, out_shape))
        specs.update(options)
        return pl.pallas_call(
            kernel,
            out_shape=out_shape,
            scratch_shapes=scratch,
            compiler_params=pltpu.CompilerParams(vmem_limit_bytes=VMEM_BYTES),
            **specs,
        )(*args)

    own_rate = decay_rates.T
    rate_parts = ring([own_rate] * n_ch, "ch")

    products, pasts = [], []
    batches = [[k] for k in range(n_raw)] + [list(range(n_raw, count))]
    for k, batch in enumerate(batches):
        products += call(
            functools.partial(product_kernel, first=firsts[batch[0]]),
            [shape(length, widths[j], bf16) for j in batch],
            [order_scr],
            (query, key_in),
        )
        if k < n_raw:
            pasts.append(from_behind(products[k], "ctx", FILTER_PARTS))

    rows = -(-(modes + 1) // SEGMENTS) * SEGMENTS
    own_weight = jnp.concatenate(
        [residues.T, skip_gain[None], jnp.zeros((rows - modes - 1, group), F32)]
    )
    weight_parts = ring([own_weight] * n_ch, "ch")

    outs = call(
        functools.partial(states_kernel, count=count, n_ch=n_ch),
        [shape(modes * SEGMENTS, width) for width in widths] + [shape(modes, group)] * n_ch + [stack(modes)],
        [tokens_scr, table_scr, pltpu.VMEM((n_ch, modes, group), F32)],
        (*products, *rate_parts),
    )
    carries, sums, rates = outs[:count], outs[count:-1], outs[-1]
    sums = ring(sums, "ch")
    weighing = call(assemble_kernel, stack(rows), [], weight_parts)

    overs = []

    def add_over(k):
        overs.append(
            call(
                functools.partial(over_kernel, span=span, first=firsts[k] // LANES),
                shape(length, widths[k]),
                [tokens_scr, table_scr, weights_scr],
                (pasts[k], rates, weighing),
            )
        )

    def ahead_of(k):
        return call(
            functools.partial(ahead_kernel, span=span, first=firsts[k] // LANES, n_ctx=n_ctx),
            shape(length, widths[k], bf16),
            [tokens_scr, table_scr, weights_scr, tokens_scr],
            (products[k], rates, weighing, carries[k]),
        )

    aheads = [ahead_of(k) for k in range(n_raw, count)]
    for k in range(n_raw):
        add_over(k)

    blocks, tails, whole = call(
        functools.partial(tails_kernel, length=length),
        [stack(modes), stack(modes), shape(modes, group)],
        [],
        (*sums, own_rate),
    )
    oldest = from_behind(tails, "ctx", FILTER_PARTS)
    wholes = []
    for j in range(1, FILTER_PARTS):
        wholes.append(from_behind(whole, "ctx", j))
    for ahead in aheads:
        overs.append(from_behind(ahead, "ctx", FILTER_PARTS))
    heads = call(
        functools.partial(heads_kernel, length=length, parts=FILTER_PARTS),
        [shape(modes, group)] * n_ch,
        [pltpu.VMEM((n_ch, modes, group), F32)],
        (blocks, own_rate, oldest, *wholes),
    )
    befores = ring(heads, "ch")

    widest = max(widths)
    partial, rest = call(
        functools.partial(finish_kernel, count=count, n_ch=n_ch),
        [shape(length, channels, bf16), shape(length, widths[-1])],
        [
            tokens_scr,
            table_scr,
            weights_scr,
            tokens_scr,
            order_scr,
            pltpu.VMEM((n_ch, modes, group), F32),
            pltpu.VMEM((length, widest), bf16),
            pltpu.VMEM((2, length, widest), bf16),
            pltpu.SemaphoreType.DMA((2,)),
        ],
        (*products, *carries, *overs[:-1], *befores, rates, weighing, value),
        out_specs=[anywhere, vmem],
    )
    return call(
        last_kernel,
        shape(length, channels, bf16),
        [order_scr, pltpu.VMEM((length, widths[-1]), bf16), pltpu.SemaphoreType.DMA((8,))],
        (rest, overs[-1], value, partial),
        in_specs=[vmem, vmem, vmem, anywhere],
        out_specs=anywhere,
        input_output_aliases={3: 0},
    )


def solution(mesh):
    return jax.shard_map(
        shard_program,
        mesh=mesh,
        in_specs=(
            P(("ctx", "ch"), None),
            P(("ctx", "ch"), None),
            P(("ctx", "ch"), None),
            P("ch", None),
            P("ch", None),
            P("ch"),
        ),
        out_specs=P(("ctx", "ch"), None),
        check_vma=False,
    )
```

```python
import functools
import math

import jax
import jax.numpy as jnp
from jax import lax
from jax.experimental import pallas as pl
from jax.experimental.pallas import tpu as pltpu
from jax.sharding import PartitionSpec as P


FILTER_PARTS = 4
LANES = 128
SEGMENTS = 8
RAW_SHARES = (5, 5)
DONE_SHARES = (6,)
VMEM_BYTES = 16 << 20
F32 = jnp.float32


def from_behind(value, axis, steps):
    count = lax.axis_size(axis)
    return lax.ppermute(value, axis, [(source, source + steps) for source in range(count - steps)])


def ring(parts, axis):
    count = lax.axis_size(axis)
    moved = []
    for k, part in enumerate(parts):
        pairs = [(source, (source + k) % count) for source in range(count)]
        moved.append(lax.ppermute(part, axis, pairs) if k else part)
    return moved


def from_ring(refs, out):
    count = len(refs)
    mine = lax.axis_index("ch")
    for k, ref in enumerate(refs):
        out[(mine - k + count) % count] = ref[...]


def to_ring(whole, refs):
    count = len(refs)
    mine = lax.axis_index("ch")
    for k, ref in enumerate(refs):
        ref[...] = whole[(mine + k) % count]


def row_of(table, m):
    return jnp.broadcast_to(table[pl.ds(m, 1), :], (SEGMENTS, LANES))


def shifted(value, steps):
    row = lax.broadcasted_iota(jnp.int32, value.shape, 0)
    return jnp.where(row >= steps, pltpu.roll(value, steps, 0), 0.0)


def step_rows(i):
    return pl.ds(i * SEGMENTS, SEGMENTS)


def lanes(start):
    return pl.ds(pl.multiple_of(start, LANES), LANES)


def over_tiles(width, body):
    def step(t, carry):
        body(t)
        return carry

    lax.fori_loop(0, width // LANES, step, 0)


def at_tile(table, tile, first=0, count=None):
    per = table.shape[2] // LANES
    count = table.shape[1] if count is None else count
    return table.at[tile // per, pl.ds(first, count), lanes(tile % per * LANES)]


def scan_segments(table, tokens):
    modes = table.shape[1]
    steps = tokens.shape[0] // SEGMENTS
    decay = [row_of(table.at[0], m) for m in range(modes)]
    state = [tokens[step_rows(0), :]] * modes
    for i in range(1, steps):
        now = tokens[step_rows(i), :]
        state = [d * s + now for d, s in zip(decay, state)]
    chained = []
    for m in range(modes):
        value = state[m]
        for level in range(3):
            value = value + row_of(table.at[1 + level], m) * shifted(value, 1 << level)
        chained.append(value)
    return chained


def fill_jumps(table, rate, steps):
    table[0] = jnp.exp(-rate)
    for level in range(3):
        table[1 + level] = jnp.exp(-rate * float(steps << level))


def emit(table, weights, state, tokens, write):
    modes = table.shape[1]
    steps = tokens.shape[0] // SEGMENTS
    decay = [row_of(table.at[0], m) for m in range(modes)]
    weight = [row_of(weights, m) for m in range(modes)]
    for i in range(steps):
        now = tokens[step_rows(i), :]
        state = [d * s + now for d, s in zip(decay, state)]
        terms = [w * s for w, s in zip(weight, state)]
        while len(terms) > 1:
            terms = [a + b for a, b in zip(terms[::2], terms[1::2])]
        write(i, terms[0], now)


def fill_order(order, back=False):
    length = order.shape[0]
    row = lax.broadcasted_iota(jnp.int32, order.shape, 0)
    col = lax.broadcasted_iota(jnp.int32, order.shape, 1)
    inner = length // SEGMENTS if back else SEGMENTS
    order[...] = jnp.where(row % inner * (length // inner) + row // inner == col, 1.0, 0.0).astype(order.dtype)


def product_kernel(query, key_in, *refs, first):
    outs, order = refs[:-1], refs[-1]
    fill_order(order)
    start = first
    for out in outs:
        width = out.shape[1]
        wide = math.gcd(width, 4 * LANES)
        for at in range(0, width, wide):
            cols = pl.ds(start + at, wide)
            product = (query[:, cols].astype(F32) * key_in[:, cols].astype(F32)).astype(jnp.bfloat16)
            out[:, pl.ds(at, wide)] = jnp.dot(
                order[...], product, preferred_element_type=F32
            ).astype(jnp.bfloat16)
        start += width


def first_product_kernel(query, key_in, out, order, left, right, sems):
    width = out.shape[1]
    wide = width // sems.shape[0]
    copies = []
    for k in range(sems.shape[0]):
        cols = pl.ds(k * wide, wide)
        for j, (source, into) in enumerate(((query, left), (key_in, right))):
            copies.append(pltpu.make_async_copy(source.at[:, cols], into.at[:, cols], sems.at[k, j]))
            copies[-1].start()
    fill_order(order)
    for k in range(sems.shape[0]):
        cols = pl.ds(k * wide, wide)
        copies[2 * k].wait()
        copies[2 * k + 1].wait()
        product = (left[:, cols].astype(F32) * right[:, cols].astype(F32)).astype(jnp.bfloat16)
        out[:, cols] = jnp.dot(order[...], product, preferred_element_type=F32).astype(jnp.bfloat16)


def states_kernel(*refs, count, n_ch):
    products, parts = refs[:count], refs[count : count + n_ch]
    carries, sums = refs[count + n_ch : 2 * count + n_ch], refs[2 * count + n_ch : 2 * count + 2 * n_ch]
    rates, tokens, table, totals = refs[2 * count + 2 * n_ch :]
    from_ring(parts, rates)
    modes = rates.shape[1]
    first = 0
    for product, carry_out in zip(products, carries):
        steps = product.shape[0] // SEGMENTS

        def body(t, first=first, product=product, carry_out=carry_out):
            cols = lanes(t * LANES)
            tokens[...] = product[:, cols].astype(F32)
            fill_jumps(table, at_tile(rates, first + t)[...], steps)
            state = scan_segments(table, tokens)
            into = at_tile(totals, first + t)
            for m in range(modes):
                carry_out[pl.ds(m * SEGMENTS, SEGMENTS), cols] = shifted(state[m], 1)
                into[pl.ds(m, 1), :] = state[m][SEGMENTS - 1 :, :]

        over_tiles(product.shape[1], body)
        first += product.shape[1] // LANES
    to_ring(totals, sums)


def assemble_kernel(*refs):
    from_ring(refs[:-1], refs[-1])


def tails_kernel(*refs, length):
    *parts, rate, blocks, tails, whole = refs
    from_ring(parts, blocks)
    count = len(parts)
    running = None
    for q in reversed(range(count)):
        now = blocks[q]
        if running is not None:
            now = running + jnp.exp(-rate[...] * float(length * (count - 1 - q))) * now
        running = now
        tails[q] = running
    whole[...] = running


def heads_kernel(*refs, length, parts):
    blocks, rate, oldest, *rest = refs
    wholes, outs, heads = rest[: parts - 1], rest[parts - 1 : -1], rest[-1]
    count = blocks.shape[0]
    rates = rate[...]
    older = wholes[0][...]
    for j in range(1, parts - 1):
        older = older + jnp.exp(-rates * float(length * count * j)) * wholes[j][...]
    last = jnp.exp(-rates * float(length * count * (parts - 1)))
    jump = jnp.exp(-rates * float(length))
    running = None
    for q in range(count):
        earlier = older + last * oldest[q]
        if running is None:
            heads[q] = earlier
            running = blocks[q]
        else:
            heads[q] = running + jnp.exp(-rates * float(length * q)) * earlier
            running = jump * running + blocks[q]
    to_ring(heads, outs)


def over_kernel(past, rates, weighing, out, tokens, table, weights, *, span, first):
    steps = past.shape[0] // SEGMENTS
    modes = rates.shape[1]
    needed = lax.axis_index("ctx") >= FILTER_PARTS

    @pl.when(needed)
    def _():
        def body(t):
            cols = lanes(t * LANES)
            tokens[...] = past[:, cols].astype(F32)
            rate = at_tile(rates, first + t)[...]
            fill_jumps(table, rate, steps)
            weights[...] = at_tile(weighing, first + t, 0, modes)[...] * jnp.exp(-rate * float(span))
            state = [shifted(s, 1) for s in scan_segments(table, tokens)]

            def write(i, value, now):
                out[step_rows(i), cols] = value

            emit(table, weights, state, tokens, write)

        over_tiles(past.shape[1], body)

    @pl.when(jnp.logical_not(needed))
    def _():
        out[...] = jnp.zeros_like(out)


def ahead_kernel(product, rates, weighing, carry, out, tokens, table, weights, scr, *, span, first, n_ctx):
    modes = rates.shape[1]

    @pl.when(lax.axis_index("ctx") + FILTER_PARTS < n_ctx)
    def _():
        def body(t):
            cols = lanes(t * LANES)
            tokens[...] = product[:, cols].astype(F32)
            rate = at_tile(rates, first + t)[...]
            table[0] = jnp.exp(-rate)
            weights[...] = at_tile(weighing, first + t, 0, modes)[...] * jnp.exp(-rate * float(span))
            state = [carry[pl.ds(m * SEGMENTS, SEGMENTS), cols] for m in range(modes)]

            def write(i, value, now):
                scr[step_rows(i), :] = value

            emit(table, weights, state, tokens, write)
            out[:, cols] = scr[...].astype(jnp.bfloat16)

        over_tiles(product.shape[1], body)


def gated(back, mixed, value):
    plain = jnp.dot(back[...], mixed, preferred_element_type=F32)
    return (value.astype(F32) * plain).astype(jnp.bfloat16)


def finish_kernel(*refs, count, n_ch):
    products, carries, overs = refs[:count], refs[count : 2 * count], refs[2 * count : 3 * count - 1]
    refs = refs[3 * count - 1 :]
    befores, (rates, weighing, value, out, rest) = refs[:n_ch], refs[n_ch : n_ch + 5]
    tokens, table, weights, scr, back, before, mixed, done, sems = refs[n_ch + 5 :]
    modes = rates.shape[1]
    length = value.shape[0]
    steps = length // SEGMENTS
    from_ring(befores, before)
    fill_order(back, True)
    copies = [None, None]
    first = 0
    for k in range(count):
        product, carry = products[k], carries[k]
        width = product.shape[1]
        slot = k % 2
        last = k == count - 1

        def body(t, first=first, product=product, carry=carry, last=last, k=k):
            cols = lanes(t * LANES)
            tokens[...] = product[:, cols].astype(F32)
            own = at_tile(rates, first + t)
            table[0] = jnp.exp(-own[...])
            weights[...] = at_tile(weighing, first + t, 0, modes)[...]
            gain = row_of(at_tile(weighing, first + t, modes, 1), 0)
            begin = (lax.broadcasted_iota(jnp.int32, (SEGMENTS, LANES), 0) * steps).astype(F32)
            ahead = at_tile(before, first + t)
            state = []
            for m in range(modes):
                state.append(
                    carry[pl.ds(m * SEGMENTS, SEGMENTS), cols]
                    + jnp.exp(-row_of(own, m) * begin) * row_of(ahead, m)
                )
            if last:

                def write(i, value, now):
                    rest[step_rows(i), cols] = value + gain * now

                emit(table, weights, state, tokens, write)
            else:

                def write(i, value, now):
                    scr[step_rows(i), :] = value + gain * now

                emit(table, weights, state, tokens, write)
                mixed[:, cols] = (scr[...] - overs[k][:, cols].astype(F32)).astype(jnp.bfloat16)

        over_tiles(width, body)
        if not last:
            if copies[slot] is not None:
                copies[slot].wait()
            wide = math.gcd(width, 4 * LANES)
            for at in range(0, width, wide):
                cols = pl.ds(at, wide)
                done[slot, :, cols] = gated(back, mixed[:, cols], value[:, pl.ds(first * LANES + at, wide)])
            copies[slot] = pltpu.make_async_copy(
                done.at[slot, :, pl.ds(0, width)], out.at[:, pl.ds(first * LANES, width)], sems.at[slot]
            )
            copies[slot].start()
        first += width // LANES
    for copy in copies:
        if copy is not None:
            copy.wait()


def last_kernel(rest, over, value, partial, out, back, done, sem):
    del partial
    _, width = rest.shape
    first = value.shape[1] - width
    fill_order(back, True)
    wide = math.gcd(width, 4 * LANES)
    copies = []
    for k, at in enumerate(range(0, width, wide)):
        cols = pl.ds(at, wide)
        mixed = (rest[:, cols] - over[:, cols].astype(F32)).astype(jnp.bfloat16)
        done[:, cols] = gated(back, mixed, value[:, pl.ds(first + at, wide)])
        copies.append(
            pltpu.make_async_copy(done.at[:, cols], out.at[:, pl.ds(first + at, wide)], sem.at[k])
        )
        copies[-1].start()
    for copy in copies:
        copy.wait()


def shard_program(query, key_in, value, residues, decay_rates, skip_gain):
    length, channels = query.shape
    group, modes = residues.shape
    n_ch, n_ctx = lax.axis_size("ch"), lax.axis_size("ctx")
    span = FILTER_PARTS * length * n_ch
    bf16 = jnp.bfloat16

    shares = RAW_SHARES + DONE_SHARES
    unit = channels // sum(shares)
    widths = [unit * share for share in shares]
    firsts = [sum(widths[:k]) for k in range(len(widths))]
    count, n_raw = len(widths), len(RAW_SHARES)

    vmem = pl.BlockSpec(memory_space=pltpu.VMEM)
    anywhere = pl.BlockSpec(memory_space=pl.ANY)
    hbm = pl.BlockSpec(memory_space=pltpu.HBM)

    def shape(rows, columns, dtype=F32):
        return jax.ShapeDtypeStruct((rows, columns), dtype)

    def stack(rows):
        return jax.ShapeDtypeStruct((n_ch, rows, group), F32)

    tokens_scr = pltpu.VMEM((length, LANES), F32)
    table_scr = pltpu.VMEM((4, modes, LANES), F32)
    weights_scr = pltpu.VMEM((modes, LANES), F32)
    order_scr = pltpu.VMEM((length, length), bf16)

    def call(kernel, out_shape, scratch, args, **options):
        specs = dict(in_specs=[vmem] * len(args), out_specs=jax.tree.map(lambda _: vmem, out_shape))
        specs.update(options)
        return pl.pallas_call(
            kernel,
            out_shape=out_shape,
            scratch_shapes=scratch,
            compiler_params=pltpu.CompilerParams(vmem_limit_bytes=VMEM_BYTES),
            **specs,
        )(*args)

    own_rate = decay_rates.T
    rate_parts = ring([own_rate] * n_ch, "ch")

    products, pasts = [], []
    batches = [[k] for k in range(n_raw)] + [list(range(n_raw, count))]
    for k, batch in enumerate(batches):
        if k == 0:
            read = pltpu.VMEM((length, widths[0]), bf16)
            product = call(
                first_product_kernel,
                shape(length, widths[0], bf16),
                [order_scr, read, read, pltpu.SemaphoreType.DMA((2, 2))],
                tuple(pltpu.with_memory_space_constraint(x, pltpu.HBM) for x in (query, key_in)),
                in_specs=[hbm, hbm],
            )
            products.append(product)
        else:
            products += call(
                functools.partial(product_kernel, first=firsts[batch[0]]),
                [shape(length, widths[j], bf16) for j in batch],
                [order_scr],
                (query, key_in),
            )
        if k < n_raw:
            pasts.append(from_behind(products[k], "ctx", FILTER_PARTS))

    rows = -(-(modes + 1) // SEGMENTS) * SEGMENTS
    own_weight = jnp.concatenate(
        [residues.T, skip_gain[None], jnp.zeros((rows - modes - 1, group), F32)]
    )
    weight_parts = ring([own_weight] * n_ch, "ch")

    outs = call(
        functools.partial(states_kernel, count=count, n_ch=n_ch),
        [shape(modes * SEGMENTS, width) for width in widths] + [shape(modes, group)] * n_ch + [stack(modes)],
        [tokens_scr, table_scr, pltpu.VMEM((n_ch, modes, group), F32)],
        (*products, *rate_parts),
    )
    carries, sums, rates = outs[:count], outs[count:-1], outs[-1]
    sums = ring(sums, "ch")
    weighing = call(assemble_kernel, stack(rows), [], weight_parts)

    overs = []

    def add_over(k):
        overs.append(
            call(
                functools.partial(over_kernel, span=span, first=firsts[k] // LANES),
                shape(length, widths[k]),
                [tokens_scr, table_scr, weights_scr],
                (pasts[k], rates, weighing),
            )
        )

    def ahead_of(k):
        return call(
            functools.partial(ahead_kernel, span=span, first=firsts[k] // LANES, n_ctx=n_ctx),
            shape(length, widths[k], bf16),
            [tokens_scr, table_scr, weights_scr, tokens_scr],
            (products[k], rates, weighing, carries[k]),
        )

    aheads = [ahead_of(k) for k in range(n_raw, count)]
    for k in range(n_raw):
        add_over(k)

    blocks, tails, whole = call(
        functools.partial(tails_kernel, length=length),
        [stack(modes), stack(modes), shape(modes, group)],
        [],
        (*sums, own_rate),
    )
    oldest = from_behind(tails, "ctx", FILTER_PARTS)
    wholes = []
    for j in range(1, FILTER_PARTS):
        wholes.append(from_behind(whole, "ctx", j))
    for ahead in aheads:
        overs.append(from_behind(ahead, "ctx", FILTER_PARTS))
    heads = call(
        functools.partial(heads_kernel, length=length, parts=FILTER_PARTS),
        [shape(modes, group)] * n_ch,
        [pltpu.VMEM((n_ch, modes, group), F32)],
        (blocks, own_rate, oldest, *wholes),
    )
    befores = ring(heads, "ch")

    widest = max(widths[:-1])
    partial, rest = call(
        functools.partial(finish_kernel, count=count, n_ch=n_ch),
        [shape(length, channels, bf16), shape(length, widths[-1])],
        [
            tokens_scr,
            table_scr,
            weights_scr,
            tokens_scr,
            order_scr,
            pltpu.VMEM((n_ch, modes, group), F32),
            pltpu.VMEM((length, widest), bf16),
            pltpu.VMEM((2, length, widest), bf16),
            pltpu.SemaphoreType.DMA((2,)),
        ],
        (*products, *carries, *overs[:-1], *befores, rates, weighing, value),
        out_specs=[anywhere, vmem],
    )
    return call(
        last_kernel,
        shape(length, channels, bf16),
        [order_scr, pltpu.VMEM((length, widths[-1]), bf16), pltpu.SemaphoreType.DMA((8,))],
        (rest, overs[-1], value, partial),
        in_specs=[vmem, vmem, vmem, anywhere],
        out_specs=anywhere,
        input_output_aliases={3: 0},
    )


def solution(mesh):
    return jax.shard_map(
        shard_program,
        mesh=mesh,
        in_specs=(
            P(("ctx", "ch"), None),
            P(("ctx", "ch"), None),
            P(("ctx", "ch"), None),
            P("ch", None),
            P("ch", None),
            P("ch"),
        ),
        out_specs=P(("ctx", "ch"), None),
        check_vma=False,
    )
```

```python
import functools
import math

import jax
import jax.numpy as jnp
from jax import lax
from jax.experimental import pallas as pl
from jax.experimental.pallas import tpu as pltpu
from jax.sharding import PartitionSpec as P


FILTER_PARTS = 4
LANES = 128
SEGMENTS = 8
RAW_SHARES = (5, 5)
DONE_SHARES = (6,)
VMEM_BYTES = 16 << 20
F32 = jnp.float32


def from_behind(value, axis, steps):
    count = lax.axis_size(axis)
    return lax.ppermute(value, axis, [(source, source + steps) for source in range(count - steps)])


def partner(mine, k, count, sign):
    if count & (count - 1) == 0:
        return mine ^ k
    return (mine + sign * k + count) % count


def ring(parts, axis):
    count = lax.axis_size(axis)
    moved = []
    for k, part in enumerate(parts):
        pairs = [(source, partner(source, k, count, 1)) for source in range(count)]
        moved.append(lax.ppermute(part, axis, pairs) if k else part)
    return moved


def from_ring(refs, out):
    count = len(refs)
    mine = lax.axis_index("ch")
    for k, ref in enumerate(refs):
        out[partner(mine, k, count, -1)] = ref[...]


def to_ring(whole, refs):
    count = len(refs)
    mine = lax.axis_index("ch")
    for k, ref in enumerate(refs):
        ref[...] = whole[partner(mine, k, count, 1)]


def row_of(table, m):
    return jnp.broadcast_to(table[pl.ds(m, 1), :], (SEGMENTS, LANES))


def shifted(value, steps):
    row = lax.broadcasted_iota(jnp.int32, value.shape, 0)
    return jnp.where(row >= steps, pltpu.roll(value, steps, 0), 0.0)


def step_rows(i):
    return pl.ds(i * SEGMENTS, SEGMENTS)


def lanes(start):
    return pl.ds(pl.multiple_of(start, LANES), LANES)


def over_tiles(width, body):
    def step(t, carry):
        body(t)
        return carry

    lax.fori_loop(0, width // LANES, step, 0)


def at_tile(table, tile, first=0, count=None):
    per = table.shape[2] // LANES
    count = table.shape[1] if count is None else count
    return table.at[tile // per, pl.ds(first, count), lanes(tile % per * LANES)]


def scan_segments(table, tokens):
    modes = table.shape[1]
    steps = tokens.shape[0] // SEGMENTS
    decay = [row_of(table.at[0], m) for m in range(modes)]
    state = [tokens[step_rows(0), :]] * modes
    for i in range(1, steps):
        now = tokens[step_rows(i), :]
        state = [d * s + now for d, s in zip(decay, state)]
    chained = []
    for m in range(modes):
        value = state[m]
        for level in range(3):
            value = value + row_of(table.at[1 + level], m) * shifted(value, 1 << level)
        chained.append(value)
    return chained


def fill_jumps(table, rate, steps):
    table[0] = jnp.exp(-rate)
    for level in range(3):
        table[1 + level] = jnp.exp(-rate * float(steps << level))


def emit(table, weights, state, tokens, write):
    modes = table.shape[1]
    steps = tokens.shape[0] // SEGMENTS
    decay = [row_of(table.at[0], m) for m in range(modes)]
    weight = [row_of(weights, m) for m in range(modes)]
    for i in range(steps):
        now = tokens[step_rows(i), :]
        state = [d * s + now for d, s in zip(decay, state)]
        terms = [w * s for w, s in zip(weight, state)]
        while len(terms) > 1:
            terms = [a + b for a, b in zip(terms[::2], terms[1::2])]
        write(i, terms[0], now)


def fill_order(order, back=False):
    length = order.shape[0]
    row = lax.broadcasted_iota(jnp.int32, order.shape, 0)
    col = lax.broadcasted_iota(jnp.int32, order.shape, 1)
    inner = length // SEGMENTS if back else SEGMENTS
    order[...] = jnp.where(row % inner * (length // inner) + row // inner == col, 1.0, 0.0).astype(order.dtype)


def product_kernel(query, key_in, *refs, first):
    outs, order = refs[:-1], refs[-1]
    fill_order(order)
    start = first
    for out in outs:
        width = out.shape[1]
        wide = math.gcd(width, 4 * LANES)
        for at in range(0, width, wide):
            cols = pl.ds(start + at, wide)
            product = (query[:, cols].astype(F32) * key_in[:, cols].astype(F32)).astype(jnp.bfloat16)
            out[:, pl.ds(at, wide)] = jnp.dot(
                order[...], product, preferred_element_type=F32
            ).astype(jnp.bfloat16)
        start += width


def first_product_kernel(query, key_in, out, order, left, right, sems):
    width = out.shape[1]
    wide = width // sems.shape[0]
    copies = []
    for k in range(sems.shape[0]):
        cols = pl.ds(k * wide, wide)
        for j, (source, into) in enumerate(((query, left), (key_in, right))):
            copies.append(pltpu.make_async_copy(source.at[:, cols], into.at[:, cols], sems.at[k, j]))
            copies[-1].start()
    fill_order(order)
    for k in range(sems.shape[0]):
        cols = pl.ds(k * wide, wide)
        copies[2 * k].wait()
        copies[2 * k + 1].wait()
        product = (left[:, cols].astype(F32) * right[:, cols].astype(F32)).astype(jnp.bfloat16)
        out[:, cols] = jnp.dot(order[...], product, preferred_element_type=F32).astype(jnp.bfloat16)


def states_kernel(*refs, count, n_ch):
    products, parts = refs[:count], refs[count : count + n_ch]
    carries, sums = refs[count + n_ch : 2 * count + n_ch], refs[2 * count + n_ch : 2 * count + 2 * n_ch]
    rates, tokens, table, totals = refs[2 * count + 2 * n_ch :]
    from_ring(parts, rates)
    modes = rates.shape[1]
    first = 0
    for product, carry_out in zip(products, carries):
        steps = product.shape[0] // SEGMENTS

        def body(t, first=first, product=product, carry_out=carry_out):
            cols = lanes(t * LANES)
            tokens[...] = product[:, cols].astype(F32)
            fill_jumps(table, at_tile(rates, first + t)[...], steps)
            state = scan_segments(table, tokens)
            into = at_tile(totals, first + t)
            for m in range(modes):
                carry_out[pl.ds(m * SEGMENTS, SEGMENTS), cols] = shifted(state[m], 1)
                into[pl.ds(m, 1), :] = state[m][SEGMENTS - 1 :, :]

        over_tiles(product.shape[1], body)
        first += product.shape[1] // LANES
    to_ring(totals, sums)


def assemble_kernel(*refs):
    from_ring(refs[:-1], refs[-1])


def tails_kernel(*refs, length):
    *parts, rate, blocks, tails, whole = refs
    from_ring(parts, blocks)
    count = len(parts)
    running = None
    for q in reversed(range(count)):
        now = blocks[q]
        if running is not None:
            now = running + jnp.exp(-rate[...] * float(length * (count - 1 - q))) * now
        running = now
        tails[q] = running
    whole[...] = running


def heads_kernel(*refs, length, parts):
    blocks, rate, oldest, *rest = refs
    wholes, outs, heads = rest[: parts - 1], rest[parts - 1 : -1], rest[-1]
    count = blocks.shape[0]
    rates = rate[...]
    older = wholes[0][...]
    for j in range(1, parts - 1):
        older = older + jnp.exp(-rates * float(length * count * j)) * wholes[j][...]
    last = jnp.exp(-rates * float(length * count * (parts - 1)))
    jump = jnp.exp(-rates * float(length))
    running = None
    for q in range(count):
        earlier = older + last * oldest[q]
        if running is None:
            heads[q] = earlier
            running = blocks[q]
        else:
            heads[q] = running + jnp.exp(-rates * float(length * q)) * earlier
            running = jump * running + blocks[q]
    to_ring(heads, outs)


def over_kernel(past, rates, weighing, out, tokens, table, weights, *, span, first):
    steps = past.shape[0] // SEGMENTS
    modes = rates.shape[1]
    needed = lax.axis_index("ctx") >= FILTER_PARTS

    @pl.when(needed)
    def _():
        def body(t):
            cols = lanes(t * LANES)
            tokens[...] = past[:, cols].astype(F32)
            rate = at_tile(rates, first + t)[...]
            fill_jumps(table, rate, steps)
            weights[...] = at_tile(weighing, first + t, 0, modes)[...] * jnp.exp(-rate * float(span))
            state = [shifted(s, 1) for s in scan_segments(table, tokens)]

            def write(i, value, now):
                out[step_rows(i), cols] = value

            emit(table, weights, state, tokens, write)

        over_tiles(past.shape[1], body)

    @pl.when(jnp.logical_not(needed))
    def _():
        out[...] = jnp.zeros_like(out)


def ahead_kernel(product, rates, weighing, carry, out, tokens, table, weights, scr, *, span, first, n_ctx):
    modes = rates.shape[1]

    @pl.when(lax.axis_index("ctx") + FILTER_PARTS < n_ctx)
    def _():
        def body(t):
            cols = lanes(t * LANES)
            tokens[...] = product[:, cols].astype(F32)
            rate = at_tile(rates, first + t)[...]
            table[0] = jnp.exp(-rate)
            weights[...] = at_tile(weighing, first + t, 0, modes)[...] * jnp.exp(-rate * float(span))
            state = [carry[pl.ds(m * SEGMENTS, SEGMENTS), cols] for m in range(modes)]

            def write(i, value, now):
                scr[step_rows(i), :] = value

            emit(table, weights, state, tokens, write)
            out[:, cols] = scr[...].astype(jnp.bfloat16)

        over_tiles(product.shape[1], body)


def gated(back, mixed, value):
    plain = jnp.dot(back[...], mixed, preferred_element_type=F32)
    return (value.astype(F32) * plain).astype(jnp.bfloat16)


def finish_kernel(*refs, count, n_ch):
    products, carries, overs = refs[:count], refs[count : 2 * count], refs[2 * count : 3 * count - 1]
    refs = refs[3 * count - 1 :]
    befores, (rates, weighing, value, out, rest) = refs[:n_ch], refs[n_ch : n_ch + 5]
    tokens, table, weights, scr, back, before, mixed, done, sems = refs[n_ch + 5 :]
    modes = rates.shape[1]
    length = value.shape[0]
    steps = length // SEGMENTS
    from_ring(befores, before)
    fill_order(back, True)
    copies = [None, None]
    first = 0
    for k in range(count):
        product, carry = products[k], carries[k]
        width = product.shape[1]
        slot = k % 2
        last = k == count - 1

        def body(t, first=first, product=product, carry=carry, last=last, k=k):
            cols = lanes(t * LANES)
            tokens[...] = product[:, cols].astype(F32)
            own = at_tile(rates, first + t)
            table[0] = jnp.exp(-own[...])
            weights[...] = at_tile(weighing, first + t, 0, modes)[...]
            gain = row_of(at_tile(weighing, first + t, modes, 1), 0)
            begin = (lax.broadcasted_iota(jnp.int32, (SEGMENTS, LANES), 0) * steps).astype(F32)
            ahead = at_tile(before, first + t)
            state = []
            for m in range(modes):
                state.append(
                    carry[pl.ds(m * SEGMENTS, SEGMENTS), cols]
                    + jnp.exp(-row_of(own, m) * begin) * row_of(ahead, m)
                )
            if last:

                def write(i, value, now):
                    rest[step_rows(i), cols] = value + gain * now

                emit(table, weights, state, tokens, write)
            else:

                def write(i, value, now):
                    scr[step_rows(i), :] = value + gain * now

                emit(table, weights, state, tokens, write)
                mixed[:, cols] = (scr[...] - overs[k][:, cols].astype(F32)).astype(jnp.bfloat16)

        over_tiles(width, body)
        if not last:
            if copies[slot] is not None:
                copies[slot].wait()
            wide = math.gcd(width, 4 * LANES)
            for at in range(0, width, wide):
                cols = pl.ds(at, wide)
                done[slot, :, cols] = gated(back, mixed[:, cols], value[:, pl.ds(first * LANES + at, wide)])
            copies[slot] = pltpu.make_async_copy(
                done.at[slot, :, pl.ds(0, width)], out.at[:, pl.ds(first * LANES, width)], sems.at[slot]
            )
            copies[slot].start()
        first += width // LANES
    for copy in copies:
        if copy is not None:
            copy.wait()


def last_kernel(rest, over, value, partial, out, back, done, sem):
    del partial
    _, width = rest.shape
    first = value.shape[1] - width
    fill_order(back, True)
    wide = math.gcd(width, 4 * LANES)
    copies = []
    for k, at in enumerate(range(0, width, wide)):
        cols = pl.ds(at, wide)
        mixed = (rest[:, cols] - over[:, cols].astype(F32)).astype(jnp.bfloat16)
        done[:, cols] = gated(back, mixed, value[:, pl.ds(first + at, wide)])
        copies.append(
            pltpu.make_async_copy(done.at[:, cols], out.at[:, pl.ds(first + at, wide)], sem.at[k])
        )
        copies[-1].start()
    for copy in copies:
        copy.wait()


def shard_program(query, key_in, value, residues, decay_rates, skip_gain):
    length, channels = query.shape
    group, modes = residues.shape
    n_ch, n_ctx = lax.axis_size("ch"), lax.axis_size("ctx")
    span = FILTER_PARTS * length * n_ch
    bf16 = jnp.bfloat16

    shares = RAW_SHARES + DONE_SHARES
    unit = channels // sum(shares)
    widths = [unit * share for share in shares]
    firsts = [sum(widths[:k]) for k in range(len(widths))]
    count, n_raw = len(widths), len(RAW_SHARES)

    vmem = pl.BlockSpec(memory_space=pltpu.VMEM)
    anywhere = pl.BlockSpec(memory_space=pl.ANY)
    hbm = pl.BlockSpec(memory_space=pltpu.HBM)

    def shape(rows, columns, dtype=F32):
        return jax.ShapeDtypeStruct((rows, columns), dtype)

    def stack(rows):
        return jax.ShapeDtypeStruct((n_ch, rows, group), F32)

    tokens_scr = pltpu.VMEM((length, LANES), F32)
    table_scr = pltpu.VMEM((4, modes, LANES), F32)
    weights_scr = pltpu.VMEM((modes, LANES), F32)
    order_scr = pltpu.VMEM((length, length), bf16)

    def call(kernel, out_shape, scratch, args, **options):
        specs = dict(in_specs=[vmem] * len(args), out_specs=jax.tree.map(lambda _: vmem, out_shape))
        specs.update(options)
        return pl.pallas_call(
            kernel,
            out_shape=out_shape,
            scratch_shapes=scratch,
            compiler_params=pltpu.CompilerParams(vmem_limit_bytes=VMEM_BYTES),
            **specs,
        )(*args)

    own_rate = decay_rates.T
    rate_parts = ring([own_rate] * n_ch, "ch")

    products, pasts = [], []
    batches = [[k] for k in range(n_raw)] + [list(range(n_raw, count))]
    for k, batch in enumerate(batches):
        if k == 0:
            read = pltpu.VMEM((length, widths[0]), bf16)
            product = call(
                first_product_kernel,
                shape(length, widths[0], bf16),
                [order_scr, read, read, pltpu.SemaphoreType.DMA((2, 2))],
                tuple(pltpu.with_memory_space_constraint(x, pltpu.HBM) for x in (query, key_in)),
                in_specs=[hbm, hbm],
            )
            products.append(product)
        else:
            products += call(
                functools.partial(product_kernel, first=firsts[batch[0]]),
                [shape(length, widths[j], bf16) for j in batch],
                [order_scr],
                (query, key_in),
            )
        if k < n_raw:
            pasts.append(from_behind(products[k], "ctx", FILTER_PARTS))

    rows = -(-(modes + 1) // SEGMENTS) * SEGMENTS
    own_weight = jnp.concatenate(
        [residues.T, skip_gain[None], jnp.zeros((rows - modes - 1, group), F32)]
    )
    weight_parts = ring([own_weight] * n_ch, "ch")

    outs = call(
        functools.partial(states_kernel, count=count, n_ch=n_ch),
        [shape(modes * SEGMENTS, width) for width in widths] + [shape(modes, group)] * n_ch + [stack(modes)],
        [tokens_scr, table_scr, pltpu.VMEM((n_ch, modes, group), F32)],
        (*products, *rate_parts),
    )
    carries, sums, rates = outs[:count], outs[count:-1], outs[-1]
    sums = ring(sums, "ch")
    weighing = call(assemble_kernel, stack(rows), [], weight_parts)

    overs = []

    def add_over(k):
        overs.append(
            call(
                functools.partial(over_kernel, span=span, first=firsts[k] // LANES),
                shape(length, widths[k]),
                [tokens_scr, table_scr, weights_scr],
                (pasts[k], rates, weighing),
            )
        )

    def ahead_of(k):
        return call(
            functools.partial(ahead_kernel, span=span, first=firsts[k] // LANES, n_ctx=n_ctx),
            shape(length, widths[k], bf16),
            [tokens_scr, table_scr, weights_scr, tokens_scr],
            (products[k], rates, weighing, carries[k]),
        )

    aheads = [ahead_of(k) for k in range(n_raw, count)]
    for k in range(n_raw):
        add_over(k)

    blocks, tails, whole = call(
        functools.partial(tails_kernel, length=length),
        [stack(modes), stack(modes), shape(modes, group)],
        [],
        (*sums, own_rate),
    )
    oldest = from_behind(tails, "ctx", FILTER_PARTS)
    wholes = []
    for j in range(1, FILTER_PARTS):
        wholes.append(from_behind(whole, "ctx", j))
    for ahead in aheads:
        overs.append(from_behind(ahead, "ctx", FILTER_PARTS))
    heads = call(
        functools.partial(heads_kernel, length=length, parts=FILTER_PARTS),
        [shape(modes, group)] * n_ch,
        [pltpu.VMEM((n_ch, modes, group), F32)],
        (blocks, own_rate, oldest, *wholes),
    )
    befores = ring(heads, "ch")

    widest = max(widths[:-1])
    partial, rest = call(
        functools.partial(finish_kernel, count=count, n_ch=n_ch),
        [shape(length, channels, bf16), shape(length, widths[-1])],
        [
            tokens_scr,
            table_scr,
            weights_scr,
            tokens_scr,
            order_scr,
            pltpu.VMEM((n_ch, modes, group), F32),
            pltpu.VMEM((length, widest), bf16),
            pltpu.VMEM((2, length, widest), bf16),
            pltpu.SemaphoreType.DMA((2,)),
        ],
        (*products, *carries, *overs[:-1], *befores, rates, weighing, value),
        out_specs=[anywhere, vmem],
    )
    return call(
        last_kernel,
        shape(length, channels, bf16),
        [order_scr, pltpu.VMEM((length, widths[-1]), bf16), pltpu.SemaphoreType.DMA((8,))],
        (rest, overs[-1], value, partial),
        in_specs=[vmem, vmem, vmem, anywhere],
        out_specs=anywhere,
        input_output_aliases={3: 0},
    )


def solution(mesh):
    return jax.shard_map(
        shard_program,
        mesh=mesh,
        in_specs=(
            P(("ctx", "ch"), None),
            P(("ctx", "ch"), None),
            P(("ctx", "ch"), None),
            P("ch", None),
            P("ch", None),
            P("ch"),
        ),
        out_specs=P(("ctx", "ch"), None),
        check_vma=False,
    )
```

```python
import functools
import math

import jax
import jax.numpy as jnp
from jax import lax
from jax.experimental import pallas as pl
from jax.experimental.pallas import tpu as pltpu
from jax.sharding import PartitionSpec as P


FILTER_PARTS = 4
LANES = 128
SEGMENTS = 8
RAW_SHARES = (4, 6)
DONE_SHARES = (6,)
VMEM_BYTES = 16 << 20
F32 = jnp.float32


def from_behind(value, axis, steps):
    count = lax.axis_size(axis)
    return lax.ppermute(value, axis, [(source, source + steps) for source in range(count - steps)])


def partner(mine, k, count, sign):
    if count & (count - 1) == 0:
        return mine ^ k
    return (mine + sign * k + count) % count


def ring(parts, axis):
    count = lax.axis_size(axis)
    moved = []
    for k, part in enumerate(parts):
        pairs = [(source, partner(source, k, count, 1)) for source in range(count)]
        moved.append(lax.ppermute(part, axis, pairs) if k else part)
    return moved


def from_ring(refs, out):
    count = len(refs)
    mine = lax.axis_index("ch")
    for k, ref in enumerate(refs):
        out[partner(mine, k, count, -1)] = ref[...]


def to_ring(whole, refs):
    count = len(refs)
    mine = lax.axis_index("ch")
    for k, ref in enumerate(refs):
        ref[...] = whole[partner(mine, k, count, 1)]


def row_of(table, m):
    return jnp.broadcast_to(table[pl.ds(m, 1), :], (SEGMENTS, LANES))


def shifted(value, steps):
    row = lax.broadcasted_iota(jnp.int32, value.shape, 0)
    return jnp.where(row >= steps, pltpu.roll(value, steps, 0), 0.0)


def step_rows(i):
    return pl.ds(i * SEGMENTS, SEGMENTS)


def lanes(start):
    return pl.ds(pl.multiple_of(start, LANES), LANES)


def over_tiles(width, body):
    def step(t, carry):
        body(t)
        return carry

    lax.fori_loop(0, width // LANES, step, 0)


def at_tile(table, tile, first=0, count=None):
    per = table.shape[2] // LANES
    count = table.shape[1] if count is None else count
    return table.at[tile // per, pl.ds(first, count), lanes(tile % per * LANES)]


def scan_segments(table, tokens):
    modes = table.shape[1]
    steps = tokens.shape[0] // SEGMENTS
    decay = [row_of(table.at[0], m) for m in range(modes)]
    state = [tokens[step_rows(0), :]] * modes
    for i in range(1, steps):
        now = tokens[step_rows(i), :]
        state = [d * s + now for d, s in zip(decay, state)]
    chained = []
    for m in range(modes):
        value = state[m]
        for level in range(3):
            value = value + row_of(table.at[1 + level], m) * shifted(value, 1 << level)
        chained.append(value)
    return chained


def fill_jumps(table, rate, steps):
    table[0] = jnp.exp(-rate)
    for level in range(3):
        table[1 + level] = jnp.exp(-rate * float(steps << level))


def emit(table, weights, state, tokens, write):
    modes = table.shape[1]
    steps = tokens.shape[0] // SEGMENTS
    decay = [row_of(table.at[0], m) for m in range(modes)]
    weight = [row_of(weights, m) for m in range(modes)]
    for i in range(steps):
        now = tokens[step_rows(i), :]
        state = [d * s + now for d, s in zip(decay, state)]
        terms = [w * s for w, s in zip(weight, state)]
        while len(terms) > 1:
            terms = [a + b for a, b in zip(terms[::2], terms[1::2])]
        write(i, terms[0], now)


def fill_order(order, back=False):
    length = order.shape[0]
    row = lax.broadcasted_iota(jnp.int32, order.shape, 0)
    col = lax.broadcasted_iota(jnp.int32, order.shape, 1)
    inner = length // SEGMENTS if back else SEGMENTS
    order[...] = jnp.where(row % inner * (length // inner) + row // inner == col, 1.0, 0.0).astype(order.dtype)


def product_kernel(query, key_in, *refs, first):
    outs, order = refs[:-1], refs[-1]
    fill_order(order)
    start = first
    for out in outs:
        width = out.shape[1]
        wide = math.gcd(width, 4 * LANES)
        for at in range(0, width, wide):
            cols = pl.ds(start + at, wide)
            product = (query[:, cols].astype(F32) * key_in[:, cols].astype(F32)).astype(jnp.bfloat16)
            out[:, pl.ds(at, wide)] = jnp.dot(
                order[...], product, preferred_element_type=F32
            ).astype(jnp.bfloat16)
        start += width


def first_product_kernel(query, key_in, out, order, left, right, sems):
    width = out.shape[1]
    wide = width // sems.shape[0]
    copies = []
    for k in range(sems.shape[0]):
        cols = pl.ds(k * wide, wide)
        for j, (source, into) in enumerate(((query, left), (key_in, right))):
            copies.append(pltpu.make_async_copy(source.at[:, cols], into.at[:, cols], sems.at[k, j]))
            copies[-1].start()
    fill_order(order)
    for k in range(sems.shape[0]):
        cols = pl.ds(k * wide, wide)
        copies[2 * k].wait()
        copies[2 * k + 1].wait()
        product = (left[:, cols].astype(F32) * right[:, cols].astype(F32)).astype(jnp.bfloat16)
        out[:, cols] = jnp.dot(order[...], product, preferred_element_type=F32).astype(jnp.bfloat16)


def states_kernel(*refs, count, n_ch):
    products, parts = refs[:count], refs[count : count + n_ch]
    carries, sums = refs[count + n_ch : 2 * count + n_ch], refs[2 * count + n_ch : 2 * count + 2 * n_ch]
    rates, tokens, table, totals = refs[2 * count + 2 * n_ch :]
    from_ring(parts, rates)
    modes = rates.shape[1]
    first = 0
    for product, carry_out in zip(products, carries):
        steps = product.shape[0] // SEGMENTS

        def body(t, first=first, product=product, carry_out=carry_out):
            cols = lanes(t * LANES)
            tokens[...] = product[:, cols].astype(F32)
            fill_jumps(table, at_tile(rates, first + t)[...], steps)
            state = scan_segments(table, tokens)
            into = at_tile(totals, first + t)
            for m in range(modes):
                carry_out[pl.ds(m * SEGMENTS, SEGMENTS), cols] = shifted(state[m], 1)
                into[pl.ds(m, 1), :] = state[m][SEGMENTS - 1 :, :]

        over_tiles(product.shape[1], body)
        first += product.shape[1] // LANES
    to_ring(totals, sums)


def assemble_kernel(*refs):
    from_ring(refs[:-1], refs[-1])


def tails_kernel(*refs, length):
    *parts, rate, blocks, tails, whole = refs
    from_ring(parts, blocks)
    count = len(parts)
    running = None
    for q in reversed(range(count)):
        now = blocks[q]
        if running is not None:
            now = running + jnp.exp(-rate[...] * float(length * (count - 1 - q))) * now
        running = now
        tails[q] = running
    whole[...] = running


def heads_kernel(*refs, length, parts):
    blocks, rate, oldest, *rest = refs
    wholes, outs, heads = rest[: parts - 1], rest[parts - 1 : -1], rest[-1]
    count = blocks.shape[0]
    rates = rate[...]
    older = wholes[0][...]
    for j in range(1, parts - 1):
        older = older + jnp.exp(-rates * float(length * count * j)) * wholes[j][...]
    last = jnp.exp(-rates * float(length * count * (parts - 1)))
    jump = jnp.exp(-rates * float(length))
    running = None
    for q in range(count):
        earlier = older + last * oldest[q]
        if running is None:
            heads[q] = earlier
            running = blocks[q]
        else:
            heads[q] = running + jnp.exp(-rates * float(length * q)) * earlier
            running = jump * running + blocks[q]
    to_ring(heads, outs)


def over_kernel(past, rates, weighing, out, tokens, table, weights, *, span, first):
    steps = past.shape[0] // SEGMENTS
    modes = rates.shape[1]
    needed = lax.axis_index("ctx") >= FILTER_PARTS

    @pl.when(needed)
    def _():
        def body(t):
            cols = lanes(t * LANES)
            tokens[...] = past[:, cols].astype(F32)
            rate = at_tile(rates, first + t)[...]
            fill_jumps(table, rate, steps)
            weights[...] = at_tile(weighing, first + t, 0, modes)[...] * jnp.exp(-rate * float(span))
            state = [shifted(s, 1) for s in scan_segments(table, tokens)]

            def write(i, value, now):
                out[step_rows(i), cols] = value

            emit(table, weights, state, tokens, write)

        over_tiles(past.shape[1], body)

    @pl.when(jnp.logical_not(needed))
    def _():
        out[...] = jnp.zeros_like(out)


def ahead_kernel(product, rates, weighing, carry, out, tokens, table, weights, scr, *, span, first, n_ctx):
    modes = rates.shape[1]

    @pl.when(lax.axis_index("ctx") + FILTER_PARTS < n_ctx)
    def _():
        def body(t):
            cols = lanes(t * LANES)
            tokens[...] = product[:, cols].astype(F32)
            rate = at_tile(rates, first + t)[...]
            table[0] = jnp.exp(-rate)
            weights[...] = at_tile(weighing, first + t, 0, modes)[...] * jnp.exp(-rate * float(span))
            state = [carry[pl.ds(m * SEGMENTS, SEGMENTS), cols] for m in range(modes)]

            def write(i, value, now):
                scr[step_rows(i), :] = value

            emit(table, weights, state, tokens, write)
            out[:, cols] = scr[...].astype(jnp.bfloat16)

        over_tiles(product.shape[1], body)


def local_kernel(product, rates, weighing, carry, out, tokens, table, weights, *, first):
    modes = rates.shape[1]

    def body(t):
        cols = lanes(t * LANES)
        tokens[...] = product[:, cols].astype(F32)
        table[0] = jnp.exp(-at_tile(rates, first + t)[...])
        weights[...] = at_tile(weighing, first + t, 0, modes)[...]
        gain = row_of(at_tile(weighing, first + t, modes, 1), 0)
        state = [carry[pl.ds(m * SEGMENTS, SEGMENTS), cols] for m in range(modes)]

        def write(i, value, now):
            out[step_rows(i), cols] = value + gain * now

        emit(table, weights, state, tokens, write)

    over_tiles(product.shape[1], body)


def gated(back, mixed, value):
    plain = jnp.dot(back[...], mixed, preferred_element_type=F32)
    return (value.astype(F32) * plain).astype(jnp.bfloat16)


def finish_kernel(*refs, count, n_ch):
    products, carries, overs = refs[:count], refs[count : 2 * count], refs[2 * count : 3 * count]
    refs = refs[3 * count :]
    befores, (rates, weighing, value, late, out, rest) = refs[:n_ch], refs[n_ch : n_ch + 6]
    tokens, table, weights, scr, back, before, mixed, done, sems = refs[n_ch + 6 :]
    modes = rates.shape[1]
    length = value.shape[0]
    steps = length // SEGMENTS
    from_ring(befores, before)
    fill_order(back, True)

    def arriving(tile):
        own, ahead = at_tile(rates, tile), at_tile(before, tile)
        table[0] = jnp.exp(-own[...])
        weights[...] = at_tile(weighing, tile, 0, modes)[...]
        begin = (lax.broadcasted_iota(jnp.int32, (SEGMENTS, LANES), 0) * steps).astype(F32)
        return [jnp.exp(-row_of(own, m) * begin) * row_of(ahead, m) for m in range(modes)]

    copies = [None, None]
    first = 0
    for k in range(count):
        product, carry = products[k], carries[k]
        width = product.shape[1]
        slot = k % 2

        def body(t, first=first, product=product, carry=carry, k=k):
            cols = lanes(t * LANES)
            tokens[...] = product[:, cols].astype(F32)
            gain = row_of(at_tile(weighing, first + t, modes, 1), 0)
            state = arriving(first + t)
            state = [carry[pl.ds(m * SEGMENTS, SEGMENTS), cols] + s for m, s in enumerate(state)]

            def write(i, value, now):
                scr[step_rows(i), :] = value + gain * now

            emit(table, weights, state, tokens, write)
            mixed[:, cols] = (scr[...] - overs[k][:, cols].astype(F32)).astype(jnp.bfloat16)

        over_tiles(width, body)
        if copies[slot] is not None:
            copies[slot].wait()
        wide = math.gcd(width, 4 * LANES)
        for at in range(0, width, wide):
            cols = pl.ds(at, wide)
            done[slot, :, cols] = gated(back, mixed[:, cols], value[:, pl.ds(first * LANES + at, wide)])
        copies[slot] = pltpu.make_async_copy(
            done.at[slot, :, pl.ds(0, width)], out.at[:, pl.ds(first * LANES, width)], sems.at[slot]
        )
        copies[slot].start()
        first += width // LANES

    def add(t):
        cols = lanes(t * LANES)
        state = [row_of(weights, m) * s for m, s in enumerate(arriving(first + t))]
        decay = [row_of(table.at[0], m) for m in range(modes)]
        for i in range(steps):
            state = [d * s for d, s in zip(decay, state)]
            terms = state
            while len(terms) > 1:
                terms = [x + y for x, y in zip(terms[::2], terms[1::2])]
            rest[step_rows(i), cols] = late[step_rows(i), cols] + terms[0]

    over_tiles(late.shape[1], add)
    for copy in copies:
        if copy is not None:
            copy.wait()


def last_kernel(rest, over, value, partial, out, back, done, sem):
    del partial
    _, width = rest.shape
    first = value.shape[1] - width
    fill_order(back, True)
    wide = math.gcd(width, 4 * LANES)
    copies = []
    for k, at in enumerate(range(0, width, wide)):
        cols = pl.ds(at, wide)
        mixed = (rest[:, cols] - over[:, cols].astype(F32)).astype(jnp.bfloat16)
        done[:, cols] = gated(back, mixed, value[:, pl.ds(first + at, wide)])
        copies.append(
            pltpu.make_async_copy(done.at[:, cols], out.at[:, pl.ds(first + at, wide)], sem.at[k])
        )
        copies[-1].start()
    for copy in copies:
        copy.wait()


def shard_program(query, key_in, value, residues, decay_rates, skip_gain):
    length, channels = query.shape
    group, modes = residues.shape
    n_ch, n_ctx = lax.axis_size("ch"), lax.axis_size("ctx")
    span = FILTER_PARTS * length * n_ch
    bf16 = jnp.bfloat16

    shares = RAW_SHARES + DONE_SHARES
    unit = channels // sum(shares)
    widths = [unit * share for share in shares]
    firsts = [sum(widths[:k]) for k in range(len(widths))]
    count, n_raw = len(widths), len(RAW_SHARES)

    vmem = pl.BlockSpec(memory_space=pltpu.VMEM)
    anywhere = pl.BlockSpec(memory_space=pl.ANY)
    hbm = pl.BlockSpec(memory_space=pltpu.HBM)

    def shape(rows, columns, dtype=F32):
        return jax.ShapeDtypeStruct((rows, columns), dtype)

    def stack(rows):
        return jax.ShapeDtypeStruct((n_ch, rows, group), F32)

    tokens_scr = pltpu.VMEM((length, LANES), F32)
    table_scr = pltpu.VMEM((4, modes, LANES), F32)
    weights_scr = pltpu.VMEM((modes, LANES), F32)
    order_scr = pltpu.VMEM((length, length), bf16)

    def call(kernel, out_shape, scratch, args, **options):
        specs = dict(in_specs=[vmem] * len(args), out_specs=jax.tree.map(lambda _: vmem, out_shape))
        specs.update(options)
        return pl.pallas_call(
            kernel,
            out_shape=out_shape,
            scratch_shapes=scratch,
            compiler_params=pltpu.CompilerParams(vmem_limit_bytes=VMEM_BYTES),
            **specs,
        )(*args)

    own_rate = decay_rates.T
    rate_parts = ring([own_rate] * n_ch, "ch")

    products, pasts = [], []
    batches = [[k] for k in range(n_raw)] + [list(range(n_raw, count))]
    for k, batch in enumerate(batches):
        if k == 0:
            read = pltpu.VMEM((length, widths[0]), bf16)
            product = call(
                first_product_kernel,
                shape(length, widths[0], bf16),
                [order_scr, read, read, pltpu.SemaphoreType.DMA((2, 2))],
                tuple(pltpu.with_memory_space_constraint(x, pltpu.HBM) for x in (query, key_in)),
                in_specs=[hbm, hbm],
            )
            products.append(product)
        else:
            products += call(
                functools.partial(product_kernel, first=firsts[batch[0]]),
                [shape(length, widths[j], bf16) for j in batch],
                [order_scr],
                (query, key_in),
            )
        if k < n_raw:
            pasts.append(from_behind(products[k], "ctx", FILTER_PARTS))

    rows = -(-(modes + 1) // SEGMENTS) * SEGMENTS
    own_weight = jnp.concatenate(
        [residues.T, skip_gain[None], jnp.zeros((rows - modes - 1, group), F32)]
    )
    weight_parts = ring([own_weight] * n_ch, "ch")

    outs = call(
        functools.partial(states_kernel, count=count, n_ch=n_ch),
        [shape(modes * SEGMENTS, width) for width in widths] + [shape(modes, group)] * n_ch + [stack(modes)],
        [tokens_scr, table_scr, pltpu.VMEM((n_ch, modes, group), F32)],
        (*products, *rate_parts),
    )
    carries, sums, rates = outs[:count], outs[count:-1], outs[-1]
    sums = ring(sums, "ch")
    weighing = call(assemble_kernel, stack(rows), [], weight_parts)

    overs = []

    def add_over(k):
        overs.append(
            call(
                functools.partial(over_kernel, span=span, first=firsts[k] // LANES),
                shape(length, widths[k]),
                [tokens_scr, table_scr, weights_scr],
                (pasts[k], rates, weighing),
            )
        )

    def ahead_of(k):
        return call(
            functools.partial(ahead_kernel, span=span, first=firsts[k] // LANES, n_ctx=n_ctx),
            shape(length, widths[k], bf16),
            [tokens_scr, table_scr, weights_scr, tokens_scr],
            (products[k], rates, weighing, carries[k]),
        )

    aheads = [ahead_of(k) for k in range(n_raw, count)]
    for k in range(n_raw):
        add_over(k)

    blocks, tails, whole = call(
        functools.partial(tails_kernel, length=length),
        [stack(modes), stack(modes), shape(modes, group)],
        [],
        (*sums, own_rate),
    )
    oldest = from_behind(tails, "ctx", FILTER_PARTS)
    wholes = []
    for j in range(1, FILTER_PARTS):
        wholes.append(from_behind(whole, "ctx", j))
    for ahead in aheads:
        overs.append(from_behind(ahead, "ctx", FILTER_PARTS))
    heads = call(
        functools.partial(heads_kernel, length=length, parts=FILTER_PARTS),
        [shape(modes, group)] * n_ch,
        [pltpu.VMEM((n_ch, modes, group), F32)],
        (blocks, own_rate, oldest, *wholes),
    )
    befores = ring(heads, "ch")

    late = call(
        functools.partial(local_kernel, first=firsts[-1] // LANES),
        shape(length, widths[-1]),
        [tokens_scr, table_scr, weights_scr],
        (products[-1], rates, weighing, carries[-1]),
    )
    widest = max(widths[:-1])
    partial, rest = call(
        functools.partial(finish_kernel, count=count - 1, n_ch=n_ch),
        [shape(length, channels, bf16), shape(length, widths[-1])],
        [
            tokens_scr,
            table_scr,
            weights_scr,
            tokens_scr,
            order_scr,
            pltpu.VMEM((n_ch, modes, group), F32),
            pltpu.VMEM((length, widest), bf16),
            pltpu.VMEM((2, length, widest), bf16),
            pltpu.SemaphoreType.DMA((2,)),
        ],
        (*products[:-1], *carries[:-1], *overs[:-1], *befores, rates, weighing, value, late),
        out_specs=[anywhere, vmem],
    )
    return call(
        last_kernel,
        shape(length, channels, bf16),
        [order_scr, pltpu.VMEM((length, widths[-1]), bf16), pltpu.SemaphoreType.DMA((8,))],
        (rest, overs[-1], value, partial),
        in_specs=[vmem, vmem, vmem, anywhere],
        out_specs=anywhere,
        input_output_aliases={3: 0},
    )


def solution(mesh):
    return jax.shard_map(
        shard_program,
        mesh=mesh,
        in_specs=(
            P(("ctx", "ch"), None),
            P(("ctx", "ch"), None),
            P(("ctx", "ch"), None),
            P("ch", None),
            P("ch", None),
            P("ch"),
        ),
        out_specs=P(("ctx", "ch"), None),
        check_vma=False,
    )
```

```python
import functools
import math

import jax
import jax.numpy as jnp
from jax import lax
from jax.experimental import pallas as pl
from jax.experimental.pallas import tpu as pltpu
from jax.sharding import PartitionSpec as P


FILTER_PARTS = 4
LANES = 128
SEGMENTS = 8
RAW_SHARES = (4, 6)
DONE_SHARES = (6,)
RUN = 8
VMEM_BYTES = 16 << 20
F32 = jnp.float32


def from_behind(value, axis, steps):
    count = lax.axis_size(axis)
    return lax.ppermute(value, axis, [(source, source + steps) for source in range(count - steps)])


def partner(mine, k, count, sign):
    if count & (count - 1) == 0:
        return mine ^ k
    return (mine + sign * k + count) % count


def ring(parts, axis):
    count = lax.axis_size(axis)
    moved = []
    for k, part in enumerate(parts):
        pairs = [(source, partner(source, k, count, 1)) for source in range(count)]
        moved.append(lax.ppermute(part, axis, pairs) if k else part)
    return moved


def from_ring(refs, out):
    count = len(refs)
    mine = lax.axis_index("ch")
    for k, ref in enumerate(refs):
        out[partner(mine, k, count, -1)] = ref[...]


def to_ring(whole, refs):
    count = len(refs)
    mine = lax.axis_index("ch")
    for k, ref in enumerate(refs):
        ref[...] = whole[partner(mine, k, count, 1)]


def row_of(table, m):
    return jnp.broadcast_to(table[pl.ds(m, 1), :], (SEGMENTS, LANES))


def shifted(value, steps):
    row = lax.broadcasted_iota(jnp.int32, value.shape, 0)
    return jnp.where(row >= steps, pltpu.roll(value, steps, 0), 0.0)


def step_rows(i):
    return pl.ds(i * SEGMENTS, SEGMENTS)


def lanes(start):
    return pl.ds(pl.multiple_of(start, LANES), LANES)


def over_tiles(width, body):
    def step(t, carry):
        body(t)
        return carry

    lax.fori_loop(0, width // LANES, step, 0)


def at_tile(table, tile, first=0, count=None):
    per = table.shape[2] // LANES
    count = table.shape[1] if count is None else count
    return table.at[tile // per, pl.ds(first, count), lanes(tile % per * LANES)]


def runs_of(length):
    steps = length // SEGMENTS
    run = min(RUN, steps)
    return run, steps // run


def mode_rows(run, m, modes):
    return pl.ds((run * modes + m) * SEGMENTS, SEGMENTS)


def scan_segments(table, tokens, keep):
    modes = table.shape[1]
    steps = tokens.shape[0] // SEGMENTS
    run, _ = runs_of(tokens.shape[0])
    decay = [row_of(table.at[0], m) for m in range(modes)]
    state = [tokens[step_rows(0), :]] * modes
    for i in range(1, steps):
        if i % run == 0:
            for m in range(modes):
                keep(i // run, m, state[m])
        now = tokens[step_rows(i), :]
        state = [d * s + now for d, s in zip(decay, state)]
    chained = []
    for m in range(modes):
        value = state[m]
        for level in range(3):
            value = value + row_of(table.at[1 + level], m) * shifted(value, 1 << level)
        chained.append(value)
    return chained


def fill_jumps(table, rate, steps):
    table[0] = jnp.exp(-rate)
    for level in range(3):
        table[1 + level] = jnp.exp(-rate * float(steps << level))


def fill_taps(mix, leaps, direct, rate, weight, gain=None):
    decay = jnp.exp(-rate)
    tap = jnp.sum(weight, axis=0, keepdims=True)
    direct[pl.ds(0, 1), :] = tap if gain is None else tap + gain
    now = weight
    for i in range(mix.shape[0]):
        now = now * decay
        mix[i] = now
        if i + 1 < mix.shape[0]:
            direct[pl.ds(i + 1, 1), :] = jnp.sum(now, axis=0, keepdims=True)
    for r in range(1, leaps.shape[0]):
        leaps[r] = jnp.exp(-rate * float(mix.shape[0] * r))


def emit(mix, leaps, direct, state, kept, tokens, write):
    run, modes = mix.shape[:2]
    runs = leaps.shape[0]
    together = min(2, runs)
    for begin in range(0, runs, together):
        group = range(begin, begin + together)
        starts = []
        for r in group:
            if r == 0:
                starts.append([state(m) for m in range(modes)])
            else:
                starts.append([kept(r, m) + row_of(leaps.at[r], m) * state(m) for m in range(modes)])
        for i in range(run):
            sums = [None] * together
            for m in range(modes):
                weight = row_of(mix.at[i], m)
                for j in range(together):
                    term = weight * starts[j][m]
                    sums[j] = term if sums[j] is None else sums[j] + term
            for d in range(i + 1):
                tap = row_of(direct, d)
                for j, r in enumerate(group):
                    sums[j] = sums[j] + tap * tokens[step_rows(r * run + i - d), :]
            for j, r in enumerate(group):
                write(r * run + i, sums[j])


def fill_order(order, back=False):
    length = order.shape[0]
    row = lax.broadcasted_iota(jnp.int32, order.shape, 0)
    col = lax.broadcasted_iota(jnp.int32, order.shape, 1)
    inner = length // SEGMENTS if back else SEGMENTS
    order[...] = jnp.where(row % inner * (length // inner) + row // inner == col, 1.0, 0.0).astype(order.dtype)


def product_kernel(query, key_in, *refs, first):
    outs, order = refs[:-1], refs[-1]
    fill_order(order)
    start = first
    for out in outs:
        width = out.shape[1]
        wide = math.gcd(width, 4 * LANES)
        for at in range(0, width, wide):
            cols = pl.ds(start + at, wide)
            product = (query[:, cols].astype(F32) * key_in[:, cols].astype(F32)).astype(jnp.bfloat16)
            out[:, pl.ds(at, wide)] = jnp.dot(
                order[...], product, preferred_element_type=F32
            ).astype(jnp.bfloat16)
        start += width


def first_product_kernel(query, key_in, out, order, left, right, sems):
    width = out.shape[1]
    wide = width // sems.shape[0]
    copies = []
    for k in range(sems.shape[0]):
        cols = pl.ds(k * wide, wide)
        for j, (source, into) in enumerate(((query, left), (key_in, right))):
            copies.append(pltpu.make_async_copy(source.at[:, cols], into.at[:, cols], sems.at[k, j]))
            copies[-1].start()
    fill_order(order)
    for k in range(sems.shape[0]):
        cols = pl.ds(k * wide, wide)
        copies[2 * k].wait()
        copies[2 * k + 1].wait()
        product = (left[:, cols].astype(F32) * right[:, cols].astype(F32)).astype(jnp.bfloat16)
        out[:, cols] = jnp.dot(order[...], product, preferred_element_type=F32).astype(jnp.bfloat16)


def states_kernel(*refs, count, n_ch):
    products, parts = refs[:count], refs[count : count + n_ch]
    carries, sums = refs[count + n_ch : 2 * count + n_ch], refs[2 * count + n_ch : 2 * count + 2 * n_ch]
    rates, tokens, table, totals = refs[2 * count + 2 * n_ch :]
    from_ring(parts, rates)
    modes = rates.shape[1]
    first = 0
    for product, carry_out in zip(products, carries):
        steps = product.shape[0] // SEGMENTS

        def body(t, first=first, product=product, carry_out=carry_out):
            cols = lanes(t * LANES)
            tokens[...] = product[:, cols].astype(F32)
            fill_jumps(table, at_tile(rates, first + t)[...], steps)

            def keep(r, m, state, cols=cols, carry_out=carry_out):
                carry_out[mode_rows(r, m, modes), cols] = state

            state = scan_segments(table, tokens, keep)
            into = at_tile(totals, first + t)
            for m in range(modes):
                carry_out[mode_rows(0, m, modes), cols] = shifted(state[m], 1)
                into[pl.ds(m, 1), :] = state[m][SEGMENTS - 1 :, :]

        over_tiles(product.shape[1], body)
        first += product.shape[1] // LANES
    to_ring(totals, sums)


def assemble_kernel(*refs):
    from_ring(refs[:-1], refs[-1])


def tails_kernel(*refs, length):
    *parts, rate, blocks, tails, whole = refs
    from_ring(parts, blocks)
    count = len(parts)
    running = None
    for q in reversed(range(count)):
        now = blocks[q]
        if running is not None:
            now = running + jnp.exp(-rate[...] * float(length * (count - 1 - q))) * now
        running = now
        tails[q] = running
    whole[...] = running


def heads_kernel(*refs, length, parts):
    blocks, rate, oldest, *rest = refs
    wholes, outs, heads = rest[: parts - 1], rest[parts - 1 : -1], rest[-1]
    count = blocks.shape[0]
    rates = rate[...]
    older = wholes[0][...]
    for j in range(1, parts - 1):
        older = older + jnp.exp(-rates * float(length * count * j)) * wholes[j][...]
    last = jnp.exp(-rates * float(length * count * (parts - 1)))
    jump = jnp.exp(-rates * float(length))
    running = None
    for q in range(count):
        earlier = older + last * oldest[q]
        if running is None:
            heads[q] = earlier
            running = blocks[q]
        else:
            heads[q] = running + jnp.exp(-rates * float(length * q)) * earlier
            running = jump * running + blocks[q]
    to_ring(heads, outs)


def over_kernel(past, rates, weighing, out, tokens, table, mix, leaps, direct, carry, *, span, first):
    steps = past.shape[0] // SEGMENTS
    modes = rates.shape[1]
    needed = lax.axis_index("ctx") >= FILTER_PARTS

    @pl.when(needed)
    def _():
        def body(t):
            cols = lanes(t * LANES)
            tokens[...] = past[:, cols].astype(F32)
            rate = at_tile(rates, first + t)[...]
            fill_jumps(table, rate, steps)
            weight = at_tile(weighing, first + t, 0, modes)[...] * jnp.exp(-rate * float(span))
            fill_taps(mix, leaps, direct, rate, weight)

            def keep(r, m, state):
                carry[mode_rows(r, m, modes), :] = state

            for m, state in enumerate(scan_segments(table, tokens, keep)):
                carry[mode_rows(0, m, modes), :] = shifted(state, 1)

            def kept(r, m):
                return carry[mode_rows(r, m, modes), :]

            def write(i, value):
                out[step_rows(i), cols] = value

            emit(mix, leaps, direct, lambda m: kept(0, m), kept, tokens, write)

        over_tiles(past.shape[1], body)

    @pl.when(jnp.logical_not(needed))
    def _():
        out[...] = jnp.zeros_like(out)


def ahead_kernel(product, rates, weighing, carry, out, tokens, mix, leaps, direct, scr, *, span, first, n_ctx):
    modes = rates.shape[1]

    @pl.when(lax.axis_index("ctx") + FILTER_PARTS < n_ctx)
    def _():
        def body(t):
            cols = lanes(t * LANES)
            tokens[...] = product[:, cols].astype(F32)
            rate = at_tile(rates, first + t)[...]
            weight = at_tile(weighing, first + t, 0, modes)[...] * jnp.exp(-rate * float(span))
            fill_taps(mix, leaps, direct, rate, weight)

            def kept(r, m):
                return carry[mode_rows(r, m, modes), cols]

            def write(i, value):
                scr[step_rows(i), :] = value

            emit(mix, leaps, direct, lambda m: kept(0, m), kept, tokens, write)
            out[:, cols] = scr[...].astype(jnp.bfloat16)

        over_tiles(product.shape[1], body)


def local_kernel(product, rates, weighing, carry, out, tokens, mix, leaps, direct, *, first):
    modes = rates.shape[1]

    def body(t):
        cols = lanes(t * LANES)
        tokens[...] = product[:, cols].astype(F32)
        own = at_tile(weighing, first + t)
        fill_taps(
            mix,
            leaps,
            direct,
            at_tile(rates, first + t)[...],
            own[pl.ds(0, modes), :],
            own[pl.ds(modes, 1), :],
        )

        def kept(r, m):
            return carry[mode_rows(r, m, modes), cols]

        def write(i, value):
            out[step_rows(i), cols] = value

        emit(mix, leaps, direct, lambda m: kept(0, m), kept, tokens, write)

    over_tiles(product.shape[1], body)


def gated(back, mixed, value):
    plain = jnp.dot(back[...], mixed, preferred_element_type=F32)
    return (value.astype(F32) * plain).astype(jnp.bfloat16)


def finish_kernel(*refs, count, n_ch):
    products, carries, overs = refs[:count], refs[count : 2 * count], refs[2 * count : 3 * count]
    refs = refs[3 * count :]
    befores, (rates, weighing, value, late, out, rest) = refs[:n_ch], refs[n_ch : n_ch + 6]
    tokens, table, weights, scr, back, before, mixed, done, sems, mix, leaps, direct, coming = refs[n_ch + 6 :]
    modes = rates.shape[1]
    length = value.shape[0]
    steps = length // SEGMENTS
    from_ring(befores, before)
    fill_order(back, True)

    def arriving(tile):
        own, ahead = at_tile(rates, tile), at_tile(before, tile)
        table[0] = jnp.exp(-own[...])
        weights[...] = at_tile(weighing, tile, 0, modes)[...]
        begin = (lax.broadcasted_iota(jnp.int32, (SEGMENTS, LANES), 0) * steps).astype(F32)
        return [jnp.exp(-row_of(own, m) * begin) * row_of(ahead, m) for m in range(modes)]

    copies = [None, None]
    first = 0
    for k in range(count):
        product, carry = products[k], carries[k]
        width = product.shape[1]
        slot = k % 2

        def body(t, first=first, product=product, carry=carry, k=k):
            cols = lanes(t * LANES)
            tokens[...] = product[:, cols].astype(F32)
            own = at_tile(weighing, first + t)
            for m, state in enumerate(arriving(first + t)):
                coming[step_rows(m), :] = carry[mode_rows(0, m, modes), cols] + state
            rate = at_tile(rates, first + t)[...]
            fill_taps(mix, leaps, direct, rate, own[pl.ds(0, modes), :], own[pl.ds(modes, 1), :])

            def kept(r, m):
                return carry[mode_rows(r, m, modes), cols]

            def write(i, value):
                scr[step_rows(i), :] = value

            emit(mix, leaps, direct, lambda m: coming[step_rows(m), :], kept, tokens, write)
            mixed[:, cols] = (scr[...] - overs[k][:, cols].astype(F32)).astype(jnp.bfloat16)

        over_tiles(width, body)
        if copies[slot] is not None:
            copies[slot].wait()
        wide = math.gcd(width, 4 * LANES)
        for at in range(0, width, wide):
            cols = pl.ds(at, wide)
            done[slot, :, cols] = gated(back, mixed[:, cols], value[:, pl.ds(first * LANES + at, wide)])
        copies[slot] = pltpu.make_async_copy(
            done.at[slot, :, pl.ds(0, width)], out.at[:, pl.ds(first * LANES, width)], sems.at[slot]
        )
        copies[slot].start()
        first += width // LANES

    def add(t):
        cols = lanes(t * LANES)
        state = [row_of(weights, m) * s for m, s in enumerate(arriving(first + t))]
        decay = [row_of(table.at[0], m) for m in range(modes)]
        for i in range(steps):
            state = [d * s for d, s in zip(decay, state)]
            terms = state
            while len(terms) > 1:
                terms = [x + y for x, y in zip(terms[::2], terms[1::2])]
            rest[step_rows(i), cols] = late[step_rows(i), cols] + terms[0]

    over_tiles(late.shape[1], add)
    for copy in copies:
        if copy is not None:
            copy.wait()


def last_kernel(rest, over, value, partial, out, back, done, sem):
    del partial
    _, width = rest.shape
    first = value.shape[1] - width
    fill_order(back, True)
    wide = math.gcd(width, 4 * LANES)
    copies = []
    for k, at in enumerate(range(0, width, wide)):
        cols = pl.ds(at, wide)
        mixed = (rest[:, cols] - over[:, cols].astype(F32)).astype(jnp.bfloat16)
        done[:, cols] = gated(back, mixed, value[:, pl.ds(first + at, wide)])
        copies.append(
            pltpu.make_async_copy(done.at[:, cols], out.at[:, pl.ds(first + at, wide)], sem.at[k])
        )
        copies[-1].start()
    for copy in copies:
        copy.wait()


def shard_program(query, key_in, value, residues, decay_rates, skip_gain):
    length, channels = query.shape
    group, modes = residues.shape
    n_ch, n_ctx = lax.axis_size("ch"), lax.axis_size("ctx")
    span = FILTER_PARTS * length * n_ch
    bf16 = jnp.bfloat16

    shares = RAW_SHARES + DONE_SHARES
    unit = channels // sum(shares)
    widths = [unit * share for share in shares]
    firsts = [sum(widths[:k]) for k in range(len(widths))]
    count, n_raw = len(widths), len(RAW_SHARES)

    vmem = pl.BlockSpec(memory_space=pltpu.VMEM)
    anywhere = pl.BlockSpec(memory_space=pl.ANY)
    hbm = pl.BlockSpec(memory_space=pltpu.HBM)

    def shape(rows, columns, dtype=F32):
        return jax.ShapeDtypeStruct((rows, columns), dtype)

    def stack(rows):
        return jax.ShapeDtypeStruct((n_ch, rows, group), F32)

    tokens_scr = pltpu.VMEM((length, LANES), F32)
    table_scr = pltpu.VMEM((4, modes, LANES), F32)
    weights_scr = pltpu.VMEM((modes, LANES), F32)
    order_scr = pltpu.VMEM((length, length), bf16)
    run, runs = runs_of(length)
    taps_scr = [
        pltpu.VMEM((run, modes, LANES), F32),
        pltpu.VMEM((runs, modes, LANES), F32),
        pltpu.VMEM((run, LANES), F32),
    ]

    def call(kernel, out_shape, scratch, args, **options):
        specs = dict(in_specs=[vmem] * len(args), out_specs=jax.tree.map(lambda _: vmem, out_shape))
        specs.update(options)
        return pl.pallas_call(
            kernel,
            out_shape=out_shape,
            scratch_shapes=scratch,
            compiler_params=pltpu.CompilerParams(vmem_limit_bytes=VMEM_BYTES),
            **specs,
        )(*args)

    own_rate = decay_rates.T
    rate_parts = ring([own_rate] * n_ch, "ch")

    products, pasts = [], []
    batches = [[k] for k in range(n_raw)] + [list(range(n_raw, count))]
    for k, batch in enumerate(batches):
        if k == 0:
            read = pltpu.VMEM((length, widths[0]), bf16)
            product = call(
                first_product_kernel,
                shape(length, widths[0], bf16),
                [order_scr, read, read, pltpu.SemaphoreType.DMA((2, 2))],
                tuple(pltpu.with_memory_space_constraint(x, pltpu.HBM) for x in (query, key_in)),
                in_specs=[hbm, hbm],
            )
            products.append(product)
        else:
            products += call(
                functools.partial(product_kernel, first=firsts[batch[0]]),
                [shape(length, widths[j], bf16) for j in batch],
                [order_scr],
                (query, key_in),
            )
        if k < n_raw:
            pasts.append(from_behind(products[k], "ctx", FILTER_PARTS))

    rows = -(-(modes + 1) // SEGMENTS) * SEGMENTS
    own_weight = jnp.concatenate(
        [residues.T, skip_gain[None], jnp.zeros((rows - modes - 1, group), F32)]
    )
    weight_parts = ring([own_weight] * n_ch, "ch")

    outs = call(
        functools.partial(states_kernel, count=count, n_ch=n_ch),
        [shape(runs * modes * SEGMENTS, width) for width in widths] + [shape(modes, group)] * n_ch + [stack(modes)],
        [tokens_scr, table_scr, pltpu.VMEM((n_ch, modes, group), F32)],
        (*products, *rate_parts),
    )
    carries, sums, rates = outs[:count], outs[count:-1], outs[-1]
    sums = ring(sums, "ch")
    weighing = call(assemble_kernel, stack(rows), [], weight_parts)

    overs = []

    def add_over(k):
        overs.append(
            call(
                functools.partial(over_kernel, span=span, first=firsts[k] // LANES),
                shape(length, widths[k]),
                [tokens_scr, table_scr, *taps_scr, pltpu.VMEM((runs * modes * SEGMENTS, LANES), F32)],
                (pasts[k], rates, weighing),
            )
        )

    def ahead_of(k):
        return call(
            functools.partial(ahead_kernel, span=span, first=firsts[k] // LANES, n_ctx=n_ctx),
            shape(length, widths[k], bf16),
            [tokens_scr, *taps_scr, tokens_scr],
            (products[k], rates, weighing, carries[k]),
        )

    aheads = [ahead_of(k) for k in range(n_raw, count)]
    for k in range(n_raw):
        add_over(k)

    blocks, tails, whole = call(
        functools.partial(tails_kernel, length=length),
        [stack(modes), stack(modes), shape(modes, group)],
        [],
        (*sums, own_rate),
    )
    oldest = from_behind(tails, "ctx", FILTER_PARTS)
    wholes = []
    for j in range(1, FILTER_PARTS):
        wholes.append(from_behind(whole, "ctx", j))
    for ahead in aheads:
        overs.append(from_behind(ahead, "ctx", FILTER_PARTS))
    heads = call(
        functools.partial(heads_kernel, length=length, parts=FILTER_PARTS),
        [shape(modes, group)] * n_ch,
        [pltpu.VMEM((n_ch, modes, group), F32)],
        (blocks, own_rate, oldest, *wholes),
    )
    befores = ring(heads, "ch")

    late = call(
        functools.partial(local_kernel, first=firsts[-1] // LANES),
        shape(length, widths[-1]),
        [tokens_scr, *taps_scr],
        (products[-1], rates, weighing, carries[-1]),
    )
    widest = max(widths[:-1])
    partial, rest = call(
        functools.partial(finish_kernel, count=count - 1, n_ch=n_ch),
        [shape(length, channels, bf16), shape(length, widths[-1])],
        [
            tokens_scr,
            table_scr,
            weights_scr,
            tokens_scr,
            order_scr,
            pltpu.VMEM((n_ch, modes, group), F32),
            pltpu.VMEM((length, widest), bf16),
            pltpu.VMEM((2, length, widest), bf16),
            pltpu.SemaphoreType.DMA((2,)),
            *taps_scr,
            pltpu.VMEM((modes * SEGMENTS, LANES), F32),
        ],
        (*products[:-1], *carries[:-1], *overs[:-1], *befores, rates, weighing, value, late),
        out_specs=[anywhere, vmem],
    )
    return call(
        last_kernel,
        shape(length, channels, bf16),
        [order_scr, pltpu.VMEM((length, widths[-1]), bf16), pltpu.SemaphoreType.DMA((8,))],
        (rest, overs[-1], value, partial),
        in_specs=[vmem, vmem, vmem, anywhere],
        out_specs=anywhere,
        input_output_aliases={3: 0},
    )


def solution(mesh):
    return jax.shard_map(
        shard_program,
        mesh=mesh,
        in_specs=(
            P(("ctx", "ch"), None),
            P(("ctx", "ch"), None),
            P(("ctx", "ch"), None),
            P("ch", None),
            P("ch", None),
            P("ch"),
        ),
        out_specs=P(("ctx", "ch"), None),
        check_vma=False,
    )
```

```python
import functools
import math

import jax
import jax.numpy as jnp
from jax import lax
from jax.experimental import pallas as pl
from jax.experimental.pallas import tpu as pltpu
from jax.sharding import PartitionSpec as P


FILTER_PARTS = 4
LANES = 128
SEGMENTS = 8
RAW_SHARES = (4, 5)
DONE_SHARES = (7,)
RUN = 8
VMEM_BYTES = 16 << 20
F32 = jnp.float32


def from_behind(value, axis, steps):
    count = lax.axis_size(axis)
    return lax.ppermute(value, axis, [(source, source + steps) for source in range(count - steps)])


def partner(mine, k, count, sign):
    if count & (count - 1) == 0:
        return mine ^ k
    return (mine + sign * k + count) % count


def ring(parts, axis):
    count = lax.axis_size(axis)
    moved = []
    for k, part in enumerate(parts):
        pairs = [(source, partner(source, k, count, 1)) for source in range(count)]
        moved.append(lax.ppermute(part, axis, pairs) if k else part)
    return moved


def from_ring(refs, out):
    count = len(refs)
    mine = lax.axis_index("ch")
    for k, ref in enumerate(refs):
        out[partner(mine, k, count, -1)] = ref[...]


def to_ring(whole, refs):
    count = len(refs)
    mine = lax.axis_index("ch")
    for k, ref in enumerate(refs):
        ref[...] = whole[partner(mine, k, count, 1)]


def row_of(table, m):
    return jnp.broadcast_to(table[pl.ds(m, 1), :], (SEGMENTS, LANES))


def shifted(value, steps):
    row = lax.broadcasted_iota(jnp.int32, value.shape, 0)
    return jnp.where(row >= steps, pltpu.roll(value, steps, 0), 0.0)


def step_rows(i):
    return pl.ds(i * SEGMENTS, SEGMENTS)


def lanes(start):
    return pl.ds(pl.multiple_of(start, LANES), LANES)


def over_tiles(width, body):
    def step(t, carry):
        body(t)
        return carry

    lax.fori_loop(0, width // LANES, step, 0)


def at_tile(table, tile, first=0, count=None):
    per = table.shape[2] // LANES
    count = table.shape[1] if count is None else count
    return table.at[tile // per, pl.ds(first, count), lanes(tile % per * LANES)]


def runs_of(length):
    steps = length // SEGMENTS
    run = min(RUN, steps)
    return run, steps // run


def mode_rows(run, m, modes):
    return pl.ds((run * modes + m) * SEGMENTS, SEGMENTS)


def scan_segments(table, tokens, keep):
    modes = table.shape[1]
    steps = tokens.shape[0] // SEGMENTS
    run, _ = runs_of(tokens.shape[0])
    decay = [row_of(table.at[0], m) for m in range(modes)]
    state = [tokens[step_rows(0), :]] * modes
    for i in range(1, steps):
        if i % run == 0:
            for m in range(modes):
                keep(i // run, m, state[m])
        now = tokens[step_rows(i), :]
        state = [d * s + now for d, s in zip(decay, state)]
    chained = []
    for m in range(modes):
        value = state[m]
        for level in range(3):
            value = value + row_of(table.at[1 + level], m) * shifted(value, 1 << level)
        chained.append(value)
    return chained


def fill_jumps(table, rate, steps):
    table[0] = jnp.exp(-rate)
    for level in range(3):
        table[1 + level] = jnp.exp(-rate * float(steps << level))


def fill_taps(mix, leaps, direct, rate, weight, gain=None):
    decay = jnp.exp(-rate)
    tap = jnp.sum(weight, axis=0, keepdims=True)
    direct[pl.ds(0, 1), :] = tap if gain is None else tap + gain
    now = weight
    for i in range(mix.shape[0]):
        now = now * decay
        mix[i] = now
        if i + 1 < mix.shape[0]:
            direct[pl.ds(i + 1, 1), :] = jnp.sum(now, axis=0, keepdims=True)
    for r in range(1, leaps.shape[0]):
        leaps[r] = jnp.exp(-rate * float(mix.shape[0] * r))


def emit(mix, leaps, direct, state, kept, tokens, write):
    run, modes = mix.shape[:2]
    runs = leaps.shape[0]
    together = min(2, runs)
    for begin in range(0, runs, together):
        group = range(begin, begin + together)
        starts = []
        for r in group:
            if r == 0:
                starts.append([state(m) for m in range(modes)])
            else:
                starts.append([kept(r, m) + row_of(leaps.at[r], m) * state(m) for m in range(modes)])
        for i in range(run):
            sums = [None] * together
            for m in range(modes):
                weight = row_of(mix.at[i], m)
                for j in range(together):
                    term = weight * starts[j][m]
                    sums[j] = term if sums[j] is None else sums[j] + term
            for d in range(i + 1):
                tap = row_of(direct, d)
                for j, r in enumerate(group):
                    sums[j] = sums[j] + tap * tokens[step_rows(r * run + i - d), :]
            for j, r in enumerate(group):
                write(r * run + i, sums[j])


def fill_order(order, back=False):
    length = order.shape[0]
    row = lax.broadcasted_iota(jnp.int32, order.shape, 0)
    col = lax.broadcasted_iota(jnp.int32, order.shape, 1)
    inner = length // SEGMENTS if back else SEGMENTS
    order[...] = jnp.where(row % inner * (length // inner) + row // inner == col, 1.0, 0.0).astype(order.dtype)


def product_kernel(query, key_in, *refs, first):
    outs, order = refs[:-1], refs[-1]
    fill_order(order)
    start = first
    for out in outs:
        width = out.shape[1]
        wide = math.gcd(width, 4 * LANES)
        for at in range(0, width, wide):
            cols = pl.ds(start + at, wide)
            product = (query[:, cols].astype(F32) * key_in[:, cols].astype(F32)).astype(jnp.bfloat16)
            out[:, pl.ds(at, wide)] = jnp.dot(
                order[...], product, preferred_element_type=F32
            ).astype(jnp.bfloat16)
        start += width


def first_product_kernel(query, key_in, out, order, left, right, sems):
    width = out.shape[1]
    wide = width // sems.shape[0]
    copies = []
    for k in range(sems.shape[0]):
        cols = pl.ds(k * wide, wide)
        for j, (source, into) in enumerate(((query, left), (key_in, right))):
            copies.append(pltpu.make_async_copy(source.at[:, cols], into.at[:, cols], sems.at[k, j]))
            copies[-1].start()
    fill_order(order)
    for k in range(sems.shape[0]):
        cols = pl.ds(k * wide, wide)
        copies[2 * k].wait()
        copies[2 * k + 1].wait()
        product = (left[:, cols].astype(F32) * right[:, cols].astype(F32)).astype(jnp.bfloat16)
        out[:, cols] = jnp.dot(order[...], product, preferred_element_type=F32).astype(jnp.bfloat16)


def states_kernel(*refs, count, n_ch):
    products, parts = refs[:count], refs[count : count + n_ch]
    carries, sums = refs[count + n_ch : 2 * count + n_ch], refs[2 * count + n_ch : 2 * count + 2 * n_ch]
    rates, tokens, table, totals = refs[2 * count + 2 * n_ch :]
    from_ring(parts, rates)
    modes = rates.shape[1]
    first = 0
    for product, carry_out in zip(products, carries):
        steps = product.shape[0] // SEGMENTS

        def body(t, first=first, product=product, carry_out=carry_out):
            cols = lanes(t * LANES)
            tokens[...] = product[:, cols].astype(F32)
            fill_jumps(table, at_tile(rates, first + t)[...], steps)

            def keep(r, m, state, cols=cols, carry_out=carry_out):
                carry_out[mode_rows(r, m, modes), cols] = state

            state = scan_segments(table, tokens, keep)
            into = at_tile(totals, first + t)
            for m in range(modes):
                carry_out[mode_rows(0, m, modes), cols] = shifted(state[m], 1)
                into[pl.ds(m, 1), :] = state[m][SEGMENTS - 1 :, :]

        over_tiles(product.shape[1], body)
        first += product.shape[1] // LANES
    to_ring(totals, sums)


def assemble_kernel(*refs):
    from_ring(refs[:-1], refs[-1])


def tails_kernel(*refs, length):
    *parts, rate, blocks, tails, whole = refs
    from_ring(parts, blocks)
    count = len(parts)
    running = None
    for q in reversed(range(count)):
        now = blocks[q]
        if running is not None:
            now = running + jnp.exp(-rate[...] * float(length * (count - 1 - q))) * now
        running = now
        tails[q] = running
    whole[...] = running


def pair_kernel(whole, earlier, rate, out, *, part):
    out[...] = whole[...] + jnp.exp(-rate[...] * float(part)) * earlier[...]


def heads_kernel(*refs, length, parts):
    blocks, rate, oldest, newer, pairs, *outs, heads = refs
    count = blocks.shape[0]
    rates = rate[...]
    older = newer[...] + jnp.exp(-rates * float(length * count)) * pairs[...]
    last = jnp.exp(-rates * float(length * count * (parts - 1)))
    jump = jnp.exp(-rates * float(length))
    running = None
    for q in range(count):
        earlier = older + last * oldest[q]
        if running is None:
            heads[q] = earlier
            running = blocks[q]
        else:
            heads[q] = running + jnp.exp(-rates * float(length * q)) * earlier
            running = jump * running + blocks[q]
    to_ring(heads, outs)


def over_kernel(past, rates, weighing, out, tokens, table, mix, leaps, direct, carry, *, span, first):
    steps = past.shape[0] // SEGMENTS
    modes = rates.shape[1]
    needed = lax.axis_index("ctx") >= FILTER_PARTS

    @pl.when(needed)
    def _():
        def body(t):
            cols = lanes(t * LANES)
            tokens[...] = past[:, cols].astype(F32)
            rate = at_tile(rates, first + t)[...]
            fill_jumps(table, rate, steps)
            weight = at_tile(weighing, first + t, 0, modes)[...] * jnp.exp(-rate * float(span))
            fill_taps(mix, leaps, direct, rate, weight)

            def keep(r, m, state):
                carry[mode_rows(r, m, modes), :] = state

            for m, state in enumerate(scan_segments(table, tokens, keep)):
                carry[mode_rows(0, m, modes), :] = shifted(state, 1)

            def kept(r, m):
                return carry[mode_rows(r, m, modes), :]

            def write(i, value):
                out[step_rows(i), cols] = value

            emit(mix, leaps, direct, lambda m: kept(0, m), kept, tokens, write)

        over_tiles(past.shape[1], body)

    @pl.when(jnp.logical_not(needed))
    def _():
        out[...] = jnp.zeros_like(out)


def ahead_kernel(product, rates, weighing, carry, out, tokens, mix, leaps, direct, scr, *, span, first, n_ctx):
    modes = rates.shape[1]

    @pl.when(lax.axis_index("ctx") + FILTER_PARTS < n_ctx)
    def _():
        def body(t):
            cols = lanes(t * LANES)
            tokens[...] = product[:, cols].astype(F32)
            rate = at_tile(rates, first + t)[...]
            weight = at_tile(weighing, first + t, 0, modes)[...] * jnp.exp(-rate * float(span))
            fill_taps(mix, leaps, direct, rate, weight)

            def kept(r, m):
                return carry[mode_rows(r, m, modes), cols]

            def write(i, value):
                scr[step_rows(i), :] = value

            emit(mix, leaps, direct, lambda m: kept(0, m), kept, tokens, write)
            out[:, cols] = scr[...].astype(jnp.bfloat16)

        over_tiles(product.shape[1], body)


def local_kernel(product, rates, weighing, carry, out, tokens, mix, leaps, direct, *, first):
    modes = rates.shape[1]

    def body(t):
        cols = lanes(t * LANES)
        tokens[...] = product[:, cols].astype(F32)
        own = at_tile(weighing, first + t)
        fill_taps(
            mix,
            leaps,
            direct,
            at_tile(rates, first + t)[...],
            own[pl.ds(0, modes), :],
            own[pl.ds(modes, 1), :],
        )

        def kept(r, m):
            return carry[mode_rows(r, m, modes), cols]

        def write(i, value):
            out[step_rows(i), cols] = value

        emit(mix, leaps, direct, lambda m: kept(0, m), kept, tokens, write)

    over_tiles(product.shape[1], body)


def gated(back, mixed, value):
    plain = jnp.dot(back[...], mixed, preferred_element_type=F32)
    return (value.astype(F32) * plain).astype(jnp.bfloat16)


def finish_kernel(*refs, count, n_ch):
    products, carries, overs = refs[:count], refs[count : 2 * count], refs[2 * count : 3 * count]
    refs = refs[3 * count :]
    befores, (rates, weighing, value, late, out, rest) = refs[:n_ch], refs[n_ch : n_ch + 6]
    tokens, table, weights, scr, back, before, mixed, done, sems, mix, leaps, direct, coming = refs[n_ch + 6 :]
    modes = rates.shape[1]
    length = value.shape[0]
    steps = length // SEGMENTS
    from_ring(befores, before)
    fill_order(back, True)

    def arriving(tile):
        own, ahead = at_tile(rates, tile), at_tile(before, tile)
        table[0] = jnp.exp(-own[...])
        weights[...] = at_tile(weighing, tile, 0, modes)[...]
        begin = (lax.broadcasted_iota(jnp.int32, (SEGMENTS, LANES), 0) * steps).astype(F32)
        return [jnp.exp(-row_of(own, m) * begin) * row_of(ahead, m) for m in range(modes)]

    copies = [None, None]
    first = 0
    for k in range(count):
        product, carry = products[k], carries[k]
        width = product.shape[1]
        slot = k % 2

        def body(t, first=first, product=product, carry=carry, k=k):
            cols = lanes(t * LANES)
            tokens[...] = product[:, cols].astype(F32)
            own = at_tile(weighing, first + t)
            for m, state in enumerate(arriving(first + t)):
                coming[step_rows(m), :] = carry[mode_rows(0, m, modes), cols] + state
            rate = at_tile(rates, first + t)[...]
            fill_taps(mix, leaps, direct, rate, own[pl.ds(0, modes), :], own[pl.ds(modes, 1), :])

            def kept(r, m):
                return carry[mode_rows(r, m, modes), cols]

            def write(i, value):
                scr[step_rows(i), :] = value

            emit(mix, leaps, direct, lambda m: coming[step_rows(m), :], kept, tokens, write)
            mixed[:, cols] = (scr[...] - overs[k][:, cols].astype(F32)).astype(jnp.bfloat16)

        over_tiles(width, body)
        if copies[slot] is not None:
            copies[slot].wait()
        wide = math.gcd(width, 4 * LANES)
        for at in range(0, width, wide):
            cols = pl.ds(at, wide)
            done[slot, :, cols] = gated(back, mixed[:, cols], value[:, pl.ds(first * LANES + at, wide)])
        copies[slot] = pltpu.make_async_copy(
            done.at[slot, :, pl.ds(0, width)], out.at[:, pl.ds(first * LANES, width)], sems.at[slot]
        )
        copies[slot].start()
        first += width // LANES

    def add(t):
        cols = lanes(t * LANES)
        state = [row_of(weights, m) * s for m, s in enumerate(arriving(first + t))]
        decay = [row_of(table.at[0], m) for m in range(modes)]
        for i in range(steps):
            state = [d * s for d, s in zip(decay, state)]
            terms = state
            while len(terms) > 1:
                terms = [x + y for x, y in zip(terms[::2], terms[1::2])]
            rest[step_rows(i), cols] = late[step_rows(i), cols] + terms[0]

    over_tiles(late.shape[1], add)
    for copy in copies:
        if copy is not None:
            copy.wait()


def last_kernel(rest, over, value, partial, out, back, done, sem):
    del partial
    _, width = rest.shape
    first = value.shape[1] - width
    fill_order(back, True)
    wide = math.gcd(width, 4 * LANES)
    copies = []
    for k, at in enumerate(range(0, width, wide)):
        cols = pl.ds(at, wide)
        mixed = (rest[:, cols] - over[:, cols].astype(F32)).astype(jnp.bfloat16)
        done[:, cols] = gated(back, mixed, value[:, pl.ds(first + at, wide)])
        copies.append(
            pltpu.make_async_copy(done.at[:, cols], out.at[:, pl.ds(first + at, wide)], sem.at[k])
        )
        copies[-1].start()
    for copy in copies:
        copy.wait()


def shard_program(query, key_in, value, residues, decay_rates, skip_gain):
    length, channels = query.shape
    group, modes = residues.shape
    n_ch, n_ctx = lax.axis_size("ch"), lax.axis_size("ctx")
    span = FILTER_PARTS * length * n_ch
    bf16 = jnp.bfloat16

    shares = RAW_SHARES + DONE_SHARES
    unit = channels // sum(shares)
    widths = [unit * share for share in shares]
    firsts = [sum(widths[:k]) for k in range(len(widths))]
    count, n_raw = len(widths), len(RAW_SHARES)

    vmem = pl.BlockSpec(memory_space=pltpu.VMEM)
    anywhere = pl.BlockSpec(memory_space=pl.ANY)
    hbm = pl.BlockSpec(memory_space=pltpu.HBM)

    def shape(rows, columns, dtype=F32):
        return jax.ShapeDtypeStruct((rows, columns), dtype)

    def stack(rows):
        return jax.ShapeDtypeStruct((n_ch, rows, group), F32)

    tokens_scr = pltpu.VMEM((length, LANES), F32)
    table_scr = pltpu.VMEM((4, modes, LANES), F32)
    weights_scr = pltpu.VMEM((modes, LANES), F32)
    order_scr = pltpu.VMEM((length, length), bf16)
    run, runs = runs_of(length)
    taps_scr = [
        pltpu.VMEM((run, modes, LANES), F32),
        pltpu.VMEM((runs, modes, LANES), F32),
        pltpu.VMEM((run, LANES), F32),
    ]

    def call(kernel, out_shape, scratch, args, **options):
        specs = dict(in_specs=[vmem] * len(args), out_specs=jax.tree.map(lambda _: vmem, out_shape))
        specs.update(options)
        return pl.pallas_call(
            kernel,
            out_shape=out_shape,
            scratch_shapes=scratch,
            compiler_params=pltpu.CompilerParams(vmem_limit_bytes=VMEM_BYTES),
            **specs,
        )(*args)

    own_rate = decay_rates.T
    rate_parts = ring([own_rate] * n_ch, "ch")

    products, pasts = [], []
    batches = [[k] for k in range(n_raw)] + [list(range(n_raw, count))]
    for k, batch in enumerate(batches):
        if k == 0:
            read = pltpu.VMEM((length, widths[0]), bf16)
            product = call(
                first_product_kernel,
                shape(length, widths[0], bf16),
                [order_scr, read, read, pltpu.SemaphoreType.DMA((2, 2))],
                tuple(pltpu.with_memory_space_constraint(x, pltpu.HBM) for x in (query, key_in)),
                in_specs=[hbm, hbm],
            )
            products.append(product)
        else:
            products += call(
                functools.partial(product_kernel, first=firsts[batch[0]]),
                [shape(length, widths[j], bf16) for j in batch],
                [order_scr],
                (query, key_in),
            )
        if k < n_raw:
            pasts.append(from_behind(products[k], "ctx", FILTER_PARTS))

    rows = -(-(modes + 1) // SEGMENTS) * SEGMENTS
    own_weight = jnp.concatenate(
        [residues.T, skip_gain[None], jnp.zeros((rows - modes - 1, group), F32)]
    )
    weight_parts = ring([own_weight] * n_ch, "ch")

    outs = call(
        functools.partial(states_kernel, count=count, n_ch=n_ch),
        [shape(runs * modes * SEGMENTS, width) for width in widths] + [shape(modes, group)] * n_ch + [stack(modes)],
        [tokens_scr, table_scr, pltpu.VMEM((n_ch, modes, group), F32)],
        (*products, *rate_parts),
    )
    carries, sums, rates = outs[:count], outs[count:-1], outs[-1]
    sums = ring(sums, "ch")
    weighing = call(assemble_kernel, stack(rows), [], weight_parts)

    overs = []

    def add_over(k):
        overs.append(
            call(
                functools.partial(over_kernel, span=span, first=firsts[k] // LANES),
                shape(length, widths[k]),
                [tokens_scr, table_scr, *taps_scr, pltpu.VMEM((runs * modes * SEGMENTS, LANES), F32)],
                (pasts[k], rates, weighing),
            )
        )

    def ahead_of(k):
        return call(
            functools.partial(ahead_kernel, span=span, first=firsts[k] // LANES, n_ctx=n_ctx),
            shape(length, widths[k], bf16),
            [tokens_scr, *taps_scr, tokens_scr],
            (products[k], rates, weighing, carries[k]),
        )

    aheads = [ahead_of(k) for k in range(n_raw, count)]
    for k in range(n_raw):
        add_over(k)

    blocks, tails, whole = call(
        functools.partial(tails_kernel, length=length),
        [stack(modes), stack(modes), shape(modes, group)],
        [],
        (*sums, own_rate),
    )
    assert FILTER_PARTS == 4
    newer = from_behind(whole, "ctx", 1)
    oldest = from_behind(tails, "ctx", FILTER_PARTS)
    pair = call(functools.partial(pair_kernel, part=length * n_ch), shape(modes, group), [], (whole, newer, own_rate))
    pairs = from_behind(pair, "ctx", 2)
    for ahead in aheads:
        overs.append(from_behind(ahead, "ctx", FILTER_PARTS))
    heads = call(
        functools.partial(heads_kernel, length=length, parts=FILTER_PARTS),
        [shape(modes, group)] * n_ch,
        [pltpu.VMEM((n_ch, modes, group), F32)],
        (blocks, own_rate, oldest, newer, pairs),
    )
    befores = ring(heads, "ch")

    late = call(
        functools.partial(local_kernel, first=firsts[-1] // LANES),
        shape(length, widths[-1]),
        [tokens_scr, *taps_scr],
        (products[-1], rates, weighing, carries[-1]),
    )
    widest = max(widths[:-1])
    partial, rest = call(
        functools.partial(finish_kernel, count=count - 1, n_ch=n_ch),
        [shape(length, channels, bf16), shape(length, widths[-1])],
        [
            tokens_scr,
            table_scr,
            weights_scr,
            tokens_scr,
            order_scr,
            pltpu.VMEM((n_ch, modes, group), F32),
            pltpu.VMEM((length, widest), bf16),
            pltpu.VMEM((2, length, widest), bf16),
            pltpu.SemaphoreType.DMA((2,)),
            *taps_scr,
            pltpu.VMEM((modes * SEGMENTS, LANES), F32),
        ],
        (*products[:-1], *carries[:-1], *overs[:-1], *befores, rates, weighing, value, late),
        out_specs=[anywhere, vmem],
    )
    return call(
        last_kernel,
        shape(length, channels, bf16),
        [order_scr, pltpu.VMEM((length, widths[-1]), bf16), pltpu.SemaphoreType.DMA((8,))],
        (rest, overs[-1], value, partial),
        in_specs=[vmem, vmem, vmem, anywhere],
        out_specs=anywhere,
        input_output_aliases={3: 0},
    )


def solution(mesh):
    return jax.shard_map(
        shard_program,
        mesh=mesh,
        in_specs=(
            P(("ctx", "ch"), None),
            P(("ctx", "ch"), None),
            P(("ctx", "ch"), None),
            P("ch", None),
            P("ch", None),
            P("ch"),
        ),
        out_specs=P(("ctx", "ch"), None),
        check_vma=False,
    )
```

```python
import functools
import math

import jax
import jax.numpy as jnp
from jax import lax
from jax.experimental import pallas as pl
from jax.experimental.pallas import tpu as pltpu
from jax.sharding import PartitionSpec as P


FILTER_PARTS = 4
LANES = 128
SEGMENTS = 8
RAW_SHARES = (4, 6)
DONE_SHARES = (6,)
RUN = 8
VMEM_BYTES = 16 << 20
F32 = jnp.float32


def from_behind(value, axis, steps):
    count = lax.axis_size(axis)
    return lax.ppermute(value, axis, [(source, source + steps) for source in range(count - steps)])


def partner(mine, k, count, sign):
    if count & (count - 1) == 0:
        return mine ^ k
    return (mine + sign * k + count) % count


def ring(parts, axis):
    count = lax.axis_size(axis)
    moved = []
    for k, part in enumerate(parts):
        pairs = [(source, partner(source, k, count, 1)) for source in range(count)]
        moved.append(lax.ppermute(part, axis, pairs) if k else part)
    return moved


def from_ring(refs, out):
    count = len(refs)
    mine = lax.axis_index("ch")
    for k, ref in enumerate(refs):
        out[partner(mine, k, count, -1)] = ref[...]


def to_ring(whole, refs):
    count = len(refs)
    mine = lax.axis_index("ch")
    for k, ref in enumerate(refs):
        ref[...] = whole[partner(mine, k, count, 1)]


def row_of(table, m):
    return jnp.broadcast_to(table[pl.ds(m, 1), :], (SEGMENTS, LANES))


def shifted(value, steps):
    row = lax.broadcasted_iota(jnp.int32, value.shape, 0)
    return jnp.where(row >= steps, pltpu.roll(value, steps, 0), 0.0)


def step_rows(i):
    return pl.ds(i * SEGMENTS, SEGMENTS)


def lanes(start):
    return pl.ds(pl.multiple_of(start, LANES), LANES)


def over_tiles(width, body):
    def step(t, carry):
        body(t)
        return carry

    lax.fori_loop(0, width // LANES, step, 0)


def at_tile(table, tile, first=0, count=None):
    per = table.shape[2] // LANES
    count = table.shape[1] if count is None else count
    return table.at[tile // per, pl.ds(first, count), lanes(tile % per * LANES)]


def runs_of(length):
    steps = length // SEGMENTS
    run = min(RUN, steps)
    return run, steps // run


def mode_rows(run, m, modes):
    return pl.ds((run * modes + m) * SEGMENTS, SEGMENTS)


def scan_segments(table, tokens, keep):
    modes = table.shape[1]
    steps = tokens.shape[0] // SEGMENTS
    run, _ = runs_of(tokens.shape[0])
    decay = [row_of(table.at[0], m) for m in range(modes)]
    state = [tokens[step_rows(0), :]] * modes
    for i in range(1, steps):
        if i % run == 0:
            for m in range(modes):
                keep(i // run, m, state[m])
        now = tokens[step_rows(i), :]
        state = [d * s + now for d, s in zip(decay, state)]
    chained = []
    for m in range(modes):
        value = state[m]
        for level in range(3):
            value = value + row_of(table.at[1 + level], m) * shifted(value, 1 << level)
        chained.append(value)
    return chained


def fill_jumps(table, rate, steps):
    table[0] = jnp.exp(-rate)
    for level in range(3):
        table[1 + level] = jnp.exp(-rate * float(steps << level))


def fill_taps(mix, leaps, direct, rate, weight, gain=None):
    decay = jnp.exp(-rate)
    tap = jnp.sum(weight, axis=0, keepdims=True)
    direct[pl.ds(0, 1), :] = tap if gain is None else tap + gain
    now = weight
    for i in range(mix.shape[0]):
        now = now * decay
        mix[i] = now
        if i + 1 < mix.shape[0]:
            direct[pl.ds(i + 1, 1), :] = jnp.sum(now, axis=0, keepdims=True)
    for r in range(1, leaps.shape[0]):
        leaps[r] = jnp.exp(-rate * float(mix.shape[0] * r))


def emit(mix, leaps, direct, state, kept, tokens, write):
    run, modes = mix.shape[:2]
    runs = leaps.shape[0]
    together = min(2, runs)
    for begin in range(0, runs, together):
        group = range(begin, begin + together)
        starts = []
        for r in group:
            if r == 0:
                starts.append([state(m) for m in range(modes)])
            else:
                starts.append([kept(r, m) + row_of(leaps.at[r], m) * state(m) for m in range(modes)])
        for i in range(run):
            sums = [None] * together
            for m in range(modes):
                weight = row_of(mix.at[i], m)
                for j in range(together):
                    term = weight * starts[j][m]
                    sums[j] = term if sums[j] is None else sums[j] + term
            for d in range(i + 1):
                tap = row_of(direct, d)
                for j, r in enumerate(group):
                    sums[j] = sums[j] + tap * tokens[step_rows(r * run + i - d), :]
            for j, r in enumerate(group):
                write(r * run + i, sums[j])


def fill_order(order, back=False):
    length = order.shape[0]
    row = lax.broadcasted_iota(jnp.int32, order.shape, 0)
    col = lax.broadcasted_iota(jnp.int32, order.shape, 1)
    inner = length // SEGMENTS if back else SEGMENTS
    order[...] = jnp.where(row % inner * (length // inner) + row // inner == col, 1.0, 0.0).astype(order.dtype)


def product_kernel(query, key_in, *refs, first):
    outs, order = refs[:-1], refs[-1]
    fill_order(order)
    start = first
    for out in outs:
        width = out.shape[1]
        wide = math.gcd(width, 4 * LANES)
        for at in range(0, width, wide):
            cols = pl.ds(start + at, wide)
            product = (query[:, cols].astype(F32) * key_in[:, cols].astype(F32)).astype(jnp.bfloat16)
            out[:, pl.ds(at, wide)] = jnp.dot(
                order[...], product, preferred_element_type=F32
            ).astype(jnp.bfloat16)
        start += width


def first_product_kernel(query, key_in, out, order, left, right, sems):
    width = out.shape[1]
    wide = width // sems.shape[0]
    copies = []
    for k in range(sems.shape[0]):
        cols = pl.ds(k * wide, wide)
        for j, (source, into) in enumerate(((query, left), (key_in, right))):
            copies.append(pltpu.make_async_copy(source.at[:, cols], into.at[:, cols], sems.at[k, j]))
            copies[-1].start()
    fill_order(order)
    for k in range(sems.shape[0]):
        cols = pl.ds(k * wide, wide)
        copies[2 * k].wait()
        copies[2 * k + 1].wait()
        product = (left[:, cols].astype(F32) * right[:, cols].astype(F32)).astype(jnp.bfloat16)
        out[:, cols] = jnp.dot(order[...], product, preferred_element_type=F32).astype(jnp.bfloat16)


def states_kernel(*refs, count, n_ch):
    products, parts = refs[:count], refs[count : count + n_ch]
    carries, sums = refs[count + n_ch : 2 * count + n_ch], refs[2 * count + n_ch : 2 * count + 2 * n_ch]
    rates, tokens, table, totals = refs[2 * count + 2 * n_ch :]
    from_ring(parts, rates)
    modes = rates.shape[1]
    first = 0
    for product, carry_out in zip(products, carries):
        steps = product.shape[0] // SEGMENTS

        def body(t, first=first, product=product, carry_out=carry_out):
            cols = lanes(t * LANES)
            tokens[...] = product[:, cols].astype(F32)
            fill_jumps(table, at_tile(rates, first + t)[...], steps)

            def keep(r, m, state, cols=cols, carry_out=carry_out):
                carry_out[mode_rows(r, m, modes), cols] = state

            state = scan_segments(table, tokens, keep)
            into = at_tile(totals, first + t)
            for m in range(modes):
                carry_out[mode_rows(0, m, modes), cols] = shifted(state[m], 1)
                into[pl.ds(m, 1), :] = state[m][SEGMENTS - 1 :, :]

        over_tiles(product.shape[1], body)
        first += product.shape[1] // LANES
    to_ring(totals, sums)


def assemble_kernel(*refs):
    from_ring(refs[:-1], refs[-1])


def tails_kernel(*refs, length):
    *parts, rate, blocks, tails, whole = refs
    from_ring(parts, blocks)
    count = len(parts)
    running = None
    for q in reversed(range(count)):
        now = blocks[q]
        if running is not None:
            now = running + jnp.exp(-rate[...] * float(length * (count - 1 - q))) * now
        running = now
        tails[q] = running
    whole[...] = running


def heads_kernel(*refs, length, parts):
    blocks, rate, oldest, *rest = refs
    wholes, outs, heads = rest[: parts - 1], rest[parts - 1 : -1], rest[-1]
    count = blocks.shape[0]
    rates = rate[...]
    older = wholes[0][...]
    for j in range(1, parts - 1):
        older = older + jnp.exp(-rates * float(length * count * j)) * wholes[j][...]
    last = jnp.exp(-rates * float(length * count * (parts - 1)))
    jump = jnp.exp(-rates * float(length))
    running = None
    for q in range(count):
        earlier = older + last * oldest[q]
        if running is None:
            heads[q] = earlier
            running = blocks[q]
        else:
            heads[q] = running + jnp.exp(-rates * float(length * q)) * earlier
            running = jump * running + blocks[q]
    to_ring(heads, outs)


def over_kernel(past, rates, weighing, out, tokens, table, mix, leaps, direct, carry, *, span, first):
    steps = past.shape[0] // SEGMENTS
    modes = rates.shape[1]
    needed = lax.axis_index("ctx") >= FILTER_PARTS

    @pl.when(needed)
    def _():
        def body(t):
            cols = lanes(t * LANES)
            tokens[...] = past[:, cols].astype(F32)
            rate = at_tile(rates, first + t)[...]
            fill_jumps(table, rate, steps)
            weight = at_tile(weighing, first + t, 0, modes)[...] * jnp.exp(-rate * float(span))
            fill_taps(mix, leaps, direct, rate, weight)

            def keep(r, m, state):
                carry[mode_rows(r, m, modes), :] = state

            for m, state in enumerate(scan_segments(table, tokens, keep)):
                carry[mode_rows(0, m, modes), :] = shifted(state, 1)

            def kept(r, m):
                return carry[mode_rows(r, m, modes), :]

            def write(i, value):
                out[step_rows(i), cols] = value

            emit(mix, leaps, direct, lambda m: kept(0, m), kept, tokens, write)

        over_tiles(past.shape[1], body)

    @pl.when(jnp.logical_not(needed))
    def _():
        out[...] = jnp.zeros_like(out)


def ahead_kernel(product, rates, weighing, carry, out, tokens, mix, leaps, direct, scr, *, span, first, n_ctx):
    modes = rates.shape[1]

    @pl.when(lax.axis_index("ctx") + FILTER_PARTS < n_ctx)
    def _():
        def body(t):
            cols = lanes(t * LANES)
            tokens[...] = product[:, cols].astype(F32)
            rate = at_tile(rates, first + t)[...]
            weight = at_tile(weighing, first + t, 0, modes)[...] * jnp.exp(-rate * float(span))
            fill_taps(mix, leaps, direct, rate, weight)

            def kept(r, m):
                return carry[mode_rows(r, m, modes), cols]

            def write(i, value):
                scr[step_rows(i), :] = value

            emit(mix, leaps, direct, lambda m: kept(0, m), kept, tokens, write)
            out[:, cols] = scr[...].astype(jnp.bfloat16)

        over_tiles(product.shape[1], body)


def local_kernel(near, product, rates, weighing, near_carry, carry, near_out, out, tokens, mix, leaps, direct, *, first):
    modes = rates.shape[1]

    def part(product, carry, out, first, skip):
        def body(t):
            cols = lanes((skip + t) * LANES)
            tokens[...] = product[:, cols].astype(F32)
            own = at_tile(weighing, first + t)
            fill_taps(
                mix,
                leaps,
                direct,
                at_tile(rates, first + t)[...],
                own[pl.ds(0, modes), :],
                own[pl.ds(modes, 1), :],
            )

            def kept(r, m):
                return carry[mode_rows(r, m, modes), cols]

            def write(i, value):
                out[step_rows(i), lanes(t * LANES)] = value

            emit(mix, leaps, direct, lambda m: kept(0, m), kept, tokens, write)

        over_tiles(out.shape[1], body)

    ahead = near_out.shape[1] // LANES
    part(near, near_carry, near_out, first - ahead, near.shape[1] // LANES - ahead)
    part(product, carry, out, first, 0)


def gated(back, mixed, value):
    plain = jnp.dot(back[...], mixed, preferred_element_type=F32)
    return (value.astype(F32) * plain).astype(jnp.bfloat16)


def finish_kernel(*refs, count, n_ch):
    products, carries, overs = refs[:count], refs[count : 2 * count], refs[2 * count : 3 * count]
    refs = refs[3 * count :]
    befores, (rates, weighing, value, near, late, out, rest) = refs[:n_ch], refs[n_ch : n_ch + 7]
    tokens, table, weights, scr, back, before, mixed, done, sems, mix, leaps, direct, coming = refs[n_ch + 7 :]
    modes = rates.shape[1]
    length = value.shape[0]
    steps = length // SEGMENTS
    from_ring(befores, before)
    fill_order(back, True)

    def arriving(tile):
        own, ahead = at_tile(rates, tile), at_tile(before, tile)
        table[0] = jnp.exp(-own[...])
        weights[...] = at_tile(weighing, tile, 0, modes)[...]
        begin = (lax.broadcasted_iota(jnp.int32, (SEGMENTS, LANES), 0) * steps).astype(F32)
        return [jnp.exp(-row_of(own, m) * begin) * row_of(ahead, m) for m in range(modes)]

    def add(tile, source, cols, write):
        state = [row_of(weights, m) * s for m, s in enumerate(arriving(tile))]
        decay = [row_of(table.at[0], m) for m in range(modes)]
        for i in range(steps):
            state = [d * s for d, s in zip(decay, state)]
            terms = state
            while len(terms) > 1:
                terms = [x + y for x, y in zip(terms[::2], terms[1::2])]
            write(i, source[step_rows(i), cols] + terms[0])

    copies = [None, None]
    first = 0
    for k in range(count):
        product, carry = products[k], carries[k]
        width = product.shape[1]
        slot = k % 2
        soon = near.shape[1] // LANES if k == count - 1 else 0
        whole = width // LANES - soon

        def write_scr(i, value):
            scr[step_rows(i), :] = value

        def body_near(t, first=first, whole=whole, k=k):
            cols = lanes((whole + t) * LANES)
            add(first + whole + t, near, lanes(t * LANES), write_scr)
            mixed[:, cols] = (scr[...] - overs[k][:, cols].astype(F32)).astype(jnp.bfloat16)

        def body(t, first=first, product=product, carry=carry, k=k):
            cols = lanes(t * LANES)
            tokens[...] = product[:, cols].astype(F32)
            own = at_tile(weighing, first + t)
            for m, state in enumerate(arriving(first + t)):
                coming[step_rows(m), :] = carry[mode_rows(0, m, modes), cols] + state
            rate = at_tile(rates, first + t)[...]
            fill_taps(mix, leaps, direct, rate, own[pl.ds(0, modes), :], own[pl.ds(modes, 1), :])

            def kept(r, m):
                return carry[mode_rows(r, m, modes), cols]

            emit(mix, leaps, direct, lambda m: coming[step_rows(m), :], kept, tokens, write_scr)
            mixed[:, cols] = (scr[...] - overs[k][:, cols].astype(F32)).astype(jnp.bfloat16)

        over_tiles(whole * LANES, body)
        if soon:
            over_tiles(soon * LANES, body_near)
        if copies[slot] is not None:
            copies[slot].wait()
        wide = math.gcd(width, 4 * LANES)
        for at in range(0, width, wide):
            cols = pl.ds(at, wide)
            done[slot, :, cols] = gated(back, mixed[:, cols], value[:, pl.ds(first * LANES + at, wide)])
        copies[slot] = pltpu.make_async_copy(
            done.at[slot, :, pl.ds(0, width)], out.at[:, pl.ds(first * LANES, width)], sems.at[slot]
        )
        copies[slot].start()
        first += width // LANES

    def body_late(t):
        cols = lanes(t * LANES)

        def write(i, value):
            rest[step_rows(i), cols] = value

        add(first + t, late, cols, write)

    over_tiles(late.shape[1], body_late)
    for copy in copies:
        if copy is not None:
            copy.wait()


def last_kernel(rest, over, value, partial, out, back, done, sem):
    del partial
    _, width = rest.shape
    first = value.shape[1] - width
    fill_order(back, True)
    wide = math.gcd(width, 4 * LANES)
    copies = []
    for k, at in enumerate(range(0, width, wide)):
        cols = pl.ds(at, wide)
        mixed = (rest[:, cols] - over[:, cols].astype(F32)).astype(jnp.bfloat16)
        done[:, cols] = gated(back, mixed, value[:, pl.ds(first + at, wide)])
        copies.append(
            pltpu.make_async_copy(done.at[:, cols], out.at[:, pl.ds(first + at, wide)], sem.at[k])
        )
        copies[-1].start()
    for copy in copies:
        copy.wait()


def shard_program(query, key_in, value, residues, decay_rates, skip_gain):
    length, channels = query.shape
    group, modes = residues.shape
    n_ch, n_ctx = lax.axis_size("ch"), lax.axis_size("ctx")
    span = FILTER_PARTS * length * n_ch
    bf16 = jnp.bfloat16

    shares = RAW_SHARES + DONE_SHARES
    unit = channels // sum(shares)
    widths = [unit * share for share in shares]
    firsts = [sum(widths[:k]) for k in range(len(widths))]
    count, n_raw = len(widths), len(RAW_SHARES)

    vmem = pl.BlockSpec(memory_space=pltpu.VMEM)
    anywhere = pl.BlockSpec(memory_space=pl.ANY)
    hbm = pl.BlockSpec(memory_space=pltpu.HBM)

    def shape(rows, columns, dtype=F32):
        return jax.ShapeDtypeStruct((rows, columns), dtype)

    def stack(rows):
        return jax.ShapeDtypeStruct((n_ch, rows, group), F32)

    tokens_scr = pltpu.VMEM((length, LANES), F32)
    table_scr = pltpu.VMEM((4, modes, LANES), F32)
    weights_scr = pltpu.VMEM((modes, LANES), F32)
    order_scr = pltpu.VMEM((length, length), bf16)
    run, runs = runs_of(length)
    taps_scr = [
        pltpu.VMEM((run, modes, LANES), F32),
        pltpu.VMEM((runs, modes, LANES), F32),
        pltpu.VMEM((run, LANES), F32),
    ]

    def call(kernel, out_shape, scratch, args, **options):
        specs = dict(in_specs=[vmem] * len(args), out_specs=jax.tree.map(lambda _: vmem, out_shape))
        specs.update(options)
        return pl.pallas_call(
            kernel,
            out_shape=out_shape,
            scratch_shapes=scratch,
            compiler_params=pltpu.CompilerParams(vmem_limit_bytes=VMEM_BYTES),
            **specs,
        )(*args)

    own_rate = decay_rates.T
    rate_parts = ring([own_rate] * n_ch, "ch")

    products, pasts = [], []
    batches = [[k] for k in range(n_raw)] + [list(range(n_raw, count))]
    for k, batch in enumerate(batches):
        if k == 0:
            read = pltpu.VMEM((length, widths[0]), bf16)
            product = call(
                first_product_kernel,
                shape(length, widths[0], bf16),
                [order_scr, read, read, pltpu.SemaphoreType.DMA((2, 2))],
                tuple(pltpu.with_memory_space_constraint(x, pltpu.HBM) for x in (query, key_in)),
                in_specs=[hbm, hbm],
            )
            products.append(product)
        else:
            products += call(
                functools.partial(product_kernel, first=firsts[batch[0]]),
                [shape(length, widths[j], bf16) for j in batch],
                [order_scr],
                (query, key_in),
            )
        if k < n_raw:
            pasts.append(from_behind(products[k], "ctx", FILTER_PARTS))

    rows = -(-(modes + 1) // SEGMENTS) * SEGMENTS
    own_weight = jnp.concatenate(
        [residues.T, skip_gain[None], jnp.zeros((rows - modes - 1, group), F32)]
    )
    weight_parts = ring([own_weight] * n_ch, "ch")

    outs = call(
        functools.partial(states_kernel, count=count, n_ch=n_ch),
        [shape(runs * modes * SEGMENTS, width) for width in widths] + [shape(modes, group)] * n_ch + [stack(modes)],
        [tokens_scr, table_scr, pltpu.VMEM((n_ch, modes, group), F32)],
        (*products, *rate_parts),
    )
    carries, sums, rates = outs[:count], outs[count:-1], outs[-1]
    sums = ring(sums, "ch")
    weighing = call(assemble_kernel, stack(rows), [], weight_parts)

    overs = []

    def add_over(k):
        overs.append(
            call(
                functools.partial(over_kernel, span=span, first=firsts[k] // LANES),
                shape(length, widths[k]),
                [tokens_scr, table_scr, *taps_scr, pltpu.VMEM((runs * modes * SEGMENTS, LANES), F32)],
                (pasts[k], rates, weighing),
            )
        )

    def ahead_of(k):
        return call(
            functools.partial(ahead_kernel, span=span, first=firsts[k] // LANES, n_ctx=n_ctx),
            shape(length, widths[k], bf16),
            [tokens_scr, *taps_scr, tokens_scr],
            (products[k], rates, weighing, carries[k]),
        )

    aheads = [ahead_of(k) for k in range(n_raw, count)]
    for k in range(n_raw):
        add_over(k)

    blocks, tails, whole = call(
        functools.partial(tails_kernel, length=length),
        [stack(modes), stack(modes), shape(modes, group)],
        [],
        (*sums, own_rate),
    )
    oldest = from_behind(tails, "ctx", FILTER_PARTS)
    wholes = []
    for j in range(1, FILTER_PARTS):
        wholes.append(from_behind(whole, "ctx", j))
    for ahead in aheads:
        overs.append(from_behind(ahead, "ctx", FILTER_PARTS))
    heads = call(
        functools.partial(heads_kernel, length=length, parts=FILTER_PARTS),
        [shape(modes, group)] * n_ch,
        [pltpu.VMEM((n_ch, modes, group), F32)],
        (blocks, own_rate, oldest, *wholes),
    )
    befores = ring(heads, "ch")

    soon = widths[-2] // LANES // 3 * LANES
    near, late = call(
        functools.partial(local_kernel, first=firsts[-1] // LANES),
        [shape(length, soon), shape(length, widths[-1])],
        [tokens_scr, *taps_scr],
        (products[-2], products[-1], rates, weighing, carries[-2], carries[-1]),
    )
    widest = max(widths[:-1])
    partial, rest = call(
        functools.partial(finish_kernel, count=count - 1, n_ch=n_ch),
        [shape(length, channels, bf16), shape(length, widths[-1])],
        [
            tokens_scr,
            table_scr,
            weights_scr,
            tokens_scr,
            order_scr,
            pltpu.VMEM((n_ch, modes, group), F32),
            pltpu.VMEM((length, widest), bf16),
            pltpu.VMEM((2, length, widest), bf16),
            pltpu.SemaphoreType.DMA((2,)),
            *taps_scr,
            pltpu.VMEM((modes * SEGMENTS, LANES), F32),
        ],
        (*products[:-1], *carries[:-1], *overs[:-1], *befores, rates, weighing, value, near, late),
        out_specs=[anywhere, vmem],
    )
    return call(
        last_kernel,
        shape(length, channels, bf16),
        [order_scr, pltpu.VMEM((length, widths[-1]), bf16), pltpu.SemaphoreType.DMA((8,))],
        (rest, overs[-1], value, partial),
        in_specs=[vmem, vmem, vmem, anywhere],
        out_specs=anywhere,
        input_output_aliases={3: 0},
    )


def solution(mesh):
    return jax.shard_map(
        shard_program,
        mesh=mesh,
        in_specs=(
            P(("ctx", "ch"), None),
            P(("ctx", "ch"), None),
            P(("ctx", "ch"), None),
            P("ch", None),
            P("ch", None),
            P("ch"),
        ),
        out_specs=P(("ctx", "ch"), None),
        check_vma=False,
    )
```

```python
import functools

import jax
import jax.numpy as jnp
from jax import lax
from jax.experimental import pallas as pl
from jax.experimental.pallas import tpu as pltpu
from jax.sharding import PartitionSpec as P


FILTER_PARTS = 4
LANES = 128
SEGMENTS = 8
RAW_SHARES = (8, 11)
DONE_SHARES = (13,)
RUN = 8
VMEM_BYTES = 16 << 20
F32 = jnp.float32


def from_behind(value, axis, steps):
    count = lax.axis_size(axis)
    return lax.ppermute(value, axis, [(source, source + steps) for source in range(count - steps)])


def partner(mine, k, count, sign):
    if count & (count - 1) == 0:
        return mine ^ k
    return (mine + sign * k + count) % count


def ring(parts, axis):
    count = lax.axis_size(axis)
    moved = []
    for k, part in enumerate(parts):
        pairs = [(source, partner(source, k, count, 1)) for source in range(count)]
        moved.append(lax.ppermute(part, axis, pairs) if k else part)
    return moved


def from_ring(refs, out):
    count = len(refs)
    mine = lax.axis_index("ch")
    for k, ref in enumerate(refs):
        out[partner(mine, k, count, -1)] = ref[...]


def to_ring(whole, refs):
    count = len(refs)
    mine = lax.axis_index("ch")
    for k, ref in enumerate(refs):
        ref[...] = whole[partner(mine, k, count, 1)]


def row_of(table, m):
    return jnp.broadcast_to(table[pl.ds(m, 1), :], (SEGMENTS, LANES))


def shifted(value, steps):
    row = lax.broadcasted_iota(jnp.int32, value.shape, 0)
    return jnp.where(row >= steps, pltpu.roll(value, steps, 0), 0.0)


def step_rows(i):
    return pl.ds(i * SEGMENTS, SEGMENTS)


def pieces(width):
    wide = 4 * LANES
    return [(at, min(wide, width - at)) for at in range(0, width, wide)]


def lanes(start):
    return pl.ds(pl.multiple_of(start, LANES), LANES)


def over_tiles(width, body):
    def step(t, carry):
        body(t)
        return carry

    lax.fori_loop(0, width // LANES, step, 0)


def at_tile(table, tile, first=0, count=None):
    per = table.shape[2] // LANES
    count = table.shape[1] if count is None else count
    return table.at[tile // per, pl.ds(first, count), lanes(tile % per * LANES)]


def runs_of(length):
    steps = length // SEGMENTS
    run = min(RUN, steps)
    return run, steps // run


def mode_rows(run, m, modes):
    return pl.ds((run * modes + m) * SEGMENTS, SEGMENTS)


def scan_segments(table, tokens, keep):
    modes = table.shape[1]
    steps = tokens.shape[0] // SEGMENTS
    run, _ = runs_of(tokens.shape[0])
    decay = [row_of(table.at[0], m) for m in range(modes)]
    state = [tokens[step_rows(0), :]] * modes
    for i in range(1, steps):
        if i % run == 0:
            for m in range(modes):
                keep(i // run, m, state[m])
        now = tokens[step_rows(i), :]
        state = [d * s + now for d, s in zip(decay, state)]
    chained = []
    for m in range(modes):
        value = state[m]
        for level in range(3):
            value = value + row_of(table.at[1 + level], m) * shifted(value, 1 << level)
        chained.append(value)
    return chained


def fill_jumps(table, rate, steps):
    table[0] = jnp.exp(-rate)
    for level in range(3):
        table[1 + level] = jnp.exp(-rate * float(steps << level))


def fill_taps(mix, leaps, direct, rate, weight, gain=None):
    decay = jnp.exp(-rate)
    tap = jnp.sum(weight, axis=0, keepdims=True)
    direct[pl.ds(0, 1), :] = tap if gain is None else tap + gain
    now = weight
    for i in range(mix.shape[0]):
        now = now * decay
        mix[i] = now
        if i + 1 < mix.shape[0]:
            direct[pl.ds(i + 1, 1), :] = jnp.sum(now, axis=0, keepdims=True)
    for r in range(1, leaps.shape[0]):
        leaps[r] = jnp.exp(-rate * float(mix.shape[0] * r))


def emit(mix, leaps, direct, state, kept, tokens, write):
    run, modes = mix.shape[:2]
    runs = leaps.shape[0]
    together = min(2, runs)
    for begin in range(0, runs, together):
        group = range(begin, begin + together)
        starts = []
        for r in group:
            if r == 0:
                starts.append([state(m) for m in range(modes)])
            else:
                starts.append([kept(r, m) + row_of(leaps.at[r], m) * state(m) for m in range(modes)])
        for i in range(run):
            sums = [None] * together
            for m in range(modes):
                weight = row_of(mix.at[i], m)
                for j in range(together):
                    term = weight * starts[j][m]
                    sums[j] = term if sums[j] is None else sums[j] + term
            for d in range(i + 1):
                tap = row_of(direct, d)
                for j, r in enumerate(group):
                    sums[j] = sums[j] + tap * tokens[step_rows(r * run + i - d), :]
            for j, r in enumerate(group):
                write(r * run + i, sums[j])


def fill_order(order, back=False):
    length = order.shape[0]
    row = lax.broadcasted_iota(jnp.int32, order.shape, 0)
    col = lax.broadcasted_iota(jnp.int32, order.shape, 1)
    inner = length // SEGMENTS if back else SEGMENTS
    order[...] = jnp.where(row % inner * (length // inner) + row // inner == col, 1.0, 0.0).astype(order.dtype)


def product_kernel(query, key_in, *refs, first):
    outs, order = refs[:-1], refs[-1]
    fill_order(order)
    start = first
    for out in outs:
        width = out.shape[1]
        for at, wide in pieces(width):
            cols = pl.ds(start + at, wide)
            product = (query[:, cols].astype(F32) * key_in[:, cols].astype(F32)).astype(jnp.bfloat16)
            out[:, pl.ds(at, wide)] = jnp.dot(
                order[...], product, preferred_element_type=F32
            ).astype(jnp.bfloat16)
        start += width


def first_product_kernel(query, key_in, out, order, left, right, sems):
    width = out.shape[1]
    wide = width // sems.shape[0]
    copies = []
    for k in range(sems.shape[0]):
        cols = pl.ds(k * wide, wide)
        for j, (source, into) in enumerate(((query, left), (key_in, right))):
            copies.append(pltpu.make_async_copy(source.at[:, cols], into.at[:, cols], sems.at[k, j]))
            copies[-1].start()
    fill_order(order)
    for k in range(sems.shape[0]):
        cols = pl.ds(k * wide, wide)
        copies[2 * k].wait()
        copies[2 * k + 1].wait()
        product = (left[:, cols].astype(F32) * right[:, cols].astype(F32)).astype(jnp.bfloat16)
        out[:, cols] = jnp.dot(order[...], product, preferred_element_type=F32).astype(jnp.bfloat16)


def states_kernel(*refs, count, n_ch):
    products, parts = refs[:count], refs[count : count + n_ch]
    carries, sums = refs[count + n_ch : 2 * count + n_ch], refs[2 * count + n_ch : 2 * count + 2 * n_ch]
    rates, tokens, table, totals = refs[2 * count + 2 * n_ch :]
    from_ring(parts, rates)
    modes = rates.shape[1]
    first = 0
    for product, carry_out in zip(products, carries):
        steps = product.shape[0] // SEGMENTS

        def body(t, first=first, product=product, carry_out=carry_out):
            cols = lanes(t * LANES)
            tokens[...] = product[:, cols].astype(F32)
            fill_jumps(table, at_tile(rates, first + t)[...], steps)

            def keep(r, m, state, cols=cols, carry_out=carry_out):
                carry_out[mode_rows(r, m, modes), cols] = state

            state = scan_segments(table, tokens, keep)
            into = at_tile(totals, first + t)
            for m in range(modes):
                carry_out[mode_rows(0, m, modes), cols] = shifted(state[m], 1)
                into[pl.ds(m, 1), :] = state[m][SEGMENTS - 1 :, :]

        over_tiles(product.shape[1], body)
        first += product.shape[1] // LANES
    to_ring(totals, sums)


def assemble_kernel(*refs):
    from_ring(refs[:-1], refs[-1])


def tails_kernel(*refs, length):
    *parts, rate, blocks, tails, whole = refs
    from_ring(parts, blocks)
    count = len(parts)
    running = None
    for q in reversed(range(count)):
        now = blocks[q]
        if running is not None:
            now = running + jnp.exp(-rate[...] * float(length * (count - 1 - q))) * now
        running = now
        tails[q] = running
    whole[...] = running


def heads_kernel(*refs, length, parts):
    blocks, rate, oldest, *rest = refs
    wholes, outs, heads = rest[: parts - 1], rest[parts - 1 : -1], rest[-1]
    count = blocks.shape[0]
    rates = rate[...]
    older = wholes[0][...]
    for j in range(1, parts - 1):
        older = older + jnp.exp(-rates * float(length * count * j)) * wholes[j][...]
    last = jnp.exp(-rates * float(length * count * (parts - 1)))
    jump = jnp.exp(-rates * float(length))
    running = None
    for q in range(count):
        earlier = older + last * oldest[q]
        if running is None:
            heads[q] = earlier
            running = blocks[q]
        else:
            heads[q] = running + jnp.exp(-rates * float(length * q)) * earlier
            running = jump * running + blocks[q]
    to_ring(heads, outs)


def over_kernel(past, rates, weighing, out, tokens, table, mix, leaps, direct, carry, *, span, first):
    steps = past.shape[0] // SEGMENTS
    modes = rates.shape[1]
    needed = lax.axis_index("ctx") >= FILTER_PARTS

    @pl.when(needed)
    def _():
        def body(t):
            cols = lanes(t * LANES)
            tokens[...] = past[:, cols].astype(F32)
            rate = at_tile(rates, first + t)[...]
            fill_jumps(table, rate, steps)
            weight = at_tile(weighing, first + t, 0, modes)[...] * jnp.exp(-rate * float(span))
            fill_taps(mix, leaps, direct, rate, weight)

            def keep(r, m, state):
                carry[mode_rows(r, m, modes), :] = state

            for m, state in enumerate(scan_segments(table, tokens, keep)):
                carry[mode_rows(0, m, modes), :] = shifted(state, 1)

            def kept(r, m):
                return carry[mode_rows(r, m, modes), :]

            def write(i, value):
                out[step_rows(i), cols] = value

            emit(mix, leaps, direct, lambda m: kept(0, m), kept, tokens, write)

        over_tiles(past.shape[1], body)

    @pl.when(jnp.logical_not(needed))
    def _():
        out[...] = jnp.zeros_like(out)


def ahead_kernel(product, rates, weighing, carry, out, tokens, mix, leaps, direct, scr, *, span, first, n_ctx):
    modes = rates.shape[1]

    @pl.when(lax.axis_index("ctx") + FILTER_PARTS < n_ctx)
    def _():
        def body(t):
            cols = lanes(t * LANES)
            tokens[...] = product[:, cols].astype(F32)
            rate = at_tile(rates, first + t)[...]
            weight = at_tile(weighing, first + t, 0, modes)[...] * jnp.exp(-rate * float(span))
            fill_taps(mix, leaps, direct, rate, weight)

            def kept(r, m):
                return carry[mode_rows(r, m, modes), cols]

            def write(i, value):
                scr[step_rows(i), :] = value

            emit(mix, leaps, direct, lambda m: kept(0, m), kept, tokens, write)
            out[:, cols] = scr[...].astype(jnp.bfloat16)

        over_tiles(product.shape[1], body)


def local_kernel(near, product, rates, weighing, near_carry, carry, near_out, out, tokens, mix, leaps, direct, *, first):
    modes = rates.shape[1]

    def part(product, carry, out, first, skip):
        def body(t):
            cols = lanes((skip + t) * LANES)
            tokens[...] = product[:, cols].astype(F32)
            own = at_tile(weighing, first + t)
            fill_taps(
                mix,
                leaps,
                direct,
                at_tile(rates, first + t)[...],
                own[pl.ds(0, modes), :],
                own[pl.ds(modes, 1), :],
            )

            def kept(r, m):
                return carry[mode_rows(r, m, modes), cols]

            def write(i, value):
                out[step_rows(i), lanes(t * LANES)] = value

            emit(mix, leaps, direct, lambda m: kept(0, m), kept, tokens, write)

        over_tiles(out.shape[1], body)

    ahead = near_out.shape[1] // LANES
    part(near, near_carry, near_out, first - ahead, near.shape[1] // LANES - ahead)
    part(product, carry, out, first, 0)


def gated(back, mixed, value):
    plain = jnp.dot(back[...], mixed, preferred_element_type=F32)
    return (value.astype(F32) * plain).astype(jnp.bfloat16)


def finish_kernel(*refs, count, n_ch):
    products, carries, overs = refs[:count], refs[count : 2 * count], refs[2 * count : 3 * count]
    refs = refs[3 * count :]
    befores, (rates, weighing, value, near, late, out, rest) = refs[:n_ch], refs[n_ch : n_ch + 7]
    tokens, table, weights, scr, back, before, mixed, done, sems, mix, leaps, direct, coming = refs[n_ch + 7 :]
    modes = rates.shape[1]
    length = value.shape[0]
    steps = length // SEGMENTS
    from_ring(befores, before)
    fill_order(back, True)

    def arriving(tile):
        own, ahead = at_tile(rates, tile), at_tile(before, tile)
        table[0] = jnp.exp(-own[...])
        weights[...] = at_tile(weighing, tile, 0, modes)[...]
        begin = (lax.broadcasted_iota(jnp.int32, (SEGMENTS, LANES), 0) * steps).astype(F32)
        return [jnp.exp(-row_of(own, m) * begin) * row_of(ahead, m) for m in range(modes)]

    def add(tile, source, cols, write):
        state = [row_of(weights, m) * s for m, s in enumerate(arriving(tile))]
        decay = [row_of(table.at[0], m) for m in range(modes)]
        for i in range(steps):
            state = [d * s for d, s in zip(decay, state)]
            terms = state
            while len(terms) > 1:
                terms = [x + y for x, y in zip(terms[::2], terms[1::2])]
            write(i, source[step_rows(i), cols] + terms[0])

    copies = [None, None]
    first = 0
    for k in range(count):
        product, carry = products[k], carries[k]
        width = product.shape[1]
        slot = k % 2
        soon = near.shape[1] // LANES if k == count - 1 else 0
        whole = width // LANES - soon

        def write_scr(i, value):
            scr[step_rows(i), :] = value

        def body_near(t, first=first, whole=whole, k=k):
            cols = lanes((whole + t) * LANES)
            add(first + whole + t, near, lanes(t * LANES), write_scr)
            mixed[:, cols] = (scr[...] - overs[k][:, cols].astype(F32)).astype(jnp.bfloat16)

        def body(t, first=first, product=product, carry=carry, k=k):
            cols = lanes(t * LANES)
            tokens[...] = product[:, cols].astype(F32)
            own = at_tile(weighing, first + t)
            for m, state in enumerate(arriving(first + t)):
                coming[step_rows(m), :] = carry[mode_rows(0, m, modes), cols] + state
            rate = at_tile(rates, first + t)[...]
            fill_taps(mix, leaps, direct, rate, own[pl.ds(0, modes), :], own[pl.ds(modes, 1), :])

            def kept(r, m):
                return carry[mode_rows(r, m, modes), cols]

            emit(mix, leaps, direct, lambda m: coming[step_rows(m), :], kept, tokens, write_scr)
            mixed[:, cols] = (scr[...] - overs[k][:, cols].astype(F32)).astype(jnp.bfloat16)

        over_tiles(whole * LANES, body)
        if soon:
            over_tiles(soon * LANES, body_near)
        if copies[slot] is not None:
            copies[slot].wait()
        for at, wide in pieces(width):
            cols = pl.ds(at, wide)
            done[slot, :, cols] = gated(back, mixed[:, cols], value[:, pl.ds(first * LANES + at, wide)])
        copies[slot] = pltpu.make_async_copy(
            done.at[slot, :, pl.ds(0, width)], out.at[:, pl.ds(first * LANES, width)], sems.at[slot]
        )
        copies[slot].start()
        first += width // LANES

    def body_late(t):
        cols = lanes(t * LANES)

        def write(i, value):
            rest[step_rows(i), cols] = value

        add(first + t, late, cols, write)

    over_tiles(late.shape[1], body_late)
    for copy in copies:
        if copy is not None:
            copy.wait()


def last_kernel(rest, over, value, partial, out, back, done, sem):
    del partial
    _, width = rest.shape
    first = value.shape[1] - width
    fill_order(back, True)
    copies = []
    for k, (at, wide) in enumerate(pieces(width)):
        cols = pl.ds(at, wide)
        mixed = (rest[:, cols] - over[:, cols].astype(F32)).astype(jnp.bfloat16)
        done[:, cols] = gated(back, mixed, value[:, pl.ds(first + at, wide)])
        copies.append(
            pltpu.make_async_copy(done.at[:, cols], out.at[:, pl.ds(first + at, wide)], sem.at[k])
        )
        copies[-1].start()
    for copy in copies:
        copy.wait()


def shard_program(query, key_in, value, residues, decay_rates, skip_gain):
    length, channels = query.shape
    group, modes = residues.shape
    n_ch, n_ctx = lax.axis_size("ch"), lax.axis_size("ctx")
    span = FILTER_PARTS * length * n_ch
    bf16 = jnp.bfloat16

    shares = RAW_SHARES + DONE_SHARES
    unit = channels // sum(shares)
    widths = [unit * share for share in shares]
    firsts = [sum(widths[:k]) for k in range(len(widths))]
    count, n_raw = len(widths), len(RAW_SHARES)

    vmem = pl.BlockSpec(memory_space=pltpu.VMEM)
    anywhere = pl.BlockSpec(memory_space=pl.ANY)
    hbm = pl.BlockSpec(memory_space=pltpu.HBM)

    def shape(rows, columns, dtype=F32):
        return jax.ShapeDtypeStruct((rows, columns), dtype)

    def stack(rows):
        return jax.ShapeDtypeStruct((n_ch, rows, group), F32)

    tokens_scr = pltpu.VMEM((length, LANES), F32)
    table_scr = pltpu.VMEM((4, modes, LANES), F32)
    weights_scr = pltpu.VMEM((modes, LANES), F32)
    order_scr = pltpu.VMEM((length, length), bf16)
    run, runs = runs_of(length)
    taps_scr = [
        pltpu.VMEM((run, modes, LANES), F32),
        pltpu.VMEM((runs, modes, LANES), F32),
        pltpu.VMEM((run, LANES), F32),
    ]

    def call(kernel, out_shape, scratch, args, **options):
        specs = dict(in_specs=[vmem] * len(args), out_specs=jax.tree.map(lambda _: vmem, out_shape))
        specs.update(options)
        return pl.pallas_call(
            kernel,
            out_shape=out_shape,
            scratch_shapes=scratch,
            compiler_params=pltpu.CompilerParams(vmem_limit_bytes=VMEM_BYTES),
            **specs,
        )(*args)

    own_rate = decay_rates.T
    rate_parts = ring([own_rate] * n_ch, "ch")

    products, pasts = [], []
    batches = [[k] for k in range(n_raw)] + [list(range(n_raw, count))]
    for k, batch in enumerate(batches):
        if k == 0:
            read = pltpu.VMEM((length, widths[0]), bf16)
            product = call(
                first_product_kernel,
                shape(length, widths[0], bf16),
                [order_scr, read, read, pltpu.SemaphoreType.DMA((2, 2))],
                tuple(pltpu.with_memory_space_constraint(x, pltpu.HBM) for x in (query, key_in)),
                in_specs=[hbm, hbm],
            )
            products.append(product)
        else:
            products += call(
                functools.partial(product_kernel, first=firsts[batch[0]]),
                [shape(length, widths[j], bf16) for j in batch],
                [order_scr],
                (query, key_in),
            )
        if k < n_raw:
            pasts.append(from_behind(products[k], "ctx", FILTER_PARTS))

    rows = -(-(modes + 1) // SEGMENTS) * SEGMENTS
    own_weight = jnp.concatenate(
        [residues.T, skip_gain[None], jnp.zeros((rows - modes - 1, group), F32)]
    )
    weight_parts = ring([own_weight] * n_ch, "ch")

    outs = call(
        functools.partial(states_kernel, count=count, n_ch=n_ch),
        [shape(runs * modes * SEGMENTS, width) for width in widths] + [shape(modes, group)] * n_ch + [stack(modes)],
        [tokens_scr, table_scr, pltpu.VMEM((n_ch, modes, group), F32)],
        (*products, *rate_parts),
    )
    carries, sums, rates = outs[:count], outs[count:-1], outs[-1]
    sums = ring(sums, "ch")
    weighing = call(assemble_kernel, stack(rows), [], weight_parts)

    overs = []

    def add_over(k):
        overs.append(
            call(
                functools.partial(over_kernel, span=span, first=firsts[k] // LANES),
                shape(length, widths[k]),
                [tokens_scr, table_scr, *taps_scr, pltpu.VMEM((runs * modes * SEGMENTS, LANES), F32)],
                (pasts[k], rates, weighing),
            )
        )

    def ahead_of(k):
        return call(
            functools.partial(ahead_kernel, span=span, first=firsts[k] // LANES, n_ctx=n_ctx),
            shape(length, widths[k], bf16),
            [tokens_scr, *taps_scr, tokens_scr],
            (products[k], rates, weighing, carries[k]),
        )

    aheads = [ahead_of(k) for k in range(n_raw, count)]
    for k in range(n_raw):
        add_over(k)

    blocks, tails, whole = call(
        functools.partial(tails_kernel, length=length),
        [stack(modes), stack(modes), shape(modes, group)],
        [],
        (*sums, own_rate),
    )
    oldest = from_behind(tails, "ctx", FILTER_PARTS)
    wholes = []
    for j in range(1, FILTER_PARTS):
        wholes.append(from_behind(whole, "ctx", j))
    for ahead in aheads:
        overs.append(from_behind(ahead, "ctx", FILTER_PARTS))
    heads = call(
        functools.partial(heads_kernel, length=length, parts=FILTER_PARTS),
        [shape(modes, group)] * n_ch,
        [pltpu.VMEM((n_ch, modes, group), F32)],
        (blocks, own_rate, oldest, *wholes),
    )
    befores = ring(heads, "ch")

    soon = widths[-2] // LANES // 3 * LANES
    near, late = call(
        functools.partial(local_kernel, first=firsts[-1] // LANES),
        [shape(length, soon), shape(length, widths[-1])],
        [tokens_scr, *taps_scr],
        (products[-2], products[-1], rates, weighing, carries[-2], carries[-1]),
    )
    widest = max(widths[:-1])
    partial, rest = call(
        functools.partial(finish_kernel, count=count - 1, n_ch=n_ch),
        [shape(length, channels, bf16), shape(length, widths[-1])],
        [
            tokens_scr,
            table_scr,
            weights_scr,
            tokens_scr,
            order_scr,
            pltpu.VMEM((n_ch, modes, group), F32),
            pltpu.VMEM((length, widest), bf16),
            pltpu.VMEM((2, length, widest), bf16),
            pltpu.SemaphoreType.DMA((2,)),
            *taps_scr,
            pltpu.VMEM((modes * SEGMENTS, LANES), F32),
        ],
        (*products[:-1], *carries[:-1], *overs[:-1], *befores, rates, weighing, value, near, late),
        out_specs=[anywhere, vmem],
    )
    return call(
        last_kernel,
        shape(length, channels, bf16),
        [order_scr, pltpu.VMEM((length, widths[-1]), bf16), pltpu.SemaphoreType.DMA((len(pieces(widths[-1])),))],
        (rest, overs[-1], value, partial),
        in_specs=[vmem, vmem, vmem, anywhere],
        out_specs=anywhere,
        input_output_aliases={3: 0},
    )


def solution(mesh):
    return jax.shard_map(
        shard_program,
        mesh=mesh,
        in_specs=(
            P(("ctx", "ch"), None),
            P(("ctx", "ch"), None),
            P(("ctx", "ch"), None),
            P("ch", None),
            P("ch", None),
            P("ch"),
        ),
        out_specs=P(("ctx", "ch"), None),
        check_vma=False,
    )
```
